32 devices in a mesh: branch: 2 (over x), tok: 16 (over z, y, core).
Axes of the slice: x: 2, y: 2, z: 4, core: 2. Of those that a mesh axis runs over, the one named last changes fastest.
Arguments:
- teacher_hidden: bfloat16 [2, 256, 4096], P('branch', 'tok'), may hold values from -400 to 400
- teacher_gain: float32 [2, 4096], P('branch'), may hold values from 0.5 to 1.5
- teacher_head: bfloat16 [2, 4096, 20480], P('branch', None, 'tok'), may hold values from -30 to 30
- student_hidden: bfloat16 [256, 4096], P('branch'), may hold values from -400 to 400
- student_gain: float32 [4096], replicated, may hold values from 0.5 to 1.5
- student_head: bfloat16 [4096, 20480], P('branch', 'tok'), may hold values from -30 to 30
- cluster_weights: int32 [256, 2], P(None, 'branch'), may hold values from 0 to 64, as said below
- token_ids: int32 [256], P('branch'), may hold values from 0 to 20479
Outputs:
- grad_head: float32 [4096, 20480], P('branch', 'tok')
- grad_hidden: float32 [256, 4096], P('branch', 'tok')
- grad_gain: float32 [4096], P('tok')
The draws below stay inside these ranges and needn't reach their ends.
Inputs may be any that keep to these rules, and one draw needn't show every extreme that they name: `cluster_weights`: each token's 2 weights sum to 64.
All inputs are finite; a program needn't handle non-finite values.
Results may differ from the reference program's by a relative error of at most 0.0063.
Values may be sent and summed in bfloat16 or wider, within the bound.
No kernel may reach another device: no remote copies, remote signals or barrier semaphores. Data moves between devices by JAX's collectives and lax.ppermute only.
A program may use at most 128 MiB of HBM per device.

```python
import math
import jax
import jax.numpy as jnp
import numpy as np
from jax import lax

D = 4096
V = 20480
DEN = 64
BRANCHES = 2
TOKENS = 256


def column_sigma():
    position = jnp.arange(V, dtype=jnp.float32) / V
    return 2.6 + 0.8 * position


def make_pair(key):
    keys = jax.random.split(key, 4)
    width_root = jnp.sqrt(jnp.float32(D))
    head = jax.random.truncated_normal(keys[0], -4.0, 4.0, (D, V), jnp.float32) * column_sigma()[None, :] / width_root
    row_spread = jnp.exp(jax.random.uniform(keys[1], (TOKENS, 1), jnp.float32) * jnp.log(10.0))
    col_spread = jnp.exp(jax.random.uniform(keys[2], (1, D), jnp.float32) * jnp.log(10.0))
    hidden = jax.random.truncated_normal(keys[3], -4.0, 4.0, (TOKENS, D), jnp.float32) * row_spread * col_spread
    return (head, hidden)


def draw_teacher_head(key, part):
    seed_base = jax.random.fold_in(key, 101)
    return lax.map(lambda branch_index: make_pair(jax.random.fold_in(seed_base, branch_index))[0], jnp.arange(BRANCHES)).astype(jnp.bfloat16)


def draw_teacher_hidden(key, part):
    seed_base = jax.random.fold_in(key, 101)
    return lax.map(lambda branch_index: make_pair(jax.random.fold_in(seed_base, branch_index))[1], jnp.arange(BRANCHES)).astype(jnp.bfloat16)


def draw_student_head(key, part):
    return make_pair(jax.random.fold_in(key, 202))[0].astype(jnp.bfloat16)


def draw_student_hidden(key, part):
    return make_pair(jax.random.fold_in(key, 202))[1].astype(jnp.bfloat16)


def draw_cluster_weights(key, part):
    cuts = jnp.sort(jax.random.randint(jax.random.fold_in(key, 303), (TOKENS, BRANCHES - 1), 0, DEN + 1), axis=1)
    single = jax.random.randint(jax.random.fold_in(key, 304), (), 0, TOKENS)
    rows = jnp.arange(TOKENS, dtype=jnp.int32)[:, None]
    cuts = jnp.where(rows == single, jnp.zeros_like(cuts), cuts)
    edges = jnp.concatenate([jnp.zeros((TOKENS, 1), jnp.int32), cuts.astype(jnp.int32), jnp.full((TOKENS, 1), DEN, jnp.int32)], axis=1)
    return (edges[:, 1:] - edges[:, :-1]).astype(jnp.int32)


def set_ends(array, rng, least, high):
    longest = array.shape.index(max(array.shape))
    spots = []
    for shift in (0, 1):
        where = [jax.random.randint(jax.random.fold_in(rng, axis), (), 0, length) for axis, length in enumerate(array.shape)]
        where[longest] = (where[longest] + shift) % array.shape[longest]
        spots.append(tuple(where))
    return array.at[spots[0]].set(least).at[spots[1]].set(high)


def cumulative_ranks(number_of, skew):
    loads = [(1 << 20) // math.isqrt(rank ** skew) + 1 for rank in range(1, number_of + 1)]
    width = 1 + sum(loads) // (1 << 30)
    return np.cumsum(np.array([max(1, weight // width) for weight in loads]))


def skewed_ids(own_key, dims, amount, lean):
    grid = cumulative_ranks(amount, lean)
    ticket = jax.random.randint(jax.random.fold_in(own_key, 1), dims, 0, int(grid[amount - 1]))
    grade = jnp.searchsorted(jnp.asarray(grid, jnp.int32), ticket, side="right")
    return jax.random.permutation(jax.random.fold_in(own_key, 2), amount)[grade].astype(jnp.int32)


def setup_inputs(seed: int = 0) -> dict:
    key_list = jax.random.split(jax.random.key(seed), 9)
    return {
        "teacher_hidden": draw_teacher_hidden(jax.random.fold_in(key_list[8], 71), 0),
        "teacher_gain": jnp.clip(1.0 + 0.1 * jax.random.normal(key_list[1], (BRANCHES, D), jnp.float32), 0.5, 1.5),
        "teacher_head": draw_teacher_head(jax.random.fold_in(key_list[8], 71), 0),
        "student_hidden": draw_student_hidden(jax.random.fold_in(key_list[8], 71), 0),
        "student_gain": jnp.clip(1.0 + 0.1 * jax.random.normal(key_list[4], (D,), jnp.float32), 0.5, 1.5),
        "student_head": draw_student_head(jax.random.fold_in(key_list[8], 71), 0),
        "cluster_weights": draw_cluster_weights(jax.random.fold_in(key_list[8], 71), 0),
        "token_ids": set_ends(skewed_ids(key_list[7], (TOKENS,), V, 2), jax.random.fold_in(key_list[7], 3), 0, V - 1).astype(jnp.int32),
    }


eps = 1e-05
mix_label = 0.25
loss_scale = 64.0

def normalize(hidden, gain):
    values = hidden.astype(jnp.float32)
    inv_scale = lax.rsqrt(lax.optimization_barrier(jnp.mean(values * values, axis=-1, keepdims=True)) + eps)
    return ((values * inv_scale * gain.astype(jnp.float32)).astype(jnp.bfloat16), inv_scale)

def softmax_rows(logits):
    top = lax.optimization_barrier(jnp.max(logits, axis=-1, keepdims=True))
    scaled = jnp.exp(logits - top)
    return scaled / lax.optimization_barrier(jnp.sum(scaled, axis=-1, keepdims=True))

def reference(teacher_hidden, teacher_gain, teacher_head, student_hidden, student_gain, student_head, cluster_weights, token_ids):
    mixed = jnp.zeros((TOKENS, V), jnp.float32)
    for branch_index in range(BRANCHES):
        normed, unused_scale = normalize(teacher_hidden[branch_index], teacher_gain[branch_index])
        logits = jnp.dot(normed, teacher_head[branch_index], preferred_element_type=jnp.float32)
        weight = cluster_weights[:, branch_index].astype(jnp.float32) / DEN
        mixed = mixed + softmax_rows(logits) * weight[:, None]
    onehot = (token_ids[:, None] == jnp.arange(V, dtype=jnp.int32)[None, :]).astype(jnp.float32)
    targets = (1.0 - mix_label) * mixed + mix_label * onehot
    student_normed, inv_scale = normalize(student_hidden, student_gain)
    student_probs = softmax_rows(jnp.dot(student_normed, student_head, preferred_element_type=jnp.float32))
    logit_grads = (loss_scale * (student_probs - targets)).astype(jnp.bfloat16)
    grad_head = jnp.dot(student_normed.T, logit_grads, preferred_element_type=jnp.float32)
    normed_grads = jnp.dot(logit_grads, student_head.T, preferred_element_type=jnp.float32)
    values = student_hidden.astype(jnp.float32)
    gain = student_gain.astype(jnp.float32)
    grad_gain = lax.optimization_barrier(jnp.sum(normed_grads * values * inv_scale, axis=0))
    row_dots = lax.optimization_barrier(jnp.sum(gain[None, :] * normed_grads * values, axis=1, keepdims=True))
    grad_hidden = inv_scale * gain[None, :] * normed_grads - values * inv_scale ** 3 * row_dots / D
    return (grad_head, grad_hidden, grad_gain)
```

```python
import functools

import jax
import jax.numpy as jnp
from jax import lax
from jax.experimental import pallas as pl
from jax.experimental.pallas import tpu as pltpu
from jax.sharding import PartitionSpec as P

DEN = 64

eps = 1e-05
mix_label = 0.25
loss_scale = 64.0


def swap(value, axis, flip):
    size = lax.axis_size(axis)
    return lax.ppermute(value, axis, [(i, i ^ flip) for i in range(size)])


def normalize(hidden, gain):
    values = hidden.astype(jnp.float32)
    inv_scale = lax.rsqrt(jnp.mean(values * values, axis=-1, keepdims=True) + eps)
    return ((values * inv_scale * gain).astype(jnp.bfloat16), inv_scale)


def gather_blocks(block, size):
    got = {0: block}
    for k in range(4, size, 4):
        got[k] = swap(block, "tok", k)
    for k in range(0, size, 4):
        got[k + 2] = swap(got[k], "tok", 2)
    evens = sorted(got)
    half = len(evens) // 2
    for part in (evens[:half], evens[half:]):
        joined = swap(jnp.concatenate([got[k] for k in part], axis=0), "tok", 1)
        for place, k in enumerate(part):
            got[k + 1] = lax.slice_in_dim(joined, place * block.shape[0], (place + 1) * block.shape[0])
    return got


def grad_kernel(place_ref, g_ref, w_ref, out_ref):
    acc = lax.dot_general(g_ref[...], w_ref[...], (((1,), (1,)), ((), ())), preferred_element_type=jnp.float32)
    rows = out_ref.shape[2]
    count = out_ref.shape[0]
    parts = [acc[k * rows : (k + 1) * rows].astype(out_ref.dtype) for k in range(count)]
    for k in range(count):
        for r in range(count):

            @pl.when((place_ref[1] ^ k) == r)
            def _():
                out_ref[k, 0] = parts[r]


def normed_grad_pieces(grads, head, place, blocks, branches):
    tokens, cols = grads.shape
    width = head.shape[0] // blocks
    rows = tokens // branches
    return pl.pallas_call(
        grad_kernel,
        out_shape=jax.ShapeDtypeStruct((branches, blocks, rows, width), jnp.bfloat16),
        grid_spec=pltpu.PrefetchScalarGridSpec(
            num_scalar_prefetch=1,
            grid=(blocks,),
            in_specs=[
                pl.BlockSpec((tokens, cols), lambda i, place: (0, 0)),
                pl.BlockSpec((width, cols), lambda i, place: (i ^ place[0], 0)),
            ],
            out_specs=pl.BlockSpec((branches, 1, rows, width), lambda i, place: (0, i, 0, 0)),
        ),
        cost_estimate=pl.CostEstimate(
            flops=2 * tokens * cols * head.shape[0], bytes_accessed=2 * head.size + 4 * grads.size, transcendentals=0
        ),
    )(place, grads, head)


def per_device(
    teacher_hidden,
    teacher_gain,
    teacher_head,
    student_hidden,
    student_gain,
    student_head,
    cluster_weights,
    token_ids,
):
    branches = lax.axis_size("branch")
    size = lax.axis_size("tok")
    b = lax.axis_index("branch")
    t = lax.axis_index("tok")
    rows, width = student_hidden.shape
    head_cols = teacher_head.shape[2]
    part = width // branches
    blocks = size // branches
    f32 = jnp.float32

    student_normed, inv_scale = normalize(student_hidden, student_gain)

    def features(r):
        return lax.dynamic_slice_in_dim(student_normed, (b ^ r) * part, part, 1)

    student_parts = [features(0)] + [swap(features(r), "branch", r) for r in range(1, branches)]
    student_rows = jnp.concatenate(student_parts, axis=0)

    teacher_block, unused = normalize(teacher_hidden[0], teacher_gain[0])
    got = gather_blocks(teacher_block, size)
    count = teacher_block.shape[0]
    teacher_rows = jnp.zeros((count * size, width), jnp.bfloat16)
    for k in range(size):
        place = (t ^ k) ^ (b * blocks)
        teacher_rows = lax.dynamic_update_slice_in_dim(teacher_rows, got[k], place * count, 0)

    partial_logits = jnp.dot(student_rows, student_head, preferred_element_type=f32)
    logits = partial_logits[:rows]
    for r in range(1, branches):
        logits = logits + swap(partial_logits[r * rows : (r + 1) * rows], "branch", r)
    student_max = jnp.max(logits, axis=1)
    student_exp = jnp.exp(logits - student_max[:, None])
    student_sum = jnp.sum(student_exp, axis=1)

    teacher_logits = jnp.dot(teacher_rows, teacher_head[0], preferred_element_type=f32)
    teacher_max = jnp.max(teacher_logits, axis=1)
    teacher_exp = jnp.exp(teacher_logits - teacher_max[:, None])
    teacher_sum = jnp.sum(teacher_exp, axis=1)
    teacher_exp = teacher_exp.astype(jnp.bfloat16)
    terms = [teacher_exp[:rows]] + [
        swap(teacher_exp[r * rows : (r + 1) * rows], "branch", r) for r in range(1, branches)
    ]

    order = jnp.arange(branches) ^ b
    weights = cluster_weights[:, 0].astype(f32).reshape(branches, rows)
    stats = jnp.stack(
        [
            teacher_max.reshape(branches, rows)[order],
            teacher_sum.reshape(branches, rows)[order],
            weights,
            jnp.broadcast_to(student_max, (branches, rows)),
            jnp.broadcast_to(student_sum, (branches, rows)),
        ],
        axis=1,
    )
    stats = jnp.broadcast_to(stats[:, None], (branches, size, 5, rows)).reshape(branches * size, 5, rows)
    stats = lax.all_to_all(stats, ("branch", "tok"), 0, 0, tiled=True).reshape(branches, size, 5, rows)
    peak = jnp.max(stats[:, :, 0], axis=1)
    total = jnp.sum(stats[:, :, 1] * jnp.exp(stats[:, :, 0] - peak[:, None]), axis=1)
    here = lax.dynamic_index_in_dim(stats, t, 1, keepdims=False)
    scale = ((1.0 - mix_label) / DEN) * here[:, 2] * jnp.exp(here[:, 0] - peak) / total
    scale = scale[order]
    student_stats = lax.dynamic_index_in_dim(stats, b, 0, keepdims=False)
    student_peak = jnp.max(student_stats[:, 3], axis=0)
    student_total = jnp.sum(student_stats[:, 4] * jnp.exp(student_stats[:, 3] - student_peak), axis=0)
    student_scale = jnp.exp(student_max - student_peak) / student_total

    ids = token_ids - t * head_cols
    onehot = (ids[:, None] == jnp.arange(head_cols, dtype=jnp.int32)[None, :]).astype(f32)
    targets = mix_label * onehot
    for r in range(branches):
        targets = targets + terms[r].astype(f32) * scale[r][:, None]
    logit_grads = (loss_scale * (student_exp * student_scale[:, None] - targets)).astype(jnp.bfloat16)
    dots = jnp.sum(logit_grads.astype(f32) * logits, axis=1)
    all_grads = jnp.concatenate(
        [logit_grads] + [swap(logit_grads, "branch", r) for r in range(1, branches)], axis=0
    )

    place = jnp.stack([t % blocks, (t // blocks) ^ b]).astype(jnp.int32)
    pieces = normed_grad_pieces(all_grads, student_head, place, blocks, branches)
    pieces = pieces.reshape(size // 2, 2, rows, width // size)
    core = pieces[:, 0].astype(f32) + swap(pieces[:, 1], "tok", 1).astype(f32)
    core = core.astype(jnp.bfloat16).reshape(size // 4, 2, rows, width // size)
    pair = core[:, 0].astype(f32) + swap(core[:, 1], "tok", 2).astype(f32)
    sent = pair.astype(jnp.bfloat16)
    normed_grads = pair[0]
    for k in range(1, size // 4):
        normed_grads = normed_grads + swap(sent[k], "tok", 4 * k).astype(f32)
    perm = []
    for i in range(branches * size):
        bb, h, q = i // size, (i % size) // blocks, i % blocks
        perm.append((i, (h * branches + bb) * blocks + q))
    normed_grads = lax.ppermute(normed_grads, ("branch", "tok"), perm)
    row_dots = lax.psum(dots, "tok") / inv_scale[:, 0]

    slice_width = width // size
    hidden_cols = lax.dynamic_slice_in_dim(student_hidden, t * slice_width, slice_width, 1).astype(f32)
    gain_cols = lax.dynamic_slice_in_dim(student_gain, t * slice_width, slice_width, 0)
    grad_gain = jnp.sum(normed_grads * hidden_cols * inv_scale, axis=0)
    flip = 1
    while flip < branches:
        grad_gain = grad_gain + swap(grad_gain, "branch", flip)
        flip *= 2
    grad_hidden = (
        inv_scale * gain_cols[None, :] * normed_grads
        - hidden_cols * inv_scale**3 * row_dots[:, None] / width
    )
    grad_head = lax.dot_general(
        student_rows, all_grads, (((0,), (0,)), ((), ())), preferred_element_type=f32
    )
    return (grad_head, grad_hidden, grad_gain)


def solution(mesh):
    in_specs = (
        P("branch", "tok", None),
        P("branch", None),
        P("branch", None, "tok"),
        P("branch", None),
        P(),
        P("branch", "tok"),
        P(None, "branch"),
        P("branch"),
    )
    out_specs = (P("branch", "tok"), P("branch", "tok"), P("tok"))
    return jax.shard_map(
        per_device, mesh=mesh, in_specs=in_specs, out_specs=out_specs, check_vma=False
    )
```

```python
import functools

import jax
import jax.numpy as jnp
from jax import lax
from jax.experimental import pallas as pl
from jax.experimental.pallas import tpu as pltpu
from jax.sharding import PartitionSpec as P

DEN = 64

eps = 1e-05
mix_label = 0.25
loss_scale = 64.0


def swap(value, axis, flip):
    size = lax.axis_size(axis)
    return lax.ppermute(value, axis, [(i, i ^ flip) for i in range(size)])


def normalize(hidden, gain):
    values = hidden.astype(jnp.float32)
    inv_scale = lax.rsqrt(jnp.mean(values * values, axis=-1, keepdims=True) + eps)
    return ((values * inv_scale * gain).astype(jnp.bfloat16), inv_scale)


def gather_blocks(block, size):
    got = {0: block}
    for k in range(4, size, 4):
        got[k] = swap(block, "tok", k)
    for k in range(0, size, 4):
        got[k + 2] = swap(got[k], "tok", 2)
    evens = sorted(got)
    half = len(evens) // 2
    arrays = [got[k] for k in evens]
    keys = [(k,) for k in evens]
    for group in (evens[:half], evens[half:]):
        arrays.append(swap(jnp.concatenate([got[k] for k in group], axis=0), "tok", 1))
        keys.append(tuple(k + 1 for k in group))
    return arrays, tuple(keys)


def tile_of(cols):
    return next((tile for tile in (256, 128) if cols % tile == 0), cols)


def column(row):
    count = row.shape[1]
    return jnp.transpose(jnp.broadcast_to(row, (128, count)))[:, :1]


def as_row(col):
    return jnp.transpose(jnp.broadcast_to(col, (col.shape[0], 128)))[:1]


def teacher_kernel(keys, half, place_ref, *refs):
    blocks = refs[: len(keys)]
    w_ref, exp_ref, stat_ref, rows_ref, logits_ref = refs[len(keys) :]
    step = pl.program_id(0)

    @pl.when(step == 0)
    def _():
        mine = place_ref[1] ^ (place_ref[0] * half)
        for ref, owned in zip(blocks, keys):
            count = ref.shape[0] // len(owned)
            for j, k in enumerate(owned):
                start = pl.multiple_of((mine ^ k) * count, count)
                rows_ref[pl.ds(start, count), :] = ref[j * count : (j + 1) * count, :]

    tile = w_ref.shape[2]
    place = pl.ds(pl.multiple_of(step * tile, tile), tile) if tile < logits_ref.shape[1] else slice(None)
    logits_ref[:, place] = jnp.dot(rows_ref[...], w_ref[0], preferred_element_type=jnp.float32)

    @pl.when(step == pl.num_programs(0) - 1)
    def _():
        logits = logits_ref[...]
        top = jnp.max(logits, axis=1, keepdims=True)
        scaled = jnp.exp(logits - top)
        exp_ref[...] = scaled.astype(exp_ref.dtype)
        stat_ref[0:1, :] = as_row(top)
        stat_ref[1:2, :] = as_row(jnp.sum(scaled, axis=1, keepdims=True))


def teacher_softmax(got, keys, head, place, half):
    width, cols = head.shape[1:]
    tokens = sum(part.shape[0] for part in got)
    tile = tile_of(cols)
    return pl.pallas_call(
        functools.partial(teacher_kernel, keys, half),
        out_shape=(
            jax.ShapeDtypeStruct((tokens, cols), jnp.bfloat16),
            jax.ShapeDtypeStruct((2, tokens), jnp.float32),
        ),
        grid_spec=pltpu.PrefetchScalarGridSpec(
            num_scalar_prefetch=1,
            grid=(cols // tile,),
            in_specs=[pl.BlockSpec(part.shape, lambda i, place: (0, 0)) for part in got]
            + [pl.BlockSpec((1, width, tile), lambda i, place: (0, 0, i))],
            out_specs=(
                pl.BlockSpec((tokens, cols), lambda i, place: (0, 0)),
                pl.BlockSpec((2, tokens), lambda i, place: (0, 0)),
            ),
            scratch_shapes=[pltpu.VMEM((tokens, width), jnp.bfloat16), pltpu.VMEM((tokens, cols), jnp.float32)],
        ),
        cost_estimate=pl.CostEstimate(
            flops=2 * tokens * width * cols, bytes_accessed=2 * width * cols, transcendentals=tokens * cols
        ),
        name="teacher",
    )(place, *got, head)


def stats_kernel(count, place_ref, *refs):
    parts = refs[:count]
    teacher_ref, weight_ref, logits_ref, out_ref = refs[count:]
    logits = parts[0][...]
    for ref in parts[1:]:
        logits = logits + ref[...]
    logits_ref[...] = logits
    top = jnp.max(logits, axis=1, keepdims=True)
    total = jnp.sum(jnp.exp(logits - top), axis=1, keepdims=True)
    rows = logits.shape[0]
    size = out_ref.shape[0] // count
    student = jnp.concatenate([as_row(top), as_row(total)], axis=0)
    for r in range(count):
        there = place_ref[0] ^ r
        block = jnp.concatenate(
            [
                teacher_ref[:, r * rows : (r + 1) * rows],
                student,
                weight_ref[pl.ds(there, 1), :],
                jnp.zeros((3, rows), jnp.float32),
            ],
            axis=0,
        )
        out_ref[pl.ds(there * size, size)] = jnp.broadcast_to(block[None], (size, 8, rows))


def student_stats(parts, teacher_stats, weights, place, size):
    rows, cols = parts[0].shape
    count = len(parts)
    vmem = pl.BlockSpec(memory_space=pltpu.VMEM)
    return pl.pallas_call(
        functools.partial(stats_kernel, count),
        out_shape=(
            jax.ShapeDtypeStruct((rows, cols), jnp.float32),
            jax.ShapeDtypeStruct((count * size, 8, rows), jnp.float32),
        ),
        in_specs=[pl.BlockSpec(memory_space=pltpu.SMEM)] + [vmem] * (count + 2),
        out_specs=(vmem, vmem),
        cost_estimate=pl.CostEstimate(flops=8 * rows * cols, bytes_accessed=12 * rows * cols, transcendentals=rows * cols),
        name="stats",
    )(place, *parts, teacher_stats, weights)


def grads_kernel(count, size, place_ref, stats_ref, logits_ref, ids_ref, *refs):
    terms = refs[:count]
    grads_ref, dots_ref = refs[count:]
    b, t = place_ref[0], place_ref[1]
    rows, cols = logits_ref.shape
    logits = logits_ref[...]
    shard = lax.broadcasted_iota(jnp.int32, (rows, cols), 1)
    targets = jnp.where(shard == ids_ref[...] - t * cols, mix_label, 0.0)
    probs = None
    for r in range(count):
        start = (b ^ r) * size
        block = stats_ref[pl.ds(start, size)]
        here = stats_ref[start + t]
        peak = jnp.max(block[:, 0, :], axis=0, keepdims=True)
        total = jnp.sum(block[:, 1, :] * jnp.exp(block[:, 0, :] - peak), axis=0, keepdims=True)
        scale = ((1.0 - mix_label) / DEN) * here[4:5] * jnp.exp(here[0:1] - peak) / total
        targets = targets + terms[r][...].astype(jnp.float32) * column(scale)
        if r == 0:
            peak = jnp.max(block[:, 2, :], axis=0, keepdims=True)
            total = jnp.sum(block[:, 3, :] * jnp.exp(block[:, 2, :] - peak), axis=0, keepdims=True)
            probs = jnp.exp(logits - column(peak)) / column(total)
    grads = (loss_scale * (probs - targets)).astype(grads_ref.dtype)
    grads_ref[...] = grads
    dots = as_row(jnp.sum(grads.astype(jnp.float32) * logits, axis=1, keepdims=True))
    dots_ref[...] = jnp.broadcast_to(dots[None], dots_ref.shape)


def make_grads(stats, logits, ids, terms, place, size):
    rows, cols = logits.shape
    count = len(terms)
    vmem = pl.BlockSpec(memory_space=pltpu.VMEM)
    return pl.pallas_call(
        functools.partial(grads_kernel, count, size),
        out_shape=(
            jax.ShapeDtypeStruct((rows, cols), jnp.bfloat16),
            jax.ShapeDtypeStruct((size, 8, rows), jnp.float32),
        ),
        in_specs=[pl.BlockSpec(memory_space=pltpu.SMEM)] + [vmem] * (count + 3),
        out_specs=(vmem, vmem),
        cost_estimate=pl.CostEstimate(flops=16 * rows * cols, bytes_accessed=10 * rows * cols, transcendentals=rows * cols),
        name="grads",
    )(place, stats, logits, ids, *terms)


def pieces_kernel(count, place_ref, *refs):
    grads = refs[:count]
    w_ref, out_ref, turned_ref = refs[count:]
    rows = grads[0].shape[0]

    @pl.when(pl.program_id(0) == 0)
    def _():
        for r in range(count):
            turned_ref[:, r * rows : (r + 1) * rows] = jnp.transpose(grads[r][...])

    acc = jnp.dot(w_ref[...], turned_ref[...], preferred_element_type=jnp.float32)
    parts = [acc[:, r * rows : (r + 1) * rows].astype(out_ref.dtype) for r in range(count)]
    for k in range(count):
        for r in range(count):

            @pl.when((place_ref[3] ^ k) == r)
            def _():
                out_ref[k, 0] = parts[r]


def normed_grad_pieces(grads, head, place, blocks):
    count = len(grads)
    rows, cols = grads[0].shape
    width = head.shape[0] // blocks
    return pl.pallas_call(
        functools.partial(pieces_kernel, count),
        out_shape=jax.ShapeDtypeStruct((count, blocks, width, rows), jnp.bfloat16),
        grid_spec=pltpu.PrefetchScalarGridSpec(
            num_scalar_prefetch=1,
            grid=(blocks,),
            in_specs=[pl.BlockSpec((rows, cols), lambda i, place: (0, 0))] * count
            + [pl.BlockSpec((width, cols), lambda i, place: (i ^ place[2], 0))],
            out_specs=pl.BlockSpec((count, 1, width, rows), lambda i, place: (0, i, 0, 0)),
            scratch_shapes=[pltpu.VMEM((cols, count * rows), jnp.bfloat16)],
        ),
        cost_estimate=pl.CostEstimate(
            flops=2 * count * rows * cols * head.shape[0], bytes_accessed=2 * head.size, transcendentals=0
        ),
        name="pieces",
    )(place, *grads, head)


def per_device(
    teacher_hidden,
    teacher_gain,
    teacher_head,
    student_hidden,
    student_gain,
    student_head,
    cluster_weights,
    token_ids,
):
    branches = lax.axis_size("branch")
    size = lax.axis_size("tok")
    b = lax.axis_index("branch")
    t = lax.axis_index("tok")
    rows, width = student_hidden.shape
    part = width // branches
    blocks = size // branches
    f32 = jnp.float32
    place = jnp.stack([b, t, t % blocks, (t // blocks) ^ b]).astype(jnp.int32)

    student_normed, inv_scale = normalize(student_hidden, student_gain)
    core = t % 2
    half = rows // 2

    def fetched(r):
        sent = lax.dynamic_slice(student_normed, (core * half, (b ^ r) * part), (half, part))
        mine = swap(sent, "branch", r)
        other = swap(mine, "tok", 1)
        first = core == 0
        return jnp.concatenate([jnp.where(first, mine, other), jnp.where(first, other, mine)], axis=0)

    student_parts = [lax.dynamic_slice_in_dim(student_normed, b * part, part, 1)]
    student_parts += [fetched(r) for r in range(1, branches)]
    own_partial = jnp.dot(student_parts[0], student_head, preferred_element_type=f32)
    partials = [own_partial]
    for r in range(1, branches):
        partial = jnp.dot(student_parts[r], student_head, preferred_element_type=f32)
        partials.append(swap(partial, "branch", r))

    teacher_block, unused = normalize(teacher_hidden[0], teacher_gain[0])
    got, keys = gather_blocks(teacher_block, size)
    teacher_exp, teacher_stats = teacher_softmax(got, keys, teacher_head, place, blocks)
    terms = [teacher_exp[:rows]] + [
        swap(teacher_exp[r * rows : (r + 1) * rows], "branch", r) for r in range(1, branches)
    ]

    weights = cluster_weights[:, 0].astype(f32).reshape(branches, rows)
    logits, stats = student_stats(partials, teacher_stats, weights, place, size)
    stats = lax.all_to_all(stats, ("branch", "tok"), 0, 0, tiled=True)
    logit_grads, dots = make_grads(stats, logits, token_ids[:, None], terms, place, size)
    all_grads = [logit_grads] + [swap(logit_grads, "branch", r) for r in range(1, branches)]
    dots = lax.all_to_all(dots, "tok", 0, 0, tiled=True)
    row_dots = jnp.sum(dots[:, 0], axis=0) / inv_scale[:, 0]

    pieces = normed_grad_pieces(all_grads, student_head, place, blocks)
    piece = (width // size, rows)
    pieces = pieces.reshape(size // 2, 2, *piece)
    pieces = (pieces[:, 0].astype(f32) + swap(pieces[:, 1], "tok", 1).astype(f32)).astype(jnp.bfloat16)
    pieces = pieces.reshape(size // 4, 2, *piece)
    pair = pieces[:, 0].astype(f32) + swap(pieces[:, 1], "tok", 2).astype(f32)
    sent = pair.astype(jnp.bfloat16)
    normed_grads = pair[0]
    for k in range(1, size // 4):
        normed_grads = normed_grads + swap(sent[k], "tok", 4 * k).astype(f32)
    perm = []
    for i in range(branches * size):
        bb, h, q = i // size, (i % size) // blocks, i % blocks
        perm.append((i, (h * branches + bb) * blocks + q))
    normed_grads = lax.ppermute(normed_grads, ("branch", "tok"), perm).T

    slice_width = width // size
    hidden_cols = lax.dynamic_slice_in_dim(student_hidden, t * slice_width, slice_width, 1).astype(f32)
    gain_cols = lax.dynamic_slice_in_dim(student_gain, t * slice_width, slice_width, 0)
    grad_gain = jnp.sum(normed_grads * hidden_cols * inv_scale, axis=0)
    flip = 1
    while flip < branches:
        grad_gain = grad_gain + swap(grad_gain, "branch", flip)
        flip *= 2
    grad_hidden = (
        inv_scale * gain_cols[None, :] * normed_grads
        - hidden_cols * inv_scale**3 * row_dots[:, None] / width
    )
    grad_head = lax.dot_general(
        jnp.concatenate(student_parts, axis=0),
        jnp.concatenate(all_grads, axis=0),
        (((0,), (0,)), ((), ())),
        preferred_element_type=f32,
    )
    return (grad_head, grad_hidden, grad_gain)


def solution(mesh):
    in_specs = (
        P("branch", "tok", None),
        P("branch", None),
        P("branch", None, "tok"),
        P("branch", None),
        P(),
        P("branch", "tok"),
        P(None, "branch"),
        P("branch"),
    )
    out_specs = (P("branch", "tok"), P("branch", "tok"), P("tok"))
    return jax.shard_map(
        per_device, mesh=mesh, in_specs=in_specs, out_specs=out_specs, check_vma=False
    )
```

```python
import functools

import jax
import jax.numpy as jnp
from jax import lax
from jax.experimental import pallas as pl
from jax.experimental.pallas import tpu as pltpu
from jax.sharding import PartitionSpec as P


DEN = 64

eps = 1e-05
mix_label = 0.25
loss_scale = 64.0


def swap(value, axis, flip):
    size = lax.axis_size(axis)
    return lax.ppermute(value, axis, [(i, i ^ flip) for i in range(size)])


VMEM = pl.BlockSpec(memory_space=pltpu.VMEM)
SMEM = pl.BlockSpec(memory_space=pltpu.SMEM)
MIB = 1 << 20


def params(mib):
    return pltpu.CompilerParams(vmem_limit_bytes=mib * MIB)


def cost(flops, nbytes, exps=0):
    return pl.CostEstimate(flops=flops, bytes_accessed=nbytes, transcendentals=exps)


def first_kernel(branches, place_ref, th_ref, tg_ref, sh_ref, sg_ref, block_ref, own_ref, inv_ref, *refs):
    sent, normed_ref = refs[:-1], refs[-1]
    values = th_ref[0].astype(jnp.float32)
    scale = lax.rsqrt(jnp.mean(values * values, axis=-1, keepdims=True) + eps)
    block_ref[...] = (values * scale * tg_ref[...]).astype(jnp.bfloat16)
    values = sh_ref[...].astype(jnp.float32)
    scale = lax.rsqrt(jnp.mean(values * values, axis=-1, keepdims=True) + eps)
    inv_ref[...] = scale
    normed_ref[...] = (values * scale * sg_ref[...]).astype(jnp.bfloat16)
    part = own_ref.shape[1]
    half = own_ref.shape[0] // 2
    b = place_ref[0]
    own_ref[...] = normed_ref[:, pl.ds(pl.multiple_of(b * part, part), part)]
    start = pl.multiple_of((place_ref[1] % 2) * half, half)
    for r in range(1, branches):
        cols = pl.ds(pl.multiple_of((b ^ r) * part, part), part)
        sent[r - 1][...] = normed_ref[pl.ds(start, half), cols]


def normalize_all(teacher_hidden, teacher_gain, student_hidden, student_gain, place, branches):
    rows, width = student_hidden.shape
    part = width // branches
    bf16 = jnp.bfloat16
    return pl.pallas_call(
        functools.partial(first_kernel, branches),
        out_shape=(
            jax.ShapeDtypeStruct(teacher_hidden.shape[1:], bf16),
            jax.ShapeDtypeStruct((rows, part), bf16),
            jax.ShapeDtypeStruct((rows, 1), jnp.float32),
            *[jax.ShapeDtypeStruct((rows // 2, part), bf16)] * (branches - 1),
        ),
        in_specs=[SMEM] + [VMEM] * 4,
        out_specs=(VMEM,) * (2 + branches),
        scratch_shapes=[pltpu.VMEM((rows, width), bf16)],
        compiler_params=params(16),
        cost_estimate=cost(8 * rows * width, 4 * rows * width),
        name="first",
    )(place, teacher_hidden, teacher_gain, student_hidden, student_gain[None])


def gather_blocks(block, size):
    got = {0: block}
    for k in range(4, size, 4):
        got[k] = swap(block, "tok", k)
    for k in range(0, size, 4):
        got[k + 2] = swap(got[k], "tok", 2)
    evens = sorted(got)
    half = len(evens) // 2
    arrays = [got[k] for k in evens]
    keys = [(k,) for k in evens]
    for group in (evens[:half], evens[half:]):
        arrays.append(swap(jnp.concatenate([got[k] for k in group], axis=0), "tok", 1))
        keys.append(tuple(k + 1 for k in group))
    return arrays, tuple(keys)


def own_dot_kernel(rows_ref, w_ref, out_ref):
    out_ref[...] = jnp.dot(rows_ref[...], w_ref[...], preferred_element_type=jnp.float32)


def own_dot(rows, head):
    return pl.pallas_call(
        own_dot_kernel,
        out_shape=jax.ShapeDtypeStruct((rows.shape[0], head.shape[1]), jnp.float32),
        in_specs=[VMEM, VMEM],
        out_specs=VMEM,
        compiler_params=params(16),
        cost_estimate=cost(2 * rows.size * head.shape[1], 2 * head.size),
        name="owndot",
    )(rows, head)


def other_dot_kernel(place_ref, mine_ref, other_ref, w_ref, out_ref, rows_ref):
    half = mine_ref.shape[0]
    core = place_ref[1] % 2
    rows_ref[pl.ds(pl.multiple_of(core * half, half), half), :] = mine_ref[...]
    rows_ref[pl.ds(pl.multiple_of((1 - core) * half, half), half), :] = other_ref[...]
    out_ref[...] = jnp.dot(rows_ref[...], w_ref[...], preferred_element_type=jnp.float32)


def other_dot(mine, other, head, place):
    rows = 2 * mine.shape[0]
    return pl.pallas_call(
        other_dot_kernel,
        out_shape=(
            jax.ShapeDtypeStruct((rows, head.shape[1]), jnp.float32),
            jax.ShapeDtypeStruct((rows, mine.shape[1]), jnp.bfloat16),
        ),
        in_specs=[SMEM, VMEM, VMEM, VMEM],
        out_specs=(VMEM, VMEM),
        compiler_params=params(16),
        cost_estimate=cost(2 * rows * head.size, 2 * head.size),
        name="otherdot",
    )(place, mine, other, head)


def tile_of(cols):
    return next((tile for tile in (256, 128) if cols % tile == 0), cols)


def column(row):
    count = row.shape[1]
    return jnp.transpose(jnp.broadcast_to(row, (128, count)))[:, :1]


def as_row(col):
    return jnp.transpose(jnp.broadcast_to(col, (col.shape[0], 128)))[:1]


def teacher_kernel(keys, half, place_ref, *refs):
    blocks = refs[: len(keys)]
    w_ref, stat_ref, *exps = refs[len(keys) : -2]
    rows_ref, logits_ref = refs[-2:]
    mine = place_ref[1] ^ (place_ref[0] * half)
    for ref, owned in zip(blocks, keys):
        count = ref.shape[0] // len(owned)
        for j, k in enumerate(owned):
            start = pl.multiple_of((mine ^ k) * count, count)
            rows_ref[pl.ds(start, count), :] = ref[j * count : (j + 1) * count, :]

    cols = w_ref.shape[2]
    tile = tile_of(cols)
    if tile == cols:
        logits_ref[...] = jnp.dot(rows_ref[...], w_ref[0], preferred_element_type=jnp.float32)
    else:

        @pl.loop(0, cols // tile)
        def _(step):
            at = pl.ds(pl.multiple_of(step * tile, tile), tile)
            logits_ref[:, at] = jnp.dot(rows_ref[...], w_ref[0, :, at], preferred_element_type=jnp.float32)

    logits = logits_ref[...]
    top = jnp.max(logits, axis=1, keepdims=True)
    scaled = jnp.exp(logits - top)
    rows = exps[0].shape[0]
    for r, ref in enumerate(exps):
        ref[...] = scaled[r * rows : (r + 1) * rows].astype(ref.dtype)
    stat_ref[0:1, :] = as_row(top)
    stat_ref[1:2, :] = as_row(jnp.sum(scaled, axis=1, keepdims=True))


def teacher_softmax(got, keys, head, place, half, branches):
    width, cols = head.shape[1:]
    tokens = sum(part.shape[0] for part in got)
    return pl.pallas_call(
        functools.partial(teacher_kernel, keys, half),
        out_shape=(
            jax.ShapeDtypeStruct((2, tokens), jnp.float32),
            *[jax.ShapeDtypeStruct((tokens // branches, cols), jnp.bfloat16)] * branches,
        ),
        in_specs=[SMEM] + [VMEM] * (len(got) + 1),
        out_specs=(VMEM,) * (1 + branches),
        scratch_shapes=[pltpu.VMEM((tokens, width), jnp.bfloat16), pltpu.VMEM((tokens, cols), jnp.float32)],
        compiler_params=params(28),
        cost_estimate=cost(2 * tokens * width * cols, 2 * width * cols, tokens * cols),
        name="teacher",
    )(place, *got, head)


def stats_kernel(count, place_ref, *refs):
    parts = refs[:count]
    teacher_ref, weight_ref, logits_ref, out_ref = refs[count:]
    logits = parts[0][...]
    for ref in parts[1:]:
        logits = logits + ref[...]
    logits_ref[...] = logits
    top = jnp.max(logits, axis=1, keepdims=True)
    total = jnp.sum(jnp.exp(logits - top), axis=1, keepdims=True)
    rows = logits.shape[0]
    size = out_ref.shape[0] // count
    student = jnp.concatenate([as_row(top), as_row(total)], axis=0)
    for r in range(count):
        there = place_ref[0] ^ r
        block = jnp.concatenate(
            [
                teacher_ref[:, r * rows : (r + 1) * rows],
                student,
                weight_ref[pl.ds(there, 1), :].astype(jnp.float32),
                jnp.zeros((3, rows), jnp.float32),
            ],
            axis=0,
        )
        out_ref[pl.ds(there * size, size)] = jnp.broadcast_to(block[None], (size, 8, rows))


def student_stats(parts, teacher_stats, weights, place, size):
    rows, cols = parts[0].shape
    count = len(parts)
    return pl.pallas_call(
        functools.partial(stats_kernel, count),
        out_shape=(
            jax.ShapeDtypeStruct((rows, cols), jnp.float32),
            jax.ShapeDtypeStruct((count * size, 8, rows), jnp.float32),
        ),
        in_specs=[SMEM] + [VMEM] * (count + 2),
        out_specs=(VMEM, VMEM),
        compiler_params=params(12),
        cost_estimate=cost(8 * rows * cols, 12 * rows * cols, rows * cols),
        name="stats",
    )(place, *parts, teacher_stats, weights)


def grads_kernel(count, size, place_ref, stats_ref, logits_ref, ids_ref, *refs):
    terms = refs[:count]
    grads_ref, dots_ref = refs[count:]
    b, t = place_ref[0], place_ref[1]
    rows, cols = logits_ref.shape
    logits = logits_ref[...]
    shard = lax.broadcasted_iota(jnp.int32, (rows, cols), 1)
    targets = jnp.where(shard == column(ids_ref[...]) - t * cols, mix_label, 0.0)
    probs = None
    for r in range(count):
        start = (b ^ r) * size
        block = stats_ref[pl.ds(start, size)]
        here = stats_ref[start + t]
        peak = jnp.max(block[:, 0, :], axis=0, keepdims=True)
        total = jnp.sum(block[:, 1, :] * jnp.exp(block[:, 0, :] - peak), axis=0, keepdims=True)
        scale = ((1.0 - mix_label) / DEN) * here[4:5] * jnp.exp(here[0:1] - peak) / total
        targets = targets + terms[r][...].astype(jnp.float32) * column(scale)
        if r == 0:
            peak = jnp.max(block[:, 2, :], axis=0, keepdims=True)
            total = jnp.sum(block[:, 3, :] * jnp.exp(block[:, 2, :] - peak), axis=0, keepdims=True)
            probs = jnp.exp(logits - column(peak)) / column(total)
    grads = (loss_scale * (probs - targets)).astype(grads_ref.dtype)
    grads_ref[...] = grads
    dots = as_row(jnp.sum(grads.astype(jnp.float32) * logits, axis=1, keepdims=True))
    dots_ref[...] = jnp.broadcast_to(dots[None], dots_ref.shape)


def make_grads(stats, logits, ids, terms, place, size):
    rows, cols = logits.shape
    count = len(terms)
    return pl.pallas_call(
        functools.partial(grads_kernel, count, size),
        out_shape=(
            jax.ShapeDtypeStruct((rows, cols), jnp.bfloat16),
            jax.ShapeDtypeStruct((size, 8, rows), jnp.float32),
        ),
        in_specs=[SMEM] + [VMEM] * (count + 3),
        out_specs=(VMEM, VMEM),
        compiler_params=params(12),
        cost_estimate=cost(16 * rows * cols, 10 * rows * cols, rows * cols),
        name="grads",
    )(place, stats, logits, ids, *terms)


def pieces_kernel(place_ref, grads_ref, w_ref, keep_ref, send_ref, turned_ref):
    turned_ref[...] = jnp.transpose(grads_ref[...])
    width = keep_ref.shape[1]
    for q in range(2 * keep_ref.shape[0]):
        acc = jnp.dot(w_ref[q * width : (q + 1) * width], turned_ref[...], preferred_element_type=jnp.float32)
        acc = acc.astype(keep_ref.dtype)
        k = place_ref[2] ^ q

        @pl.when(k % 2 == 0)
        def _():
            keep_ref[k // 2] = acc

        @pl.when(k % 2 == 1)
        def _():
            send_ref[k // 2] = acc


def normed_grad_pieces(grads, head, place, blocks):
    rows, cols = grads.shape
    width = head.shape[0] // blocks
    return pl.pallas_call(
        pieces_kernel,
        out_shape=(jax.ShapeDtypeStruct((blocks // 2, width, rows), jnp.bfloat16),) * 2,
        in_specs=[SMEM, VMEM, VMEM],
        out_specs=(VMEM, VMEM),
        scratch_shapes=[pltpu.VMEM((cols, rows), jnp.bfloat16)],
        compiler_params=params(16),
        cost_estimate=cost(2 * rows * head.size, 2 * head.size),
        name="pieces",
    )(place, grads, head)


def fold_kernel(mine_ref, got_ref, keep_ref, send_ref):
    for k in range(mine_ref.shape[0]):
        total = mine_ref[k].astype(jnp.float32) + got_ref[k].astype(jnp.float32)
        (send_ref if k % 2 else keep_ref)[k // 2] = total.astype(keep_ref.dtype)


def fold(mine, got):
    count, width, rows = mine.shape
    return pl.pallas_call(
        fold_kernel,
        out_shape=(jax.ShapeDtypeStruct((count // 2, width, rows), mine.dtype),) * 2,
        in_specs=[VMEM, VMEM],
        out_specs=(VMEM, VMEM),
        compiler_params=params(8),
        cost_estimate=cost(mine.size, 6 * mine.size),
        name="fold",
    )(mine, got)


def split_kernel(count, place_ref, *refs):
    mine, got, out = refs[:count], refs[count : 2 * count], refs[2 * count :]
    lows = mine[0].shape[0]
    for r in range(count):
        for low in range(lows):
            total = (mine[r][low].astype(jnp.float32) + got[r][low].astype(jnp.float32)).astype(mine[r].dtype)
            for kh in range(count):

                @pl.when((place_ref[3] ^ kh) == r)
                def _():
                    out[kh * lows + low][...] = total


def split(mine, got, place):
    count = len(mine)
    lows, width, rows = mine[0].shape
    return pl.pallas_call(
        functools.partial(split_kernel, count),
        out_shape=(jax.ShapeDtypeStruct((width, rows), mine[0].dtype),) * (count * lows),
        in_specs=[SMEM] + [VMEM] * (2 * count),
        out_specs=(VMEM,) * (count * lows),
        compiler_params=params(8),
        cost_estimate=cost(count * mine[0].size, 6 * count * mine[0].size),
        name="split",
    )(place, *mine, *got)


def load_kernel(from_ref, to_ref, sem):
    copy = pltpu.make_async_copy(from_ref, to_ref, sem)
    copy.start()
    copy.wait()


def load(value):
    return pl.pallas_call(
        load_kernel,
        out_shape=jax.ShapeDtypeStruct(value.shape, value.dtype),
        in_specs=[pl.BlockSpec(memory_space=pltpu.HBM)],
        out_specs=VMEM,
        scratch_shapes=[pltpu.SemaphoreType.DMA],
        compiler_params=params(16),
        cost_estimate=cost(0, 4 * value.size),
        name="load",
    )(value)


def head_grad_kernel(count, *refs):
    grads, parts = refs[:count], refs[count : 2 * count]
    out_ref, grads_ref = refs[2 * count :]
    rows = grads[0].shape[0]

    @pl.when(pl.program_id(0) == 0)
    def _():
        for r in range(count):
            grads_ref[r * rows : (r + 1) * rows, :] = grads[r][...]

    turned = jnp.transpose(jnp.concatenate([ref[...] for ref in parts], axis=0))
    out_ref[...] = jnp.dot(turned, grads_ref[...], preferred_element_type=jnp.float32)


def head_grad(grads, parts):
    count = len(grads)
    rows, cols = grads[0].shape
    part = parts[0].shape[1]
    tile = tile_of(part)
    return pl.pallas_call(
        functools.partial(head_grad_kernel, count),
        out_shape=jax.ShapeDtypeStruct((part, cols), jnp.float32),
        grid=(part // tile,),
        in_specs=[pl.BlockSpec((rows, cols), lambda i: (0, 0))] * count
        + [pl.BlockSpec((rows, tile), lambda i: (0, i))] * count,
        out_specs=pl.BlockSpec((tile, cols), lambda i: (i, 0)),
        scratch_shapes=[pltpu.VMEM((count * rows, cols), jnp.bfloat16)],
        compiler_params=params(16),
        cost_estimate=cost(2 * count * rows * part * cols, 4 * part * cols),
        name="headgrad",
    )(*grads, *parts)


def last_kernel(count, width, dots_ref, inv_ref, hidden_ref, gain_ref, *refs):
    parts = refs[:count]
    out_ref, gain_out_ref = refs[count:]
    total = parts[0][...].astype(jnp.float32)
    for ref in parts[1:]:
        total = total + ref[...].astype(jnp.float32)
    normed_grads = jnp.transpose(total)
    inv = inv_ref[...]
    hidden = hidden_ref[...].astype(jnp.float32)
    scaled = hidden * inv
    gain_out_ref[...] = jnp.sum(normed_grads * scaled, axis=0, keepdims=True)
    row_dots = column(jnp.sum(dots_ref[:, 0, :], axis=0, keepdims=True))
    out_ref[...] = inv * gain_ref[...] * normed_grads - scaled * (inv * row_dots / width)


def finish(parts, dots, inv, hidden, gain, width):
    piece, rows = parts[0].shape
    return pl.pallas_call(
        functools.partial(last_kernel, len(parts), width),
        out_shape=(
            jax.ShapeDtypeStruct((rows, piece), jnp.float32),
            jax.ShapeDtypeStruct((1, piece), jnp.float32),
        ),
        in_specs=[VMEM] * (4 + len(parts)),
        out_specs=(VMEM, VMEM),
        compiler_params=params(12),
        cost_estimate=cost(16 * rows * piece, 12 * rows * piece),
        name="last",
    )(dots, inv, hidden, gain, *parts)


def per_device(
    teacher_hidden,
    teacher_gain,
    teacher_head,
    student_hidden,
    student_gain,
    student_head,
    cluster_weights,
    token_ids,
):
    branches = lax.axis_size("branch")
    size = lax.axis_size("tok")
    b = lax.axis_index("branch")
    t = lax.axis_index("tok")
    rows, width = student_hidden.shape
    blocks = size // branches
    place = jnp.stack([b, t, t % blocks, (t // blocks) ^ b]).astype(jnp.int32)
    teacher_block, own, inv_scale, *sent = normalize_all(
        teacher_hidden, teacher_gain, student_hidden, student_gain, place, branches
    )

    loaded = load(student_head)
    student_parts, partials = [own], []
    for r in range(1, branches):
        mine = swap(sent[r - 1], "branch", r)
        other = swap(mine, "tok", 1)
        partial, fetched = other_dot(mine, other, loaded, place)
        student_parts.append(fetched)
        partials.append(swap(partial, "branch", r))
    partials = [own_dot(own, loaded)] + partials

    got, keys = gather_blocks(teacher_block, size)
    teacher_stats, *exps = teacher_softmax(got, keys, teacher_head, place, blocks, branches)
    terms = [exps[0]] + [swap(exps[r], "branch", r) for r in range(1, branches)]

    weights = cluster_weights[:, 0].reshape(branches, rows)
    logits, stats = student_stats(partials, teacher_stats, weights, place, size)
    stats = lax.all_to_all(stats, ("branch", "tok"), 0, 0, tiled=True)
    logit_grads, dots = make_grads(stats, logits, token_ids[None], terms, place, size)
    all_grads = [logit_grads] + [swap(logit_grads, "branch", r) for r in range(1, branches)]
    dots = lax.all_to_all(dots, "tok", 0, 0, tiled=True)

    kept, got = [], []
    for r in range(branches):
        keep, send = normed_grad_pieces(all_grads[r], loaded, place, blocks)
        keep, send = fold(keep, swap(send, "tok", 1))
        kept.append(keep)
        got.append(swap(send, "tok", 2))
    owned = split(kept, got, place)
    arrived = []
    for kh in range(branches):
        for kl in range(blocks // 4):
            perm = []
            for i in range(branches * size):
                bb, h, l, rest = i // size, (i % size) // blocks, (i % blocks) // 4, i % 4
                perm.append((i, (h ^ kh) * size + bb * blocks + (l ^ kl) * 4 + rest))
            arrived.append(lax.ppermute(owned[kh * (blocks // 4) + kl], ("branch", "tok"), perm))

    grad_head = head_grad(all_grads, student_parts)

    slice_width = width // size
    hidden_cols = lax.dynamic_slice_in_dim(student_hidden, t * slice_width, slice_width, 1)
    gain_cols = lax.dynamic_slice_in_dim(student_gain, t * slice_width, slice_width, 0)
    grad_hidden, grad_gain = finish(arrived, dots, inv_scale, hidden_cols, gain_cols[None], width)
    flip = 1
    while flip < branches:
        grad_gain = grad_gain + swap(grad_gain, "branch", flip)
        flip *= 2
    return (grad_head, grad_hidden, grad_gain[0])


def solution(mesh):
    in_specs = (
        P("branch", "tok", None),
        P("branch", None),
        P("branch", None, "tok"),
        P("branch", None),
        P(),
        P("branch", "tok"),
        P(None, "branch"),
        P("branch"),
    )
    out_specs = (P("branch", "tok"), P("branch", "tok"), P("tok"))
    return jax.shard_map(per_device, mesh=mesh, in_specs=in_specs, out_specs=out_specs, check_vma=False)
```

```python
import functools

import jax
import jax.numpy as jnp
from jax import lax
from jax.experimental import pallas as pl
from jax.experimental.pallas import tpu as pltpu
from jax.sharding import PartitionSpec as P


DEN = 64

eps = 1e-05
mix_label = 0.25
loss_scale = 64.0


def swap(value, axis, flip):
    size = lax.axis_size(axis)
    return lax.ppermute(value, axis, [(i, i ^ flip) for i in range(size)])


VMEM = pl.BlockSpec(memory_space=pltpu.VMEM)
SMEM = pl.BlockSpec(memory_space=pltpu.SMEM)
MIB = 1 << 20


def params(mib):
    return pltpu.CompilerParams(vmem_limit_bytes=mib * MIB)


def cost(flops, nbytes, exps=0):
    return pl.CostEstimate(flops=flops, bytes_accessed=nbytes, transcendentals=exps)


def first_kernel(branches, place_ref, th_ref, tg_ref, sh_ref, sg_ref, block_ref, own_ref, turned_ref, inv_ref, *refs):
    sent, normed_ref = refs[:-1], refs[-1]
    values = th_ref[0].astype(jnp.float32)
    scale = lax.rsqrt(jnp.mean(values * values, axis=-1, keepdims=True) + eps)
    block_ref[...] = (values * scale * tg_ref[...]).astype(jnp.bfloat16)
    values = sh_ref[...].astype(jnp.float32)
    scale = lax.rsqrt(jnp.mean(values * values, axis=-1, keepdims=True) + eps)
    inv_ref[...] = scale
    normed_ref[...] = (values * scale * sg_ref[...]).astype(jnp.bfloat16)
    part = own_ref.shape[1]
    half = own_ref.shape[0] // 2
    b = place_ref[0]
    own = normed_ref[:, pl.ds(pl.multiple_of(b * part, part), part)]
    own_ref[...] = own
    turned_ref[...] = jnp.transpose(own)
    start = pl.multiple_of((place_ref[1] % 2) * half, half)
    for r in range(1, branches):
        cols = pl.ds(pl.multiple_of((b ^ r) * part, part), part)
        sent[r - 1][...] = normed_ref[pl.ds(start, half), cols]


def normalize_all(teacher_hidden, teacher_gain, student_hidden, student_gain, place, branches):
    rows, width = student_hidden.shape
    part = width // branches
    bf16 = jnp.bfloat16
    return pl.pallas_call(
        functools.partial(first_kernel, branches),
        out_shape=(
            jax.ShapeDtypeStruct(teacher_hidden.shape[1:], bf16),
            jax.ShapeDtypeStruct((rows, part), bf16),
            jax.ShapeDtypeStruct((part, rows), bf16),
            jax.ShapeDtypeStruct((rows, 1), jnp.float32),
            *[jax.ShapeDtypeStruct((rows // 2, part), bf16)] * (branches - 1),
        ),
        in_specs=[SMEM] + [VMEM] * 4,
        out_specs=(VMEM,) * (3 + branches),
        scratch_shapes=[pltpu.VMEM((rows, width), bf16)],
        compiler_params=params(16),
        cost_estimate=cost(8 * rows * width, 4 * rows * width),
        name="first",
    )(place, teacher_hidden, teacher_gain, student_hidden, student_gain[None])


def gather_blocks(block, size):
    got = {0: block}
    for k in range(8, size, 8):
        got[k] = swap(block, "tok", k)
    for k in range(0, size, 8):
        got[k + 4] = swap(got[k], "tok", 4)
    for k in range(0, size, 4):
        got[k + 2] = swap(got[k], "tok", 2)
    evens = sorted(got)
    half = len(evens) // 2
    arrays = [got[k] for k in evens]
    keys = [(k,) for k in evens]
    for group in (evens[:half], evens[half:]):
        arrays.append(swap(jnp.concatenate([got[k] for k in group], axis=0), "tok", 1))
        keys.append(tuple(k + 1 for k in group))
    return arrays, tuple(keys)


def own_dot_kernel(rows_ref, w_ref, out_ref):
    out_ref[...] = jnp.dot(rows_ref[...], w_ref[...], preferred_element_type=jnp.float32)


def own_dot(rows, head):
    return pl.pallas_call(
        own_dot_kernel,
        out_shape=jax.ShapeDtypeStruct((rows.shape[0], head.shape[1]), jnp.float32),
        in_specs=[VMEM, VMEM],
        out_specs=VMEM,
        compiler_params=params(16),
        cost_estimate=cost(2 * rows.size * head.shape[1], 2 * head.size),
        name="owndot",
    )(rows, head)


def other_dot_kernel(place_ref, mine_ref, other_ref, w_ref, out_ref, turned_ref, rows_ref):
    half = mine_ref.shape[0]
    core = place_ref[1] % 2
    rows_ref[pl.ds(pl.multiple_of(core * half, half), half), :] = mine_ref[...]
    rows_ref[pl.ds(pl.multiple_of((1 - core) * half, half), half), :] = other_ref[...]
    out_ref[...] = jnp.dot(rows_ref[...], w_ref[...], preferred_element_type=jnp.float32)
    turned_ref[...] = jnp.transpose(rows_ref[...])


def other_dot(mine, other, head, place):
    rows = 2 * mine.shape[0]
    return pl.pallas_call(
        other_dot_kernel,
        out_shape=(
            jax.ShapeDtypeStruct((rows, head.shape[1]), jnp.float32),
            jax.ShapeDtypeStruct((mine.shape[1], rows), jnp.bfloat16),
        ),
        in_specs=[SMEM, VMEM, VMEM, VMEM],
        out_specs=(VMEM, VMEM),
        scratch_shapes=[pltpu.VMEM((rows, mine.shape[1]), jnp.bfloat16)],
        compiler_params=params(16),
        cost_estimate=cost(2 * rows * head.size, 2 * head.size),
        name="otherdot",
    )(place, mine, other, head)


EXTRA = 8


def extra_rows(values, dtype):
    first = [value.astype(dtype).astype(jnp.float32) for value in values]
    rest = [value - lead for value, lead in zip(values, first)]
    empty = jnp.zeros((EXTRA - 2 * len(values), values[0].shape[1]), jnp.float32)
    return jnp.concatenate(first + rest + [empty], axis=0).astype(dtype)


def extra_values(rows, count):
    rows = rows.astype(jnp.float32)
    return [rows[i : i + 1] + rows[count + i : count + i + 1] for i in range(count)]


def tile_of(cols):
    return next((tile for tile in (256, 128) if cols % tile == 0), cols)


def column(row):
    count = row.shape[1]
    return jnp.transpose(jnp.broadcast_to(row, (128, count)))[:, :1]


def as_row(col):
    return jnp.transpose(jnp.broadcast_to(col, (col.shape[0], 128)))[:1]


def teacher_kernel(keys, half, place_ref, *refs):
    blocks = refs[: len(keys)]
    w_ref, stat_ref, *exps = refs[len(keys) : -2]
    rows_ref, logits_ref = refs[-2:]
    mine = place_ref[1] ^ (place_ref[0] * half)
    for ref, owned in zip(blocks, keys):
        count = ref.shape[0] // len(owned)
        for j, k in enumerate(owned):
            start = pl.multiple_of((mine ^ k) * count, count)
            rows_ref[pl.ds(start, count), :] = ref[j * count : (j + 1) * count, :]

    cols = w_ref.shape[2]
    tile = tile_of(cols)
    if tile == cols:
        logits_ref[...] = jnp.dot(rows_ref[...], w_ref[0], preferred_element_type=jnp.float32)
    else:

        @pl.loop(0, cols // tile)
        def _(step):
            at = pl.ds(pl.multiple_of(step * tile, tile), tile)
            logits_ref[:, at] = jnp.dot(rows_ref[...], w_ref[0, :, at], preferred_element_type=jnp.float32)

    logits = logits_ref[...]
    top = jnp.max(logits, axis=1, keepdims=True)
    scaled = jnp.exp(logits - top)
    rows = exps[0].shape[0]
    for r, ref in enumerate(exps):
        ref[...] = scaled[r * rows : (r + 1) * rows].astype(ref.dtype)
    stat_ref[0:1, :] = as_row(top)
    stat_ref[1:2, :] = as_row(jnp.sum(scaled, axis=1, keepdims=True))


def teacher_softmax(got, keys, head, place, half, branches):
    width, cols = head.shape[1:]
    tokens = sum(part.shape[0] for part in got)
    return pl.pallas_call(
        functools.partial(teacher_kernel, keys, half),
        out_shape=(
            jax.ShapeDtypeStruct((2, tokens), jnp.float32),
            *[jax.ShapeDtypeStruct((tokens // branches, cols), jnp.bfloat16)] * branches,
        ),
        in_specs=[SMEM] + [VMEM] * (len(got) + 1),
        out_specs=(VMEM,) * (1 + branches),
        scratch_shapes=[pltpu.VMEM((tokens, width), jnp.bfloat16), pltpu.VMEM((tokens, cols), jnp.float32)],
        compiler_params=params(28),
        cost_estimate=cost(2 * tokens * width * cols, 2 * width * cols, tokens * cols),
        name="teacher",
    )(place, *got, head)


def stats_kernel(count, place_ref, *refs):
    parts = refs[:count]
    teacher_ref, weight_ref, logits_ref, out_ref = refs[count:]
    logits = parts[0][...]
    for ref in parts[1:]:
        logits = logits + ref[...]
    logits_ref[...] = logits
    top = jnp.max(logits, axis=1, keepdims=True)
    total = jnp.sum(jnp.exp(logits - top), axis=1, keepdims=True)
    rows = logits.shape[0]
    size = out_ref.shape[0] // count
    student = jnp.concatenate([as_row(top), as_row(total)], axis=0)
    for r in range(count):
        there = place_ref[0] ^ r
        block = jnp.concatenate(
            [
                teacher_ref[:, r * rows : (r + 1) * rows],
                student,
                weight_ref[pl.ds(there, 1), :].astype(jnp.float32),
                jnp.zeros((3, rows), jnp.float32),
            ],
            axis=0,
        )
        out_ref[pl.ds(there * size, size)] = jnp.broadcast_to(block[None], (size, 8, rows))


def student_stats(parts, teacher_stats, weights, place, size):
    rows, cols = parts[0].shape
    count = len(parts)
    return pl.pallas_call(
        functools.partial(stats_kernel, count),
        out_shape=(
            jax.ShapeDtypeStruct((rows, cols), jnp.float32),
            jax.ShapeDtypeStruct((count * size, 8, rows), jnp.float32),
        ),
        in_specs=[SMEM] + [VMEM] * (count + 2),
        out_specs=(VMEM, VMEM),
        compiler_params=params(12),
        cost_estimate=cost(8 * rows * cols, 12 * rows * cols, rows * cols),
        name="stats",
    )(place, *parts, teacher_stats, weights)


def grads_kernel(count, size, place_ref, stats_ref, logits_ref, ids_ref, *refs):
    terms = refs[:count]
    grads_ref = refs[count]
    b, t = place_ref[0], place_ref[1]
    rows, cols = logits_ref.shape
    logits = logits_ref[...]
    shard = lax.broadcasted_iota(jnp.int32, (rows, cols), 1)
    targets = jnp.where(shard == column(ids_ref[...]) - t * cols, mix_label, 0.0)
    probs = None
    for r in range(count):
        start = (b ^ r) * size
        block = stats_ref[pl.ds(start, size)]
        here = stats_ref[start + t]
        peak = jnp.max(block[:, 0, :], axis=0, keepdims=True)
        total = jnp.sum(block[:, 1, :] * jnp.exp(block[:, 0, :] - peak), axis=0, keepdims=True)
        scale = ((1.0 - mix_label) / DEN) * here[4:5] * jnp.exp(here[0:1] - peak) / total
        targets = targets + terms[r][...].astype(jnp.float32) * column(scale)
        if r == 0:
            peak = jnp.max(block[:, 2, :], axis=0, keepdims=True)
            total = jnp.sum(block[:, 3, :] * jnp.exp(block[:, 2, :] - peak), axis=0, keepdims=True)
            probs = jnp.exp(logits - column(peak)) / column(total)
    grads = (loss_scale * (probs - targets)).astype(grads_ref.dtype)
    grads_ref[:rows] = grads
    grads_ref[rows:] = jnp.zeros((EXTRA, cols), grads.dtype)
    dots = as_row(jnp.sum(grads.astype(jnp.float32) * logits, axis=1, keepdims=True))
    grads_ref[rows:, :rows] = extra_rows([dots], grads.dtype)


def make_grads(stats, logits, ids, terms, place, size):
    rows, cols = logits.shape
    count = len(terms)
    return pl.pallas_call(
        functools.partial(grads_kernel, count, size),
        out_shape=jax.ShapeDtypeStruct((rows + EXTRA, cols), jnp.bfloat16),
        in_specs=[SMEM] + [VMEM] * (count + 3),
        out_specs=VMEM,
        compiler_params=params(12),
        cost_estimate=cost(16 * rows * cols, 10 * rows * cols, rows * cols),
        name="grads",
    )(place, stats, logits, ids, *terms)


def pieces_kernel(parity, width, place_ref, grads_ref, w_ref, out_ref, turned_ref):
    rows = out_ref.shape[1]
    turned_ref[...] = jnp.transpose(grads_ref[:rows])
    count = (out_ref.shape[0] - EXTRA) // width
    for k in range(count):
        start = pl.multiple_of((place_ref[2] ^ (2 * k + parity)) * width, width)
        acc = jnp.dot(w_ref[pl.ds(start, width)], turned_ref[...], preferred_element_type=jnp.float32)
        out_ref[k * width : (k + 1) * width] = acc.astype(out_ref.dtype)
    out_ref[count * width :] = grads_ref[rows:, :rows]


def normed_grad_pieces(grads, head, place, blocks, parity):
    rows, cols = grads.shape[0] - EXTRA, grads.shape[1]
    width = head.shape[0] // blocks
    return pl.pallas_call(
        functools.partial(pieces_kernel, parity, width),
        out_shape=jax.ShapeDtypeStruct((blocks // 2 * width + EXTRA, rows), jnp.bfloat16),
        in_specs=[SMEM, VMEM, VMEM],
        out_specs=VMEM,
        scratch_shapes=[pltpu.VMEM((cols, rows), jnp.bfloat16)],
        compiler_params=params(16),
        cost_estimate=cost(rows * head.size, head.size),
        name="pieces",
    )(place, grads, head)


def fold_kernel(width, mine_ref, got_ref, keep_ref, send_ref):
    f32 = jnp.float32
    count = (mine_ref.shape[0] - EXTRA) // width
    for k in range(count):
        at = slice(k * width, (k + 1) * width)
        total = mine_ref[at].astype(f32) + got_ref[at].astype(f32)
        to = slice(k // 2 * width, (k // 2 + 1) * width)
        (send_ref if k % 2 else keep_ref)[to] = total.astype(keep_ref.dtype)
    dots = extra_values(mine_ref[count * width :], 1)[0] + extra_values(got_ref[count * width :], 1)[0]
    extra = extra_rows([dots], keep_ref.dtype)
    keep_ref[count // 2 * width :] = extra
    send_ref[count // 2 * width :] = extra


def fold(mine, got, width):
    full, rows = mine.shape
    half = (full - EXTRA) // 2 + EXTRA
    return pl.pallas_call(
        functools.partial(fold_kernel, width),
        out_shape=(jax.ShapeDtypeStruct((half, rows), mine.dtype),) * 2,
        in_specs=[VMEM, VMEM],
        out_specs=(VMEM, VMEM),
        compiler_params=params(8),
        cost_estimate=cost(mine.size, 6 * mine.size),
        name="fold",
    )(mine, got)


def split_kernel(count, width, place_ref, *refs):
    mine, got, turned = (refs[i * count : (i + 1) * count] for i in range(3))
    out = refs[3 * count :]
    f32 = jnp.float32
    lows = (mine[0].shape[0] - EXTRA) // width
    rows = mine[0].shape[1]
    dots = [
        extra_values(mine[r][lows * width :], 1)[0] + extra_values(got[r][lows * width :], 1)[0] for r in range(count)
    ]
    for low in range(lows):
        at = slice(low * width, (low + 1) * width)
        block = pl.multiple_of((place_ref[2] ^ (4 * low)) * width, width)
        totals = [mine[r][at].astype(f32) + got[r][at].astype(f32) for r in range(count)]
        gain = sum(
            jnp.sum(totals[r] * turned[r][pl.ds(block, width)].astype(f32), axis=1, keepdims=True)
            for r in range(count)
        )
        gain = as_row(gain)
        lanes = min(width, rows)
        gains = [gain[:, i : i + lanes] for i in range(0, width, lanes)]
        if lanes < rows:
            gains = [jnp.concatenate([row, jnp.zeros((1, rows - lanes), f32)], axis=1) for row in gains]
        for r in range(count):
            total = totals[r].astype(mine[r].dtype)
            extra = extra_rows([dots[r]] + gains, mine[r].dtype)
            for kh in range(count):

                @pl.when((place_ref[3] ^ kh) == r)
                def _():
                    out[kh * lows + low][:width] = total
                    out[kh * lows + low][width:] = extra


def split(mine, got, turned, width, place):
    count = len(mine)
    rows = mine[0].shape[1]
    lows = (mine[0].shape[0] - EXTRA) // width
    return pl.pallas_call(
        functools.partial(split_kernel, count, width),
        out_shape=(jax.ShapeDtypeStruct((width + EXTRA, rows), mine[0].dtype),) * (count * lows),
        in_specs=[SMEM] + [VMEM] * (3 * count),
        out_specs=(VMEM,) * (count * lows),
        compiler_params=params(8),
        cost_estimate=cost(4 * count * mine[0].size, 8 * count * mine[0].size),
        name="split",
    )(place, *mine, *got, *turned)


def head_grad_kernel(count, *refs):
    grads, turned = refs[:count], refs[count : 2 * count]
    out_ref, grads_ref = refs[-2:]
    rows = grads_ref.shape[0] // count

    @pl.when(pl.program_id(0) == 0)
    def _():
        for r in range(count):
            grads_ref[r * rows : (r + 1) * rows, :] = grads[r][:rows]

    lhs = jnp.concatenate([ref[...] for ref in turned], axis=1)
    out_ref[...] = jnp.dot(lhs, grads_ref[...], preferred_element_type=jnp.float32)


def head_grad(grads, turned, half, done):
    count = len(grads)
    full, cols = grads[0].shape
    part, rows = turned[0].shape
    tile = tile_of(part)
    steps = part // tile // 2
    return pl.pallas_call(
        functools.partial(head_grad_kernel, count),
        out_shape=jax.ShapeDtypeStruct((part, cols), jnp.float32),
        grid=(steps,),
        in_specs=[pl.BlockSpec((full, cols), lambda i: (0, 0))] * count
        + [pl.BlockSpec((tile, rows), lambda i: (i + half * steps, 0))] * count
        + [pl.BlockSpec(memory_space=pl.ANY)] * len(done),
        out_specs=pl.BlockSpec((tile, cols), lambda i: (i + half * steps, 0)),
        scratch_shapes=[pltpu.VMEM((count * rows, cols), jnp.bfloat16)],
        input_output_aliases={2 * count: 0} if done else {},
        compiler_params=params(16),
        cost_estimate=cost(count * rows * part * cols, 2 * part * cols),
        name="headgrad",
    )(*grads, *turned, *done)


def last_kernel(count, width, inv_ref, hidden_ref, gain_ref, *refs):
    parts = refs[:count]
    out_ref, gain_out_ref = refs[count:]
    total = parts[0][...].astype(jnp.float32)
    for ref in parts[1:]:
        total = total + ref[...].astype(jnp.float32)
    piece, rows = total.shape[0] - EXTRA, total.shape[1]
    lanes = min(piece, rows)
    dots, *gains = extra_values(total[piece:], 1 + piece // lanes)
    gain_out_ref[...] = jnp.concatenate([row[:, :lanes] for row in gains], axis=1) / gain_ref[...]
    normed_grads = jnp.transpose(total[:piece])
    inv = inv_ref[...]
    scaled = hidden_ref[...].astype(jnp.float32) * inv
    out_ref[...] = inv * gain_ref[...] * normed_grads - scaled * (inv * column(dots) / width)


def finish(parts, inv, hidden, gain, width):
    piece, rows = parts[0].shape[0] - EXTRA, parts[0].shape[1]
    return pl.pallas_call(
        functools.partial(last_kernel, len(parts), width),
        out_shape=(
            jax.ShapeDtypeStruct((rows, piece), jnp.float32),
            jax.ShapeDtypeStruct((1, piece), jnp.float32),
        ),
        in_specs=[VMEM] * (3 + len(parts)),
        out_specs=(VMEM, VMEM),
        compiler_params=params(12),
        cost_estimate=cost(16 * rows * piece, 12 * rows * piece),
        name="last",
    )(inv, hidden, gain, *parts)


def load_kernel(from_ref, to_ref, sem):
    copy = pltpu.make_async_copy(from_ref, to_ref, sem)
    copy.start()
    copy.wait()


def load(value):
    return pl.pallas_call(
        load_kernel,
        out_shape=jax.ShapeDtypeStruct(value.shape, value.dtype),
        in_specs=[pl.BlockSpec(memory_space=pltpu.HBM)],
        out_specs=VMEM,
        scratch_shapes=[pltpu.SemaphoreType.DMA],
        compiler_params=params(16),
        cost_estimate=cost(0, 4 * value.size),
        name="load",
    )(value)


def per_device(
    teacher_hidden,
    teacher_gain,
    teacher_head,
    student_hidden,
    student_gain,
    student_head,
    cluster_weights,
    token_ids,
):
    branches = lax.axis_size("branch")
    size = lax.axis_size("tok")
    b = lax.axis_index("branch")
    t = lax.axis_index("tok")
    rows, width = student_hidden.shape
    blocks = size // branches
    place = jnp.stack([b, t, t % blocks, (t // blocks) ^ b]).astype(jnp.int32)
    teacher_block, own, own_turned, inv_scale, *sent = normalize_all(
        teacher_hidden, teacher_gain, student_hidden, student_gain, place, branches
    )

    loaded = load(student_head)
    turned, partials = [own_turned], []
    for r in range(1, branches):
        mine = swap(sent[r - 1], "branch", r)
        other = swap(mine, "tok", 1)
        partial, fetched = other_dot(mine, other, loaded, place)
        turned.append(fetched)
        partials.append(swap(partial, "branch", r))
    partials = [own_dot(own, loaded)] + partials

    got, keys = gather_blocks(teacher_block, size)
    teacher_stats, *exps = teacher_softmax(got, keys, teacher_head, place, blocks, branches)
    terms = [exps[0]] + [swap(exps[r], "branch", r) for r in range(1, branches)]

    weights = cluster_weights[:, 0].reshape(branches, rows)
    logits, stats = student_stats(partials, teacher_stats, weights, place, size)
    stats = lax.all_to_all(stats, ("branch", "tok"), 0, 0, tiled=True)
    logit_grads = make_grads(stats, logits, token_ids[None], terms, place, size)
    all_grads = [logit_grads] + [swap(logit_grads, "branch", r) for r in range(1, branches)]

    slice_width = width // size
    kept, got = [], []
    for r in range(branches):
        send = normed_grad_pieces(all_grads[r], loaded, place, blocks, 1)
        send = swap(send, "tok", 1)
        keep = normed_grad_pieces(all_grads[r], loaded, place, blocks, 0)
        keep, send = fold(keep, send, slice_width)
        kept.append(keep)
        got.append(swap(send, "tok", 2))
    owned = split(kept, got, turned, slice_width, place)
    arrived = []
    for kh in range(branches):
        for kl in range(blocks // 4):
            perm = []
            for i in range(branches * size):
                bb, h, l, rest = i // size, (i % size) // blocks, (i % blocks) // 4, i % 4
                perm.append((i, (h ^ kh) * size + bb * blocks + (l ^ kl) * 4 + rest))
            arrived.append(lax.ppermute(owned[kh * (blocks // 4) + kl], ("branch", "tok"), perm))

    grad_head = head_grad(all_grads, turned, 0, [])
    grad_head = head_grad(all_grads, turned, 1, [grad_head])

    hidden_cols = lax.dynamic_slice_in_dim(student_hidden, t * slice_width, slice_width, 1)
    gain_cols = lax.dynamic_slice_in_dim(student_gain, t * slice_width, slice_width, 0)
    grad_hidden, grad_gain = finish(arrived, inv_scale, hidden_cols, gain_cols[None], width)
    return (grad_head, grad_hidden, grad_gain[0])


def solution(mesh):
    in_specs = (
        P("branch", "tok", None),
        P("branch", None),
        P("branch", None, "tok"),
        P("branch", None),
        P(),
        P("branch", "tok"),
        P(None, "branch"),
        P("branch"),
    )
    out_specs = (P("branch", "tok"), P("branch", "tok"), P("tok"))
    return jax.shard_map(per_device, mesh=mesh, in_specs=in_specs, out_specs=out_specs, check_vma=False)
```

```python
import functools

import jax
import jax.numpy as jnp
from jax import lax
from jax.experimental import pallas as pl
from jax.experimental.pallas import tpu as pltpu
from jax.sharding import PartitionSpec as P


DEN = 64

eps = 1e-05
mix_label = 0.25
loss_scale = 64.0


def swap(value, axis, flip):
    size = lax.axis_size(axis)
    return lax.ppermute(value, axis, [(i, i ^ flip) for i in range(size)])


VMEM = pl.BlockSpec(memory_space=pltpu.VMEM)
SMEM = pl.BlockSpec(memory_space=pltpu.SMEM)
MIB = 1 << 20


def params(mib):
    return pltpu.CompilerParams(vmem_limit_bytes=mib * MIB)


def cost(flops, nbytes, exps=0):
    return pl.CostEstimate(flops=flops, bytes_accessed=nbytes, transcendentals=exps)


def first_kernel(branches, place_ref, *refs):
    sources, (block_ref, own_ref, inv_ref) = refs[:4], refs[4:7]
    sent, (normed_ref, th_ref, tg_ref, sh_ref, sg_ref, sems) = refs[7 : 6 + branches], refs[6 + branches :]
    copies = [
        pltpu.make_async_copy(source, target, sems.at[i])
        for i, (source, target) in enumerate(zip(sources, (th_ref, tg_ref, sh_ref, sg_ref)))
    ]
    for copy in copies:
        copy.start()
    for copy in copies[:2]:
        copy.wait()
    values = th_ref[0].astype(jnp.float32)
    scale = lax.rsqrt(jnp.mean(values * values, axis=-1, keepdims=True) + eps)
    block_ref[...] = (values * scale * tg_ref[...]).astype(jnp.bfloat16)
    for copy in copies[2:]:
        copy.wait()
    values = sh_ref[...].astype(jnp.float32)
    scale = lax.rsqrt(jnp.mean(values * values, axis=-1, keepdims=True) + eps)
    inv_ref[...] = scale
    normed_ref[...] = (values * scale * sg_ref[...]).astype(jnp.bfloat16)
    part = own_ref.shape[1]
    half = own_ref.shape[0] // 2
    b = place_ref[0]
    own_ref[...] = normed_ref[:, pl.ds(pl.multiple_of(b * part, part), part)]
    start = pl.multiple_of((place_ref[1] % 2) * half, half)
    for r in range(1, branches):
        cols = pl.ds(pl.multiple_of((b ^ r) * part, part), part)
        sent[r - 1][...] = normed_ref[pl.ds(start, half), cols]


def normalize_all(teacher_hidden, teacher_gain, student_hidden, student_gain, place, branches):
    rows, width = student_hidden.shape
    part = width // branches
    bf16 = jnp.bfloat16
    return pl.pallas_call(
        functools.partial(first_kernel, branches),
        out_shape=(
            jax.ShapeDtypeStruct(teacher_hidden.shape[1:], bf16),
            jax.ShapeDtypeStruct((rows, part), bf16),
            jax.ShapeDtypeStruct((rows, 1), jnp.float32),
            *[jax.ShapeDtypeStruct((rows // 2, part), bf16)] * (branches - 1),
        ),
        in_specs=[SMEM] + [pl.BlockSpec(memory_space=pl.ANY)] * 4,
        out_specs=(VMEM,) * (2 + branches),
        scratch_shapes=[pltpu.VMEM((rows, width), bf16)]
        + [pltpu.VMEM(value.shape, value.dtype) for value in (teacher_hidden, teacher_gain, student_hidden)]
        + [pltpu.VMEM((1, width), jnp.float32), pltpu.SemaphoreType.DMA((4,))],
        compiler_params=params(60),
        cost_estimate=cost(8 * rows * width, 4 * rows * width),
        name="first",
    )(place, teacher_hidden, teacher_gain, student_hidden, student_gain[None])


def gather_blocks(block, size):
    got = {0: block}
    for k in range(8, size, 8):
        got[k] = swap(block, "tok", k)
    for k in range(0, size, 8):
        got[k + 4] = swap(got[k], "tok", 4)
    for k in range(0, size, 4):
        got[k + 2] = swap(got[k], "tok", 2)
    evens = sorted(got)
    half = len(evens) // 2
    arrays = [got[k] for k in evens]
    keys = [(k,) for k in evens]
    for group in (evens[:half], evens[half:]):
        arrays.append(swap(jnp.concatenate([got[k] for k in group], axis=0), "tok", 1))
        keys.append(tuple(k + 1 for k in group))
    return arrays, tuple(keys)


def own_dot_kernel(rows_ref, w_ref, out_ref, turned_ref):
    turned_ref[...] = jnp.transpose(rows_ref[...])
    out_ref[...] = jnp.dot(rows_ref[...], w_ref[...], preferred_element_type=jnp.float32)


def own_dot(rows, head):
    return pl.pallas_call(
        own_dot_kernel,
        out_shape=(
            jax.ShapeDtypeStruct((rows.shape[0], head.shape[1]), jnp.float32),
            jax.ShapeDtypeStruct(rows.shape[::-1], rows.dtype),
        ),
        in_specs=[VMEM, VMEM],
        out_specs=(VMEM, VMEM),
        compiler_params=params(16),
        cost_estimate=cost(2 * rows.size * head.shape[1], 2 * head.size),
        name="owndot",
    )(rows, head)


def other_dot_kernel(place_ref, mine_ref, other_ref, w_ref, out_ref, turned_ref, rows_ref):
    half = mine_ref.shape[0]
    core = place_ref[1] % 2
    rows_ref[pl.ds(pl.multiple_of(core * half, half), half), :] = mine_ref[...]
    rows_ref[pl.ds(pl.multiple_of((1 - core) * half, half), half), :] = other_ref[...]
    out_ref[...] = jnp.dot(rows_ref[...], w_ref[...], preferred_element_type=jnp.float32)
    turned_ref[...] = jnp.transpose(rows_ref[...])


def other_dot(mine, other, head, place):
    rows = 2 * mine.shape[0]
    return pl.pallas_call(
        other_dot_kernel,
        out_shape=(
            jax.ShapeDtypeStruct((rows, head.shape[1]), jnp.float32),
            jax.ShapeDtypeStruct((mine.shape[1], rows), jnp.bfloat16),
        ),
        in_specs=[SMEM, VMEM, VMEM, VMEM],
        out_specs=(VMEM, VMEM),
        scratch_shapes=[pltpu.VMEM((rows, mine.shape[1]), jnp.bfloat16)],
        compiler_params=params(16),
        cost_estimate=cost(2 * rows * head.size, 2 * head.size),
        name="otherdot",
    )(place, mine, other, head)


EXTRA = 8


def extra_rows(values, dtype):
    first = [value.astype(dtype).astype(jnp.float32) for value in values]
    rest = [value - lead for value, lead in zip(values, first)]
    empty = jnp.zeros((EXTRA - 2 * len(values), values[0].shape[1]), jnp.float32)
    return jnp.concatenate(first + rest + [empty], axis=0).astype(dtype)


def extra_values(rows, count):
    rows = rows.astype(jnp.float32)
    return [rows[i : i + 1] + rows[count + i : count + i + 1] for i in range(count)]


def tile_of(cols):
    return next((tile for tile in (256, 128) if cols % tile == 0), cols)


def column(row):
    count = row.shape[1]
    return jnp.transpose(jnp.broadcast_to(row, (128, count)))[:, :1]


def as_row(col):
    return jnp.transpose(jnp.broadcast_to(col, (col.shape[0], 128)))[:1]


def teacher_kernel(keys, half, place_ref, *refs):
    blocks = refs[: len(keys)]
    w_ref, stat_ref, *exps = refs[len(keys) : -2]
    rows_ref, logits_ref = refs[-2:]
    mine = place_ref[1] ^ (place_ref[0] * half)
    for ref, owned in zip(blocks, keys):
        count = ref.shape[0] // len(owned)
        for j, k in enumerate(owned):
            start = pl.multiple_of((mine ^ k) * count, count)
            rows_ref[pl.ds(start, count), :] = ref[j * count : (j + 1) * count, :]

    cols = w_ref.shape[2]
    tile = tile_of(cols)
    if tile == cols:
        logits_ref[...] = jnp.dot(rows_ref[...], w_ref[0], preferred_element_type=jnp.float32)
    else:

        @pl.loop(0, cols // tile)
        def _(step):
            at = pl.ds(pl.multiple_of(step * tile, tile), tile)
            logits_ref[:, at] = jnp.dot(rows_ref[...], w_ref[0, :, at], preferred_element_type=jnp.float32)

    logits = logits_ref[...]
    top = jnp.max(logits, axis=1, keepdims=True)
    scaled = jnp.exp(logits - top)
    rows = exps[0].shape[0]
    for r, ref in enumerate(exps):
        ref[...] = scaled[r * rows : (r + 1) * rows].astype(ref.dtype)
    stat_ref[0:1, :] = as_row(top)
    stat_ref[1:2, :] = as_row(jnp.sum(scaled, axis=1, keepdims=True))


def teacher_softmax(got, keys, head, place, half, branches):
    width, cols = head.shape[1:]
    tokens = sum(part.shape[0] for part in got)
    return pl.pallas_call(
        functools.partial(teacher_kernel, keys, half),
        out_shape=(
            jax.ShapeDtypeStruct((2, tokens), jnp.float32),
            *[jax.ShapeDtypeStruct((tokens // branches, cols), jnp.bfloat16)] * branches,
        ),
        in_specs=[SMEM] + [VMEM] * (len(got) + 1),
        out_specs=(VMEM,) * (1 + branches),
        scratch_shapes=[pltpu.VMEM((tokens, width), jnp.bfloat16), pltpu.VMEM((tokens, cols), jnp.float32)],
        compiler_params=params(28),
        cost_estimate=cost(2 * tokens * width * cols, 2 * width * cols, tokens * cols),
        name="teacher",
    )(place, *got, head)


def stats_kernel(count, place_ref, *refs):
    parts = refs[:count]
    teacher_ref, weight_ref, logits_ref, out_ref = refs[count:]
    logits = parts[0][...]
    for ref in parts[1:]:
        logits = logits + ref[...]
    logits_ref[...] = logits
    top = jnp.max(logits, axis=1, keepdims=True)
    total = jnp.sum(jnp.exp(logits - top), axis=1, keepdims=True)
    rows = logits.shape[0]
    size = out_ref.shape[0] // count
    student = jnp.concatenate([as_row(top), as_row(total)], axis=0)
    for r in range(count):
        there = place_ref[0] ^ r
        block = jnp.concatenate(
            [
                teacher_ref[:, r * rows : (r + 1) * rows],
                student,
                weight_ref[pl.ds(there, 1), :].astype(jnp.float32),
                jnp.zeros((3, rows), jnp.float32),
            ],
            axis=0,
        )
        out_ref[pl.ds(there * size, size)] = jnp.broadcast_to(block[None], (size, 8, rows))


def student_stats(parts, teacher_stats, weights, place, size):
    rows, cols = parts[0].shape
    count = len(parts)
    return pl.pallas_call(
        functools.partial(stats_kernel, count),
        out_shape=(
            jax.ShapeDtypeStruct((rows, cols), jnp.float32),
            jax.ShapeDtypeStruct((count * size, 8, rows), jnp.float32),
        ),
        in_specs=[SMEM] + [VMEM] * (count + 2),
        out_specs=(VMEM, VMEM),
        compiler_params=params(12),
        cost_estimate=cost(8 * rows * cols, 12 * rows * cols, rows * cols),
        name="stats",
    )(place, *parts, teacher_stats, weights)


def grads_kernel(count, size, place_ref, stats_ref, logits_ref, ids_ref, *refs):
    terms = refs[:count]
    grads_ref = refs[count]
    b, t = place_ref[0], place_ref[1]
    rows, cols = logits_ref.shape
    logits = logits_ref[...]
    shard = lax.broadcasted_iota(jnp.int32, (rows, cols), 1)
    targets = jnp.where(shard == column(ids_ref[...]) - t * cols, mix_label, 0.0)
    probs = None
    for r in range(count):
        start = (b ^ r) * size
        block = stats_ref[pl.ds(start, size)]
        here = stats_ref[start + t]
        peak = jnp.max(block[:, 0, :], axis=0, keepdims=True)
        total = jnp.sum(block[:, 1, :] * jnp.exp(block[:, 0, :] - peak), axis=0, keepdims=True)
        scale = ((1.0 - mix_label) / DEN) * here[4:5] * jnp.exp(here[0:1] - peak) / total
        targets = targets + terms[r][...].astype(jnp.float32) * column(scale)
        if r == 0:
            peak = jnp.max(block[:, 2, :], axis=0, keepdims=True)
            total = jnp.sum(block[:, 3, :] * jnp.exp(block[:, 2, :] - peak), axis=0, keepdims=True)
            probs = jnp.exp(logits - column(peak)) / column(total)
    grads = (loss_scale * (probs - targets)).astype(grads_ref.dtype)
    grads_ref[:rows] = grads
    grads_ref[rows:] = jnp.zeros((EXTRA, cols), grads.dtype)
    dots = as_row(jnp.sum(grads.astype(jnp.float32) * logits, axis=1, keepdims=True))
    grads_ref[rows:, :rows] = extra_rows([dots], grads.dtype)


def make_grads(stats, logits, ids, terms, place, size):
    rows, cols = logits.shape
    count = len(terms)
    return pl.pallas_call(
        functools.partial(grads_kernel, count, size),
        out_shape=jax.ShapeDtypeStruct((rows + EXTRA, cols), jnp.bfloat16),
        in_specs=[SMEM] + [VMEM] * (count + 3),
        out_specs=VMEM,
        compiler_params=params(12),
        cost_estimate=cost(16 * rows * cols, 10 * rows * cols, rows * cols),
        name="grads",
    )(place, stats, logits, ids, *terms)


def pieces_kernel(parity, width, place_ref, grads_ref, w_ref, out_ref, turned_ref):
    rows = out_ref.shape[1]
    turned_ref[...] = jnp.transpose(grads_ref[:rows])
    count = (out_ref.shape[0] - EXTRA) // width
    for k in range(count):
        start = pl.multiple_of((place_ref[2] ^ (2 * k + parity)) * width, width)
        acc = jnp.dot(w_ref[pl.ds(start, width)], turned_ref[...], preferred_element_type=jnp.float32)
        out_ref[k * width : (k + 1) * width] = acc.astype(out_ref.dtype)
    out_ref[count * width :] = grads_ref[rows:, :rows]


def normed_grad_pieces(grads, head, place, blocks, parity):
    rows, cols = grads.shape[0] - EXTRA, grads.shape[1]
    width = head.shape[0] // blocks
    return pl.pallas_call(
        functools.partial(pieces_kernel, parity, width),
        out_shape=jax.ShapeDtypeStruct((blocks // 2 * width + EXTRA, rows), jnp.bfloat16),
        in_specs=[SMEM, VMEM, VMEM],
        out_specs=VMEM,
        scratch_shapes=[pltpu.VMEM((cols, rows), jnp.bfloat16)],
        compiler_params=params(16),
        cost_estimate=cost(rows * head.size, head.size),
        name="pieces",
    )(place, grads, head)


def fold_kernel(mine_ref, got_ref, *out):
    f32 = jnp.float32
    width = out[0].shape[0] - EXTRA
    full = len(out) * width
    dots = extra_values(mine_ref[full:], 1)[0] + extra_values(got_ref[full:], 1)[0]
    for k, ref in enumerate(out):
        at = slice(k * width, (k + 1) * width)
        ref[:width] = (mine_ref[at].astype(f32) + got_ref[at].astype(f32)).astype(ref.dtype)
        ref[width:] = extra_rows([dots], ref.dtype)


def fold(mine, got, width):
    full, rows = mine.shape
    count = (full - EXTRA) // width
    return pl.pallas_call(
        fold_kernel,
        out_shape=(jax.ShapeDtypeStruct((width + EXTRA, rows), mine.dtype),) * count,
        in_specs=[VMEM, VMEM],
        out_specs=(VMEM,) * count,
        compiler_params=params(8),
        cost_estimate=cost(mine.size, 6 * mine.size),
        name="fold",
    )(mine, got)


def split_kernel(count, place_ref, *refs):
    turned, out = refs[-2 * count : -count], refs[-count:]
    each = len(refs) // count - 2
    f32 = jnp.float32
    width, rows = out[0].shape[0] - EXTRA, out[0].shape[1]
    block = pl.multiple_of(place_ref[2] * width, width)
    totals, dots, gain = [], [], 0.0
    for r in range(count):
        total = refs[r * each][...].astype(f32)
        for ref in refs[r * each + 1 : (r + 1) * each]:
            total = total + ref[...].astype(f32)
        dots.append(extra_values(total[width:], 1)[0])
        totals.append(total[:width])
        gain = gain + jnp.sum(totals[r] * turned[r][pl.ds(block, width)].astype(f32), axis=1, keepdims=True)
    gain = as_row(gain)
    lanes = min(width, rows)
    gains = [gain[:, i : i + lanes] for i in range(0, width, lanes)]
    if lanes < rows:
        gains = [jnp.concatenate([row, jnp.zeros((1, rows - lanes), f32)], axis=1) for row in gains]
    for r in range(count):
        total = totals[r].astype(out[0].dtype)
        extra = extra_rows([dots[r]] + gains, out[0].dtype)
        for kh in range(count):

            @pl.when((place_ref[3] ^ kh) == r)
            def _():
                out[kh][:width] = total
                out[kh][width:] = extra


def split(parts, turned, place):
    count = len(parts)
    shape = parts[0][0].shape
    each = len(parts[0])
    return pl.pallas_call(
        functools.partial(split_kernel, count),
        out_shape=(jax.ShapeDtypeStruct(shape, parts[0][0].dtype),) * count,
        in_specs=[SMEM] + [VMEM] * (count * (each + 1)),
        out_specs=(VMEM,) * count,
        compiler_params=params(8),
        cost_estimate=cost(8 * count * shape[0] * shape[1], 12 * count * shape[0] * shape[1]),
        name="split",
    )(place, *[part for some in parts for part in some], *turned)


def head_grad_kernel(count, *refs):
    grads, turned = refs[:count], refs[count : 2 * count]
    out_ref, grads_ref = refs[-2:]
    rows = grads_ref.shape[0] // count

    @pl.when(pl.program_id(0) == 0)
    def _():
        for r in range(count):
            grads_ref[r * rows : (r + 1) * rows, :] = grads[r][:rows]

    lhs = jnp.concatenate([ref[...] for ref in turned], axis=1)
    out_ref[...] = jnp.dot(lhs, grads_ref[...], preferred_element_type=jnp.float32)


def head_grad(grads, turned, half, done):
    count = len(grads)
    full, cols = grads[0].shape
    part, rows = turned[0].shape
    tile = tile_of(part)
    steps = part // tile // 2
    return pl.pallas_call(
        functools.partial(head_grad_kernel, count),
        out_shape=jax.ShapeDtypeStruct((part, cols), jnp.float32),
        grid=(steps,),
        in_specs=[pl.BlockSpec((full, cols), lambda i: (0, 0))] * count
        + [pl.BlockSpec((tile, rows), lambda i: (i + half * steps, 0))] * count
        + [pl.BlockSpec(memory_space=pl.ANY)] * len(done),
        out_specs=pl.BlockSpec((tile, cols), lambda i: (i + half * steps, 0)),
        scratch_shapes=[pltpu.VMEM((count * rows, cols), jnp.bfloat16)],
        input_output_aliases={2 * count: 0} if done else {},
        compiler_params=params(16),
        cost_estimate=cost(count * rows * part * cols, 2 * part * cols),
        name="headgrad",
    )(*grads, *turned, *done)


def last_kernel(count, width, inv_ref, hidden_ref, gain_ref, *refs):
    parts = refs[:count]
    out_ref, gain_out_ref = refs[count:]
    total = parts[0][...].astype(jnp.float32)
    for ref in parts[1:]:
        total = total + ref[...].astype(jnp.float32)
    piece, rows = total.shape[0] - EXTRA, total.shape[1]
    lanes = min(piece, rows)
    dots, *gains = extra_values(total[piece:], 1 + piece // lanes)
    gain_out_ref[...] = jnp.concatenate([row[:, :lanes] for row in gains], axis=1) / gain_ref[...]
    normed_grads = jnp.transpose(total[:piece])
    inv = inv_ref[...]
    scaled = hidden_ref[...].astype(jnp.float32) * inv
    out_ref[...] = inv * gain_ref[...] * normed_grads - scaled * (inv * column(dots) / width)


def finish(parts, inv, hidden, gain, width):
    piece, rows = parts[0].shape[0] - EXTRA, parts[0].shape[1]
    return pl.pallas_call(
        functools.partial(last_kernel, len(parts), width),
        out_shape=(
            jax.ShapeDtypeStruct((rows, piece), jnp.float32),
            jax.ShapeDtypeStruct((1, piece), jnp.float32),
        ),
        in_specs=[VMEM] * (3 + len(parts)),
        out_specs=(VMEM, VMEM),
        compiler_params=params(12),
        cost_estimate=cost(16 * rows * piece, 12 * rows * piece),
        name="last",
    )(inv, hidden, gain, *parts)


def load_kernel(from_ref, to_ref, sem):
    copy = pltpu.make_async_copy(from_ref, to_ref, sem)
    copy.start()
    copy.wait()


def load(value):
    return pl.pallas_call(
        load_kernel,
        out_shape=jax.ShapeDtypeStruct(value.shape, value.dtype),
        in_specs=[pl.BlockSpec(memory_space=pltpu.HBM)],
        out_specs=VMEM,
        scratch_shapes=[pltpu.SemaphoreType.DMA],
        compiler_params=params(16),
        cost_estimate=cost(0, 4 * value.size),
        name="load",
    )(value)


def per_device(
    teacher_hidden,
    teacher_gain,
    teacher_head,
    student_hidden,
    student_gain,
    student_head,
    cluster_weights,
    token_ids,
):
    branches = lax.axis_size("branch")
    size = lax.axis_size("tok")
    b = lax.axis_index("branch")
    t = lax.axis_index("tok")
    rows, width = student_hidden.shape
    blocks = size // branches
    place = jnp.stack([b, t, t % blocks, (t // blocks) ^ b]).astype(jnp.int32)
    teacher_block, own, inv_scale, *sent = normalize_all(
        teacher_hidden, teacher_gain, student_hidden, student_gain, place, branches
    )

    loaded = load(student_head)
    own_partial, own_turned = own_dot(own, loaded)
    turned, partials = [own_turned], [own_partial]
    for r in range(1, branches):
        mine = swap(sent[r - 1], "branch", r)
        other = swap(mine, "tok", 1)
        partial, fetched = other_dot(mine, other, loaded, place)
        turned.append(fetched)
        partials.append(swap(partial, "branch", r))

    got, keys = gather_blocks(teacher_block, size)
    teacher_stats, *exps = teacher_softmax(got, keys, teacher_head, place, blocks, branches)
    terms = [exps[0]] + [swap(exps[r], "branch", r) for r in range(1, branches)]

    weights = cluster_weights[:, 0].reshape(branches, rows)
    logits, stats = student_stats(partials, teacher_stats, weights, place, size)
    stats = lax.all_to_all(stats, ("branch", "tok"), 0, 0, tiled=True)
    logit_grads = make_grads(stats, logits, token_ids[None], terms, place, size)
    all_grads = [logit_grads] + [swap(logit_grads, "branch", r) for r in range(1, branches)]

    slice_width = width // size
    parts = []
    for r in range(branches):
        send = normed_grad_pieces(all_grads[r], loaded, place, blocks, 1)
        send = swap(send, "tok", 1)
        keep = normed_grad_pieces(all_grads[r], loaded, place, blocks, 0)
        folded = fold(keep, send, slice_width)
        parts.append([folded[0]] + [swap(folded[k], "tok", 2 * k) for k in range(1, blocks // 2)])
    owned = split(parts, turned, place)
    arrived = []
    for kh in range(branches):
        perm = []
        for i in range(branches * size):
            bb, h, rest = i // size, (i % size) // blocks, i % blocks
            perm.append((i, (h ^ kh) * size + bb * blocks + rest))
        arrived.append(lax.ppermute(owned[kh], ("branch", "tok"), perm))

    grad_head = head_grad(all_grads, turned, 0, [])
    grad_head = head_grad(all_grads, turned, 1, [grad_head])

    hidden_cols = lax.dynamic_slice_in_dim(student_hidden, t * slice_width, slice_width, 1)
    gain_cols = lax.dynamic_slice_in_dim(student_gain, t * slice_width, slice_width, 0)
    grad_hidden, grad_gain = finish(arrived, inv_scale, hidden_cols, gain_cols[None], width)
    return (grad_head, grad_hidden, grad_gain[0])


def solution(mesh):
    in_specs = (
        P("branch", "tok", None),
        P("branch", None),
        P("branch", None, "tok"),
        P("branch", None),
        P(),
        P("branch", "tok"),
        P(None, "branch"),
        P("branch"),
    )
    out_specs = (P("branch", "tok"), P("branch", "tok"), P("tok"))
    return jax.shard_map(per_device, mesh=mesh, in_specs=in_specs, out_specs=out_specs, check_vma=False)
```

```python
import functools

import jax
import jax.numpy as jnp
from jax import lax
from jax.experimental import pallas as pl
from jax.experimental.pallas import tpu as pltpu
from jax.sharding import PartitionSpec as P


DEN = 64

eps = 1e-05
mix_label = 0.25
loss_scale = 64.0


def swap(value, axis, flip):
    size = lax.axis_size(axis)
    return lax.ppermute(value, axis, [(i, i ^ flip) for i in range(size)])


VMEM = pl.BlockSpec(memory_space=pltpu.VMEM)
MIB = 1 << 20


def params(mib):
    return pltpu.CompilerParams(vmem_limit_bytes=mib * MIB)


def cost(flops, nbytes, exps=0):
    return pl.CostEstimate(flops=flops, bytes_accessed=nbytes, transcendentals=exps)


def position():
    b, t = lax.axis_index("branch"), lax.axis_index("tok")
    blocks = lax.axis_size("tok") // lax.axis_size("branch")
    return b, t, lax.rem(t, blocks), lax.div(t, blocks) ^ b


def normalized(values, gain):
    values = values.astype(jnp.float32)
    scale = lax.rsqrt(jnp.mean(values * values, axis=-1, keepdims=True) + eps)
    return (values * scale * gain).astype(jnp.bfloat16), scale


def first_kernel(branches, *refs):
    teacher, teacher_gain, student, student_gain = refs[:4]
    block_ref, *sent = refs[4 : 4 + branches]
    th_ref, tg_ref, sh_ref, sg_ref, normed_ref, sems = refs[4 + branches :]
    b = lax.axis_index("branch")
    half, part = sent[0].shape
    rows = pl.ds(pl.multiple_of(lax.axis_index("tok") % 2 * half, half), half)
    copies = [
        pltpu.make_async_copy(source, target, sems.at[i])
        for i, (source, target) in enumerate(
            ((student.at[rows], sh_ref), (student_gain, sg_ref), (teacher, th_ref), (teacher_gain, tg_ref))
        )
    ]
    for copy in copies:
        copy.start()
    for copy in copies[:2]:
        copy.wait()
    normed_ref[...], unused = normalized(sh_ref[...], sg_ref[...])
    for r in range(1, branches):
        sent[r - 1][...] = normed_ref[:, pl.ds(pl.multiple_of((b ^ r) * part, part), part)]
    for copy in copies[2:]:
        copy.wait()
    block_ref[...], unused = normalized(th_ref[0], tg_ref[...])


def first_blocks(teacher_hidden, teacher_gain, student_hidden, student_gain, branches):
    rows, width = student_hidden.shape
    part = width // branches
    bf16, f32 = jnp.bfloat16, jnp.float32
    return pl.pallas_call(
        functools.partial(first_kernel, branches),
        out_shape=(
            jax.ShapeDtypeStruct(teacher_hidden.shape[1:], bf16),
            *[jax.ShapeDtypeStruct((rows // 2, part), bf16)] * (branches - 1),
        ),
        in_specs=[pl.BlockSpec(memory_space=pl.ANY)] * 4,
        out_specs=(VMEM,) * branches,
        scratch_shapes=[
            pltpu.VMEM(teacher_hidden.shape, bf16),
            pltpu.VMEM((1, width), f32),
            pltpu.VMEM((rows // 2, width), bf16),
            pltpu.VMEM((1, width), f32),
            pltpu.VMEM((rows // 2, width), bf16),
            pltpu.SemaphoreType.DMA((4,)),
        ],
        compiler_params=params(60),
        cost_estimate=cost(8 * rows * width, 4 * rows * width),
        name="first",
    )(teacher_hidden, teacher_gain, student_hidden, student_gain[None])


def gather_blocks(block, size):
    got = {0: block}
    for k in range(8, size, 8):
        got[k] = swap(block, "tok", k)
    for k in range(0, size, 8):
        got[k + 4] = swap(got[k], "tok", 4)
    got[6] = swap(block, "tok", 6)
    for k in range(0, size, 4):
        if k != 4:
            got[k + 2] = swap(got[k], "tok", 2)
    evens = sorted(got)
    half = len(evens) // 2
    arrays = [got[k] for k in evens]
    keys = [(k,) for k in evens]
    for group in (evens[:half], evens[half:]):
        arrays.append(swap(jnp.concatenate([got[k] for k in group], axis=0), "tok", 1))
        keys.append(tuple(k + 1 for k in group))
    return arrays, tuple(keys)


def own_dot_kernel(rows_ref, gain_ref, w_ref, out_ref, turned_ref, inv_ref, normed_ref):
    place = position()
    normed_ref[...], inv_ref[...] = normalized(rows_ref[...], gain_ref[...])
    part = turned_ref.shape[0]
    own = normed_ref[:, pl.ds(pl.multiple_of(place[0] * part, part), part)]
    turned_ref[...] = jnp.transpose(own)
    out_ref[...] = jnp.dot(own, w_ref[...], preferred_element_type=jnp.float32)


def own_dot(hidden, gain, head):
    rows, width = hidden.shape
    return pl.pallas_call(
        own_dot_kernel,
        out_shape=(
            jax.ShapeDtypeStruct((rows, head.shape[1]), jnp.float32),
            jax.ShapeDtypeStruct((head.shape[0], rows), jnp.bfloat16),
            jax.ShapeDtypeStruct((rows, 1), jnp.float32),
        ),
        in_specs=[VMEM] * 3,
        out_specs=(VMEM,) * 3,
        scratch_shapes=[pltpu.VMEM((rows, width), jnp.bfloat16)],
        compiler_params=params(16),
        cost_estimate=cost(2 * rows * head.size, 2 * head.size),
        name="owndot",
    )(hidden, gain[None], head)


def other_dot_kernel(mine_ref, other_ref, w_ref, out_ref, turned_ref, rows_ref):
    place = position()
    half = mine_ref.shape[0]
    core = place[1] % 2
    rows_ref[pl.ds(pl.multiple_of(core * half, half), half), :] = mine_ref[...]
    rows_ref[pl.ds(pl.multiple_of((1 - core) * half, half), half), :] = other_ref[...]
    out_ref[...] = jnp.dot(rows_ref[...], w_ref[...], preferred_element_type=jnp.float32)
    turned_ref[...] = jnp.transpose(rows_ref[...])


def other_dot(mine, other, head):
    rows = 2 * mine.shape[0]
    return pl.pallas_call(
        other_dot_kernel,
        out_shape=(
            jax.ShapeDtypeStruct((rows, head.shape[1]), jnp.float32),
            jax.ShapeDtypeStruct((mine.shape[1], rows), jnp.bfloat16),
        ),
        in_specs=[VMEM] * 3,
        out_specs=(VMEM, VMEM),
        scratch_shapes=[pltpu.VMEM((rows, mine.shape[1]), jnp.bfloat16)],
        compiler_params=params(16),
        cost_estimate=cost(2 * rows * head.size, 2 * head.size),
        name="otherdot",
    )(mine, other, head)


EXTRA = 8


def extra_rows(values, dtype):
    first = [value.astype(dtype).astype(jnp.float32) for value in values]
    rest = [value - lead for value, lead in zip(values, first)]
    empty = jnp.zeros((EXTRA - 2 * len(values), values[0].shape[1]), jnp.float32)
    return jnp.concatenate(first + rest + [empty], axis=0).astype(dtype)


def extra_values(rows, count):
    rows = rows.astype(jnp.float32)
    return [rows[i : i + 1] + rows[count + i : count + i + 1] for i in range(count)]


def tile_of(cols):
    return next((tile for tile in (256, 128) if cols % tile == 0), cols)


def column(row):
    count = row.shape[1]
    return jnp.transpose(jnp.broadcast_to(row, (128, count)))[:, :1]


def as_row(col):
    return jnp.transpose(jnp.broadcast_to(col, (col.shape[0], 128)))[:1]


def teacher_kernel(keys, half, *refs):
    place = position()
    blocks = refs[: len(keys)]
    w_ref, stat_ref, *exps = refs[len(keys) : -2]
    rows_ref, logits_ref = refs[-2:]
    mine = place[1] ^ (place[0] * half)
    for ref, owned in zip(blocks, keys):
        count = ref.shape[0] // len(owned)
        for j, k in enumerate(owned):
            start = pl.multiple_of((mine ^ k) * count, count)
            rows_ref[pl.ds(start, count), :] = ref[j * count : (j + 1) * count, :]

    cols = w_ref.shape[2]
    tile = tile_of(cols)
    if tile == cols:
        logits_ref[...] = jnp.dot(rows_ref[...], w_ref[0], preferred_element_type=jnp.float32)
    else:

        @pl.loop(0, cols // tile)
        def _(step):
            at = pl.ds(pl.multiple_of(step * tile, tile), tile)
            logits_ref[:, at] = jnp.dot(rows_ref[...], w_ref[0, :, at], preferred_element_type=jnp.float32)

    logits = logits_ref[...]
    top = jnp.max(logits, axis=1, keepdims=True)
    scaled = jnp.exp(logits - top)
    rows = exps[0].shape[0]
    for r, ref in enumerate(exps):
        ref[...] = scaled[r * rows : (r + 1) * rows].astype(ref.dtype)
    stat_ref[0:1, :] = as_row(top)
    stat_ref[1:2, :] = as_row(jnp.sum(scaled, axis=1, keepdims=True))


def teacher_softmax(got, keys, head, half, branches):
    width, cols = head.shape[1:]
    tokens = sum(part.shape[0] for part in got)
    return pl.pallas_call(
        functools.partial(teacher_kernel, keys, half),
        out_shape=(
            jax.ShapeDtypeStruct((2, tokens), jnp.float32),
            *[jax.ShapeDtypeStruct((tokens // branches, cols), jnp.bfloat16)] * branches,
        ),
        in_specs=[VMEM] * (len(got) + 1),
        out_specs=(VMEM,) * (1 + branches),
        scratch_shapes=[pltpu.VMEM((tokens, width), jnp.bfloat16), pltpu.VMEM((tokens, cols), jnp.float32)],
        compiler_params=params(28),
        cost_estimate=cost(2 * tokens * width * cols, 2 * width * cols, tokens * cols),
        name="teacher",
    )(*got, head)


def stats_kernel(count, *refs):
    place = position()
    parts = refs[:count]
    teacher_ref, weight_ref, logits_ref, out_ref = refs[count:]
    logits = parts[0][...]
    for ref in parts[1:]:
        logits = logits + ref[...]
    logits_ref[...] = logits
    top = jnp.max(logits, axis=1, keepdims=True)
    total = jnp.sum(jnp.exp(logits - top), axis=1, keepdims=True)
    rows = logits.shape[0]
    size = out_ref.shape[0] // count
    student = jnp.concatenate([as_row(top), as_row(total)], axis=0)
    for r in range(count):
        there = place[0] ^ r
        block = jnp.concatenate(
            [
                teacher_ref[:, r * rows : (r + 1) * rows],
                student,
                weight_ref[pl.ds(there, 1), :].astype(jnp.float32),
                jnp.zeros((3, rows), jnp.float32),
            ],
            axis=0,
        )
        out_ref[pl.ds(there * size, size)] = jnp.broadcast_to(block[None], (size, 8, rows))


def student_stats(parts, teacher_stats, weights, size):
    rows, cols = parts[0].shape
    count = len(parts)
    return pl.pallas_call(
        functools.partial(stats_kernel, count),
        out_shape=(
            jax.ShapeDtypeStruct((rows, cols), jnp.float32),
            jax.ShapeDtypeStruct((count * size, 8, rows), jnp.float32),
        ),
        in_specs=[VMEM] * (count + 2),
        out_specs=(VMEM, VMEM),
        compiler_params=params(12),
        cost_estimate=cost(8 * rows * cols, 12 * rows * cols, rows * cols),
        name="stats",
    )(*parts, teacher_stats, weights)


def grads_kernel(count, size, stats_ref, logits_ref, ids_ref, *refs):
    place = position()
    terms = refs[:count]
    grads_ref = refs[count]
    b, t = place[0], place[1]
    rows, cols = logits_ref.shape
    logits = logits_ref[...]
    shard = lax.broadcasted_iota(jnp.int32, (rows, cols), 1)
    targets = jnp.where(shard == column(ids_ref[...]) - t * cols, mix_label, 0.0)
    probs = None
    for r in range(count):
        start = (b ^ r) * size
        block = stats_ref[pl.ds(start, size)]
        here = stats_ref[start + t]
        peak = jnp.max(block[:, 0, :], axis=0, keepdims=True)
        total = jnp.sum(block[:, 1, :] * jnp.exp(block[:, 0, :] - peak), axis=0, keepdims=True)
        scale = ((1.0 - mix_label) / DEN) * here[4:5] * jnp.exp(here[0:1] - peak) / total
        targets = targets + terms[r][...].astype(jnp.float32) * column(scale)
        if r == 0:
            peak = jnp.max(block[:, 2, :], axis=0, keepdims=True)
            total = jnp.sum(block[:, 3, :] * jnp.exp(block[:, 2, :] - peak), axis=0, keepdims=True)
            probs = jnp.exp(logits - column(peak)) / column(total)
    grads = (loss_scale * (probs - targets)).astype(grads_ref.dtype)
    grads_ref[:rows] = grads
    grads_ref[rows:] = jnp.zeros((EXTRA, cols), grads.dtype)
    dots = as_row(jnp.sum(grads.astype(jnp.float32) * logits, axis=1, keepdims=True))
    grads_ref[rows:, :rows] = extra_rows([dots], grads.dtype)


def make_grads(stats, logits, ids, terms, size):
    rows, cols = logits.shape
    count = len(terms)
    return pl.pallas_call(
        functools.partial(grads_kernel, count, size),
        out_shape=jax.ShapeDtypeStruct((rows + EXTRA, cols), jnp.bfloat16),
        in_specs=[VMEM] * (count + 3),
        out_specs=VMEM,
        compiler_params=params(12),
        cost_estimate=cost(16 * rows * cols, 10 * rows * cols, rows * cols),
        name="grads",
    )(stats, logits, ids, *terms)


def pieces_kernel(parity, width, grads_ref, w_ref, out_ref, turned_ref):
    place = position()
    rows = out_ref.shape[1]
    turned_ref[...] = jnp.transpose(grads_ref[:rows])
    count = (out_ref.shape[0] - EXTRA) // width
    for k in range(count):
        start = pl.multiple_of((place[2] ^ (2 * k + parity)) * width, width)
        acc = jnp.dot(w_ref[pl.ds(start, width)], turned_ref[...], preferred_element_type=jnp.float32)
        out_ref[k * width : (k + 1) * width] = acc.astype(out_ref.dtype)
    out_ref[count * width :] = grads_ref[rows:, :rows]


def normed_grad_pieces(grads, head, blocks, parity):
    rows, cols = grads.shape[0] - EXTRA, grads.shape[1]
    width = head.shape[0] // blocks
    return pl.pallas_call(
        functools.partial(pieces_kernel, parity, width),
        out_shape=jax.ShapeDtypeStruct((blocks // 2 * width + EXTRA, rows), jnp.bfloat16),
        in_specs=[VMEM] * 2,
        out_specs=VMEM,
        scratch_shapes=[pltpu.VMEM((cols, rows), jnp.bfloat16)],
        compiler_params=params(16),
        cost_estimate=cost(rows * head.size, head.size),
        name="pieces",
    )(grads, head)


def fold_kernel(mine_ref, got_ref, *out):
    f32 = jnp.float32
    width = out[0].shape[0] - EXTRA
    full = len(out) * width
    dots = extra_values(mine_ref[full:], 1)[0] + extra_values(got_ref[full:], 1)[0]
    for k, ref in enumerate(out):
        at = slice(k * width, (k + 1) * width)
        ref[:width] = (mine_ref[at].astype(f32) + got_ref[at].astype(f32)).astype(ref.dtype)
        ref[width:] = extra_rows([dots], ref.dtype)


def fold(mine, got, width):
    full, rows = mine.shape
    count = (full - EXTRA) // width
    return pl.pallas_call(
        fold_kernel,
        out_shape=(jax.ShapeDtypeStruct((width + EXTRA, rows), mine.dtype),) * count,
        in_specs=[VMEM, VMEM],
        out_specs=(VMEM,) * count,
        compiler_params=params(8),
        cost_estimate=cost(mine.size, 6 * mine.size),
        name="fold",
    )(mine, got)


def split_kernel(count, *refs):
    place = position()
    turned, out = refs[-2 * count : -count], refs[-count:]
    each = len(refs) // count - 2
    f32 = jnp.float32
    width, rows = out[0].shape[0] - EXTRA, out[0].shape[1]
    block = pl.multiple_of(place[2] * width, width)
    totals, dots, gain = [], [], 0.0
    for r in range(count):
        total = refs[r * each][...].astype(f32)
        for ref in refs[r * each + 1 : (r + 1) * each]:
            total = total + ref[...].astype(f32)
        dots.append(extra_values(total[width:], 1)[0])
        totals.append(total[:width])
        gain = gain + jnp.sum(totals[r] * turned[r][pl.ds(block, width)].astype(f32), axis=1, keepdims=True)
    gain = as_row(gain)
    lanes = min(width, rows)
    gains = [gain[:, i : i + lanes] for i in range(0, width, lanes)]
    if lanes < rows:
        gains = [jnp.concatenate([row, jnp.zeros((1, rows - lanes), f32)], axis=1) for row in gains]
    for r in range(count):
        total = totals[r].astype(out[0].dtype)
        extra = extra_rows([dots[r]] + gains, out[0].dtype)
        for kh in range(count):

            @pl.when((place[3] ^ kh) == r)
            def _():
                out[kh][:width] = total
                out[kh][width:] = extra


def split(parts, turned):
    count = len(parts)
    shape = parts[0][0].shape
    each = len(parts[0])
    return pl.pallas_call(
        functools.partial(split_kernel, count),
        out_shape=(jax.ShapeDtypeStruct(shape, parts[0][0].dtype),) * count,
        in_specs=[VMEM] * (count * (each + 1)),
        out_specs=(VMEM,) * count,
        compiler_params=params(8),
        cost_estimate=cost(8 * count * shape[0] * shape[1], 12 * count * shape[0] * shape[1]),
        name="split",
    )(*[part for some in parts for part in some], *turned)


def head_grad_kernel(count, *refs):
    grads, turned = refs[:count], refs[count : 2 * count]
    out_ref, grads_ref = refs[-2:]
    rows = grads_ref.shape[0] // count

    @pl.when(pl.program_id(0) == 0)
    def _():
        for r in range(count):
            grads_ref[r * rows : (r + 1) * rows, :] = grads[r][:rows]

    lhs = jnp.concatenate([ref[...] for ref in turned], axis=1)
    out_ref[...] = jnp.dot(lhs, grads_ref[...], preferred_element_type=jnp.float32)


def head_grad(grads, turned, half, done):
    count = len(grads)
    full, cols = grads[0].shape
    part, rows = turned[0].shape
    tile = tile_of(part)
    steps = part // tile // 2
    return pl.pallas_call(
        functools.partial(head_grad_kernel, count),
        out_shape=jax.ShapeDtypeStruct((part, cols), jnp.float32),
        grid=(steps,),
        in_specs=[pl.BlockSpec((full, cols), lambda i: (0, 0))] * count
        + [pl.BlockSpec((tile, rows), lambda i: (i + half * steps, 0))] * count
        + [pl.BlockSpec(memory_space=pl.ANY)] * len(done),
        out_specs=pl.BlockSpec((tile, cols), lambda i: (i + half * steps, 0)),
        scratch_shapes=[pltpu.VMEM((count * rows, cols), jnp.bfloat16)],
        input_output_aliases={2 * count: 0} if done else {},
        compiler_params=params(16),
        cost_estimate=cost(count * rows * part * cols, 2 * part * cols),
        name="headgrad",
    )(*grads, *turned, *done)


def last_kernel(count, width, inv_ref, hidden_ref, gain_ref, *refs):
    parts = refs[:count]
    out_ref, gain_out_ref = refs[count:]
    total = parts[0][...].astype(jnp.float32)
    for ref in parts[1:]:
        total = total + ref[...].astype(jnp.float32)
    piece, rows = total.shape[0] - EXTRA, total.shape[1]
    lanes = min(piece, rows)
    dots, *gains = extra_values(total[piece:], 1 + piece // lanes)
    gain_out_ref[...] = jnp.concatenate([row[:, :lanes] for row in gains], axis=1) / gain_ref[...]
    normed_grads = jnp.transpose(total[:piece])
    inv = inv_ref[...]
    scaled = hidden_ref[...].astype(jnp.float32) * inv
    out_ref[...] = inv * gain_ref[...] * normed_grads - scaled * (inv * column(dots) / width)


def finish(parts, inv, hidden, gain, width):
    piece, rows = parts[0].shape[0] - EXTRA, parts[0].shape[1]
    return pl.pallas_call(
        functools.partial(last_kernel, len(parts), width),
        out_shape=(
            jax.ShapeDtypeStruct((rows, piece), jnp.float32),
            jax.ShapeDtypeStruct((1, piece), jnp.float32),
        ),
        in_specs=[VMEM] * (3 + len(parts)),
        out_specs=(VMEM, VMEM),
        compiler_params=params(12),
        cost_estimate=cost(16 * rows * piece, 12 * rows * piece),
        name="last",
    )(inv, hidden, gain, *parts)


def load_kernel(from_ref, to_ref, sem):
    copy = pltpu.make_async_copy(from_ref, to_ref, sem)
    copy.start()
    copy.wait()


def load(value):
    return pl.pallas_call(
        load_kernel,
        out_shape=jax.ShapeDtypeStruct(value.shape, value.dtype),
        in_specs=[pl.BlockSpec(memory_space=pltpu.HBM)],
        out_specs=VMEM,
        scratch_shapes=[pltpu.SemaphoreType.DMA],
        compiler_params=params(16),
        cost_estimate=cost(0, 4 * value.size),
        name="load",
    )(value)


def per_device(
    teacher_hidden,
    teacher_gain,
    teacher_head,
    student_hidden,
    student_gain,
    student_head,
    cluster_weights,
    token_ids,
):
    branches = lax.axis_size("branch")
    size = lax.axis_size("tok")
    t = lax.axis_index("tok")
    rows, width = student_hidden.shape
    blocks = size // branches
    teacher_block, *sent = first_blocks(teacher_hidden, teacher_gain, student_hidden, student_gain, branches)

    loaded = load(student_head)
    own_partial, own_turned, inv_scale = own_dot(student_hidden, student_gain, loaded)
    turned, partials = [own_turned], [own_partial]
    for r in range(1, branches):
        mine = swap(sent[r - 1], "branch", r)
        other = swap(mine, "tok", 1)
        partial, fetched = other_dot(mine, other, loaded)
        turned.append(fetched)
        partials.append(swap(partial, "branch", r))

    got, keys = gather_blocks(teacher_block, size)
    teacher_stats, *exps = teacher_softmax(got, keys, teacher_head, blocks, branches)
    terms = [exps[0]] + [swap(exps[r], "branch", r) for r in range(1, branches)]

    weights = cluster_weights[:, 0].reshape(branches, rows)
    logits, stats = student_stats(partials, teacher_stats, weights, size)
    stats = lax.all_to_all(stats, ("branch", "tok"), 0, 0, tiled=True)
    logit_grads = make_grads(stats, logits, token_ids[None], terms, size)
    all_grads = [logit_grads] + [swap(logit_grads, "branch", r) for r in range(1, branches)]

    slice_width = width // size
    parts = []
    for r in range(branches):
        send = normed_grad_pieces(all_grads[r], loaded, blocks, 1)
        send = swap(send, "tok", 1)
        keep = normed_grad_pieces(all_grads[r], loaded, blocks, 0)
        folded = fold(keep, send, slice_width)
        parts.append([folded[0]] + [swap(folded[k], "tok", 2 * k) for k in range(1, blocks // 2)])
    owned = split(parts, turned)
    arrived = []
    for kh in range(branches):
        perm = []
        for i in range(branches * size):
            bb, h, rest = i // size, (i % size) // blocks, i % blocks
            perm.append((i, (h ^ kh) * size + bb * blocks + rest))
        arrived.append(lax.ppermute(owned[kh], ("branch", "tok"), perm))

    grad_head = head_grad(all_grads, turned, 0, [])
    grad_head = head_grad(all_grads, turned, 1, [grad_head])

    hidden_cols = lax.dynamic_slice_in_dim(student_hidden, t * slice_width, slice_width, 1)
    gain_cols = lax.dynamic_slice_in_dim(student_gain, t * slice_width, slice_width, 0)
    grad_hidden, grad_gain = finish(arrived, inv_scale, hidden_cols, gain_cols[None], width)
    return (grad_head, grad_hidden, grad_gain[0])


def solution(mesh):
    in_specs = (
        P("branch", "tok", None),
        P("branch", None),
        P("branch", None, "tok"),
        P("branch", None),
        P(),
        P("branch", "tok"),
        P(None, "branch"),
        P("branch"),
    )
    out_specs = (P("branch", "tok"), P("branch", "tok"), P("tok"))
    return jax.shard_map(per_device, mesh=mesh, in_specs=in_specs, out_specs=out_specs, check_vma=False)
```

```python
import functools

import jax
import jax.numpy as jnp
from jax import lax
from jax.experimental import pallas as pl
from jax.experimental.pallas import tpu as pltpu
from jax.sharding import PartitionSpec as P


DEN = 64

eps = 1e-05
mix_label = 0.25
loss_scale = 64.0


def swap(value, axis, flip):
    size = lax.axis_size(axis)
    return lax.ppermute(value, axis, [(i, i ^ flip) for i in range(size)])


VMEM = pl.BlockSpec(memory_space=pltpu.VMEM)
MIB = 1 << 20


def params(mib):
    return pltpu.CompilerParams(vmem_limit_bytes=mib * MIB)


def cost(flops, nbytes, exps=0):
    return pl.CostEstimate(flops=flops, bytes_accessed=nbytes, transcendentals=exps)


def position():
    b, t = lax.axis_index("branch"), lax.axis_index("tok")
    blocks = lax.axis_size("tok") // lax.axis_size("branch")
    return b, t, lax.rem(t, blocks), lax.div(t, blocks) ^ b


def normalized(values, gain):
    values = values.astype(jnp.float32)
    scale = lax.rsqrt(jnp.mean(values * values, axis=-1, keepdims=True) + eps)
    return (values * scale * gain).astype(jnp.bfloat16), scale


def first_kernel(branches, *refs):
    teacher, teacher_gain, student, student_gain = refs[:4]
    block_ref, *sent = refs[4 : 4 + branches]
    th_ref, tg_ref, sh_ref, sg_ref, normed_ref, sems = refs[4 + branches :]
    b = lax.axis_index("branch")
    half, part = sent[0].shape
    rows = pl.ds(pl.multiple_of(lax.axis_index("tok") % 2 * half, half), half)
    copies = [
        pltpu.make_async_copy(source, target, sems.at[i])
        for i, (source, target) in enumerate(
            ((student.at[rows], sh_ref), (student_gain, sg_ref), (teacher, th_ref), (teacher_gain, tg_ref))
        )
    ]
    for copy in copies:
        copy.start()
    for copy in copies[:2]:
        copy.wait()
    normed_ref[...], unused = normalized(sh_ref[...], sg_ref[...])
    for r in range(1, branches):
        sent[r - 1][...] = normed_ref[:, pl.ds(pl.multiple_of((b ^ r) * part, part), part)]
    for copy in copies[2:]:
        copy.wait()
    block_ref[...], unused = normalized(th_ref[0], tg_ref[...])


def first_blocks(teacher_hidden, teacher_gain, student_hidden, student_gain, branches):
    rows, width = student_hidden.shape
    part = width // branches
    bf16, f32 = jnp.bfloat16, jnp.float32
    return pl.pallas_call(
        functools.partial(first_kernel, branches),
        out_shape=(
            jax.ShapeDtypeStruct(teacher_hidden.shape[1:], bf16),
            *[jax.ShapeDtypeStruct((rows // 2, part), bf16)] * (branches - 1),
        ),
        in_specs=[pl.BlockSpec(memory_space=pl.ANY)] * 4,
        out_specs=(VMEM,) * branches,
        scratch_shapes=[
            pltpu.VMEM(teacher_hidden.shape, bf16),
            pltpu.VMEM((1, width), f32),
            pltpu.VMEM((rows // 2, width), bf16),
            pltpu.VMEM((1, width), f32),
            pltpu.VMEM((rows // 2, width), bf16),
            pltpu.SemaphoreType.DMA((4,)),
        ],
        compiler_params=params(60),
        cost_estimate=cost(8 * rows * width, 4 * rows * width),
        name="first",
    )(teacher_hidden, teacher_gain, student_hidden, student_gain[None])


def gather_blocks(block, size):
    got = {0: block}
    for k in range(8, size, 8):
        got[k] = swap(block, "tok", k)
    for k in range(0, size, 8):
        got[k + 4] = swap(got[k], "tok", 4)
    got[6] = swap(block, "tok", 6)
    for k in range(0, size, 4):
        if k != 4:
            got[k + 2] = swap(got[k], "tok", 2)
    evens = sorted(got)
    half = len(evens) // 2
    arrays = [got[k] for k in evens]
    keys = [(k,) for k in evens]
    for group in (evens[:half], evens[half:]):
        joined = jnp.concatenate([got[k] for k in group], axis=0) if len(group) > 1 else got[group[0]]
        arrays.append(swap(joined, "tok", 1))
        keys.append(tuple(k + 1 for k in group))
    return arrays, tuple(keys)


def own_dot_kernel(rows_ref, gain_ref, w_ref, out_ref, turned_ref, inv_ref, normed_ref):
    place = position()
    normed_ref[...], inv_ref[...] = normalized(rows_ref[...], gain_ref[...])
    part = turned_ref.shape[0]
    own = normed_ref[:, pl.ds(pl.multiple_of(place[0] * part, part), part)]
    turned_ref[...] = jnp.transpose(own)
    out_ref[...] = jnp.dot(own, w_ref[...], preferred_element_type=jnp.float32)


def own_dot(hidden, gain, head):
    rows, width = hidden.shape
    return pl.pallas_call(
        own_dot_kernel,
        out_shape=(
            jax.ShapeDtypeStruct((rows, head.shape[1]), jnp.float32),
            jax.ShapeDtypeStruct((head.shape[0], rows), jnp.bfloat16),
            jax.ShapeDtypeStruct((rows, 1), jnp.float32),
        ),
        in_specs=[VMEM] * 3,
        out_specs=(VMEM,) * 3,
        scratch_shapes=[pltpu.VMEM((rows, width), jnp.bfloat16)],
        compiler_params=params(16),
        cost_estimate=cost(2 * rows * head.size, 2 * head.size),
        name="owndot",
    )(hidden, gain[None], head)


def other_dot_kernel(mine_ref, other_ref, w_ref, out_ref, turned_ref, rows_ref):
    place = position()
    half = mine_ref.shape[0]
    core = place[1] % 2
    rows_ref[pl.ds(pl.multiple_of(core * half, half), half), :] = mine_ref[...]
    rows_ref[pl.ds(pl.multiple_of((1 - core) * half, half), half), :] = other_ref[...]
    out_ref[...] = jnp.dot(rows_ref[...], w_ref[...], preferred_element_type=jnp.float32)
    turned_ref[...] = jnp.transpose(rows_ref[...])


def other_dot(mine, other, head):
    rows = 2 * mine.shape[0]
    return pl.pallas_call(
        other_dot_kernel,
        out_shape=(
            jax.ShapeDtypeStruct((rows, head.shape[1]), jnp.float32),
            jax.ShapeDtypeStruct((mine.shape[1], rows), jnp.bfloat16),
        ),
        in_specs=[VMEM] * 3,
        out_specs=(VMEM, VMEM),
        scratch_shapes=[pltpu.VMEM((rows, mine.shape[1]), jnp.bfloat16)],
        compiler_params=params(16),
        cost_estimate=cost(2 * rows * head.size, 2 * head.size),
        name="otherdot",
    )(mine, other, head)


EXTRA = 8


def extra_rows(values, dtype):
    first = [value.astype(dtype).astype(jnp.float32) for value in values]
    rest = [value - lead for value, lead in zip(values, first)]
    empty = jnp.zeros((EXTRA - 2 * len(values), values[0].shape[1]), jnp.float32)
    return jnp.concatenate(first + rest + [empty], axis=0).astype(dtype)


def extra_values(rows, count):
    rows = rows.astype(jnp.float32)
    return [rows[i : i + 1] + rows[count + i : count + i + 1] for i in range(count)]


def tile_of(cols):
    return next((tile for tile in (256, 128) if cols % tile == 0), cols)


def column(row):
    count = row.shape[1]
    return jnp.transpose(jnp.broadcast_to(row, (128, count)))[:, :1]


def as_row(col):
    return jnp.transpose(jnp.broadcast_to(col, (col.shape[0], 128)))[:1]


def teacher_kernel(keys, half, *refs):
    place = position()
    blocks = refs[: len(keys)]
    w_ref, stat_ref, *exps = refs[len(keys) : -2]
    rows_ref, logits_ref = refs[-2:]
    mine = place[1] ^ (place[0] * half)
    for ref, owned in zip(blocks, keys):
        count = ref.shape[0] // len(owned)
        for j, k in enumerate(owned):
            start = pl.multiple_of((mine ^ k) * count, count)
            rows_ref[pl.ds(start, count), :] = ref[j * count : (j + 1) * count, :]

    cols = w_ref.shape[2]
    tile = tile_of(cols)
    if tile == cols:
        logits_ref[...] = jnp.dot(rows_ref[...], w_ref[0], preferred_element_type=jnp.float32)
    else:

        @pl.loop(0, cols // tile)
        def _(step):
            at = pl.ds(pl.multiple_of(step * tile, tile), tile)
            logits_ref[:, at] = jnp.dot(rows_ref[...], w_ref[0, :, at], preferred_element_type=jnp.float32)

    logits = logits_ref[...]
    top = jnp.max(logits, axis=1, keepdims=True)
    scaled = jnp.exp(logits - top)
    rows = exps[0].shape[0]
    for r, ref in enumerate(exps):
        ref[...] = scaled[r * rows : (r + 1) * rows].astype(ref.dtype)
    stat_ref[0:1, :] = as_row(top)
    stat_ref[1:2, :] = as_row(jnp.sum(scaled, axis=1, keepdims=True))


def teacher_softmax(got, keys, head, half, branches):
    width, cols = head.shape[1:]
    tokens = sum(part.shape[0] for part in got)
    return pl.pallas_call(
        functools.partial(teacher_kernel, keys, half),
        out_shape=(
            jax.ShapeDtypeStruct((2, tokens), jnp.float32),
            *[jax.ShapeDtypeStruct((tokens // branches, cols), jnp.bfloat16)] * branches,
        ),
        in_specs=[VMEM] * (len(got) + 1),
        out_specs=(VMEM,) * (1 + branches),
        scratch_shapes=[pltpu.VMEM((tokens, width), jnp.bfloat16), pltpu.VMEM((tokens, cols), jnp.float32)],
        compiler_params=params(28),
        cost_estimate=cost(2 * tokens * width * cols, 2 * width * cols, tokens * cols),
        name="teacher",
    )(*got, head)


def stats_kernel(count, *refs):
    place = position()
    parts = refs[:count]
    teacher_ref, weight_ref, logits_ref, out_ref = refs[count:]
    logits = parts[0][...]
    for ref in parts[1:]:
        logits = logits + ref[...]
    logits_ref[...] = logits
    top = jnp.max(logits, axis=1, keepdims=True)
    total = jnp.sum(jnp.exp(logits - top), axis=1, keepdims=True)
    rows = logits.shape[0]
    size = out_ref.shape[0] // count
    student = jnp.concatenate([as_row(top), as_row(total)], axis=0)
    for r in range(count):
        there = place[0] ^ r
        block = jnp.concatenate(
            [
                teacher_ref[:, r * rows : (r + 1) * rows],
                student,
                weight_ref[pl.ds(there, 1), :].astype(jnp.float32),
                jnp.zeros((3, rows), jnp.float32),
            ],
            axis=0,
        )
        out_ref[pl.ds(there * size, size)] = jnp.broadcast_to(block[None], (size, 8, rows))


def student_stats(parts, teacher_stats, weights, size):
    rows, cols = parts[0].shape
    count = len(parts)
    return pl.pallas_call(
        functools.partial(stats_kernel, count),
        out_shape=(
            jax.ShapeDtypeStruct((rows, cols), jnp.float32),
            jax.ShapeDtypeStruct((count * size, 8, rows), jnp.float32),
        ),
        in_specs=[VMEM] * (count + 2),
        out_specs=(VMEM, VMEM),
        compiler_params=params(12),
        cost_estimate=cost(8 * rows * cols, 12 * rows * cols, rows * cols),
        name="stats",
    )(*parts, teacher_stats, weights)


def grads_kernel(count, size, stats_ref, logits_ref, ids_ref, *refs):
    place = position()
    terms = refs[:count]
    grads_ref = refs[count]
    b, t = place[0], place[1]
    rows, cols = logits_ref.shape
    logits = logits_ref[...]
    shard = lax.broadcasted_iota(jnp.int32, (rows, cols), 1)
    targets = jnp.where(shard == column(ids_ref[...]) - t * cols, mix_label, 0.0)
    probs = None
    for r in range(count):
        start = (b ^ r) * size
        block = stats_ref[pl.ds(start, size)]
        here = stats_ref[start + t]
        peak = jnp.max(block[:, 0, :], axis=0, keepdims=True)
        total = jnp.sum(block[:, 1, :] * jnp.exp(block[:, 0, :] - peak), axis=0, keepdims=True)
        scale = ((1.0 - mix_label) / DEN) * here[4:5] * jnp.exp(here[0:1] - peak) / total
        targets = targets + terms[r][...].astype(jnp.float32) * column(scale)
        if r == 0:
            peak = jnp.max(block[:, 2, :], axis=0, keepdims=True)
            total = jnp.sum(block[:, 3, :] * jnp.exp(block[:, 2, :] - peak), axis=0, keepdims=True)
            probs = jnp.exp(logits - column(peak)) / column(total)
    grads = (loss_scale * (probs - targets)).astype(grads_ref.dtype)
    grads_ref[:rows] = grads
    grads_ref[rows:] = jnp.zeros((EXTRA, cols), grads.dtype)
    dots = as_row(jnp.sum(grads.astype(jnp.float32) * logits, axis=1, keepdims=True))
    grads_ref[rows:, :rows] = extra_rows([dots], grads.dtype)


def make_grads(stats, logits, ids, terms, size):
    rows, cols = logits.shape
    count = len(terms)
    return pl.pallas_call(
        functools.partial(grads_kernel, count, size),
        out_shape=jax.ShapeDtypeStruct((rows + EXTRA, cols), jnp.bfloat16),
        in_specs=[VMEM] * (count + 3),
        out_specs=VMEM,
        compiler_params=params(12),
        cost_estimate=cost(16 * rows * cols, 10 * rows * cols, rows * cols),
        name="grads",
    )(stats, logits, ids, *terms)


def pieces_kernel(parity, width, grads_ref, w_ref, out_ref, turned_ref):
    place = position()
    rows = out_ref.shape[1]
    turned_ref[...] = jnp.transpose(grads_ref[:rows])
    count = (out_ref.shape[0] - EXTRA) // width
    for k in range(count):
        start = pl.multiple_of((place[2] ^ (2 * k + parity)) * width, width)
        acc = jnp.dot(w_ref[pl.ds(start, width)], turned_ref[...], preferred_element_type=jnp.float32)
        out_ref[k * width : (k + 1) * width] = acc.astype(out_ref.dtype)
    out_ref[count * width :] = grads_ref[rows:, :rows]


def normed_grad_pieces(grads, head, blocks, parity):
    rows, cols = grads.shape[0] - EXTRA, grads.shape[1]
    width = head.shape[0] // blocks
    return pl.pallas_call(
        functools.partial(pieces_kernel, parity, width),
        out_shape=jax.ShapeDtypeStruct((blocks // 2 * width + EXTRA, rows), jnp.bfloat16),
        in_specs=[VMEM] * 2,
        out_specs=VMEM,
        scratch_shapes=[pltpu.VMEM((cols, rows), jnp.bfloat16)],
        compiler_params=params(16),
        cost_estimate=cost(rows * head.size, head.size),
        name="pieces",
    )(grads, head)


def fold_kernel(mine_ref, got_ref, *out):
    f32 = jnp.float32
    width = out[0].shape[0] - EXTRA
    full = len(out) * width
    dots = extra_values(mine_ref[full:], 1)[0] + extra_values(got_ref[full:], 1)[0]
    for k, ref in enumerate(out):
        at = slice(k * width, (k + 1) * width)
        ref[:width] = (mine_ref[at].astype(f32) + got_ref[at].astype(f32)).astype(ref.dtype)
        ref[width:] = extra_rows([dots], ref.dtype)


def fold(mine, got, width):
    full, rows = mine.shape
    count = (full - EXTRA) // width
    return pl.pallas_call(
        fold_kernel,
        out_shape=(jax.ShapeDtypeStruct((width + EXTRA, rows), mine.dtype),) * count,
        in_specs=[VMEM, VMEM],
        out_specs=(VMEM,) * count,
        compiler_params=params(8),
        cost_estimate=cost(mine.size, 6 * mine.size),
        name="fold",
    )(mine, got)


def join_kernel(gains, *refs):
    out = refs[-1]
    width, rows = out.shape[0] - EXTRA, out.shape[1]
    total = refs[0][...].astype(jnp.float32)
    for ref in refs[1:-1]:
        total = total + ref[...].astype(jnp.float32)
    dots = extra_values(total[width:], 1)
    out[:width] = total[:width].astype(out.dtype)
    out[width:] = extra_rows(dots + [jnp.zeros((1, rows), jnp.float32)] * gains, out.dtype)


def join(parts, gains):
    shape, dtype = parts[0].shape, parts[0].dtype
    return pl.pallas_call(
        functools.partial(join_kernel, gains),
        out_shape=jax.ShapeDtypeStruct(shape, dtype),
        in_specs=[VMEM] * len(parts),
        out_specs=VMEM,
        compiler_params=params(8),
        cost_estimate=cost(4 * shape[0] * shape[1], 10 * shape[0] * shape[1]),
        name="join",
    )(*parts)


def split_kernel(count, own_ref, *refs):
    place = position()
    turned, out, rest_ref = refs[-2 * count : -count], refs[-count:-1], refs[-1]
    each = (len(refs) - 2 * count) // (count - 1)
    f32 = jnp.float32
    width, rows = own_ref.shape[0] - EXTRA, own_ref.shape[1]
    block = pl.ds(pl.multiple_of(place[2] * width, width), width)
    totals, dots = [own_ref[:width].astype(f32)], [jnp.zeros((1, rows), f32)]
    for r in range(count - 1):
        total = refs[r * each][...].astype(f32)
        for ref in refs[r * each + 1 : (r + 1) * each]:
            total = total + ref[...].astype(f32)
        dots.append(extra_values(total[width:], 1)[0])
        totals.append(total[:width])
    gain = sum(
        jnp.sum(totals[r] * turned[r][block].astype(f32), axis=1, keepdims=True) for r in range(count)
    )
    gain = as_row(gain)
    lanes = min(width, rows)
    gains = [gain[:, i : i + lanes] for i in range(0, width, lanes)]
    if lanes < rows:
        gains = [jnp.concatenate([row, jnp.zeros((1, rows - lanes), f32)], axis=1) for row in gains]
    for r in range(1, count):
        out[r - 1][:width] = totals[r].astype(own_ref.dtype)
        out[r - 1][width:] = extra_rows([dots[r]] + gains, own_ref.dtype)
    rest_ref[...] = extra_rows([dots[0]] + gains, own_ref.dtype)


def split(own, parts, turned):
    shape, dtype = own.shape, own.dtype
    count = len(turned)
    flat = [part for some in parts for part in some]
    return pl.pallas_call(
        functools.partial(split_kernel, count),
        out_shape=(*[jax.ShapeDtypeStruct(shape, dtype)] * (count - 1), jax.ShapeDtypeStruct((EXTRA, shape[1]), dtype)),
        in_specs=[VMEM] * (1 + len(flat) + count),
        out_specs=(VMEM,) * count,
        compiler_params=params(8),
        cost_estimate=cost(8 * count * shape[0] * shape[1], 12 * count * shape[0] * shape[1]),
        name="split",
    )(own, *flat, *turned)


def head_grad_kernel(count, half, tile, *refs):
    grads, turned = refs[:count], refs[count : 2 * count]
    out_ref, grads_ref, total_ref, sems = refs[-4:]
    rows = grads_ref.shape[0] // count
    for r in range(count):
        grads_ref[r * rows : (r + 1) * rows, :] = grads[r][:rows]
    copies = []
    for i in range(total_ref.shape[0] // tile):
        here = slice(i * tile, (i + 1) * tile)
        start = half * total_ref.shape[0] + i * tile
        lhs = jnp.concatenate([ref[start : start + tile] for ref in turned], axis=1)
        total_ref[here] = jnp.dot(lhs, grads_ref[...], preferred_element_type=jnp.float32)
        copy = pltpu.make_async_copy(total_ref.at[here], out_ref.at[pl.ds(start, tile)], sems.at[i])
        copy.start()
        copies.append(copy)
    for copy in copies:
        copy.wait()


def head_grad(grads, turned, half, done):
    count = len(grads)
    cols = grads[0].shape[1]
    part, rows = turned[0].shape
    tile = tile_of(part // 2)
    steps = part // tile // 2
    whole = pl.BlockSpec(memory_space=pl.ANY)
    return pl.pallas_call(
        functools.partial(head_grad_kernel, count, half, tile),
        out_shape=jax.ShapeDtypeStruct((part, cols), jnp.float32),
        in_specs=[VMEM] * (2 * count) + [whole] * len(done),
        out_specs=whole,
        scratch_shapes=[
            pltpu.VMEM((count * rows, cols), jnp.bfloat16),
            pltpu.VMEM((part // 2, cols), jnp.float32),
            pltpu.SemaphoreType.DMA((steps,)),
        ],
        input_output_aliases={2 * count: 0} if done else {},
        compiler_params=params(16),
        cost_estimate=cost(count * rows * part * cols, 2 * part * cols),
        name="headgrad",
    )(*grads, *turned, *done)


def last_kernel(count, extras, width, inv_ref, hidden_ref, gain_ref, *refs):
    parts, rests = refs[:count], refs[count : count + extras]
    out_ref, gain_out_ref = refs[-2:]
    mine = jnp.where(position()[3] == 0, 1.0, 0.0)
    total = parts[0][...].astype(jnp.float32) * mine
    for ref in parts[1:]:
        total = total + ref[...].astype(jnp.float32)
    piece, rows = total.shape[0] - EXTRA, total.shape[1]
    extra = total[piece:] + rests[0][...].astype(jnp.float32) * mine
    for ref in rests[1:]:
        extra = extra + ref[...].astype(jnp.float32)
    lanes = min(piece, rows)
    dots, *gains = extra_values(extra, 1 + piece // lanes)
    gain_out_ref[...] = jnp.concatenate([row[:, :lanes] for row in gains], axis=1) / gain_ref[...]
    normed_grads = jnp.transpose(total[:piece])
    inv = inv_ref[...]
    scaled = hidden_ref[...].astype(jnp.float32) * inv
    out_ref[...] = inv * gain_ref[...] * normed_grads - scaled * (inv * column(dots) / width)


def finish(parts, rests, inv, hidden, gain, width):
    piece, rows = parts[0].shape[0] - EXTRA, parts[0].shape[1]
    return pl.pallas_call(
        functools.partial(last_kernel, len(parts), len(rests), width),
        out_shape=(
            jax.ShapeDtypeStruct((rows, piece), jnp.float32),
            jax.ShapeDtypeStruct((1, piece), jnp.float32),
        ),
        in_specs=[VMEM] * (3 + len(parts) + len(rests)),
        out_specs=(VMEM, VMEM),
        compiler_params=params(12),
        cost_estimate=cost(16 * rows * piece, 12 * rows * piece),
        name="last",
    )(inv, hidden, gain, *parts, *rests)


def load_kernel(from_ref, to_ref, sem):
    copy = pltpu.make_async_copy(from_ref, to_ref, sem)
    copy.start()
    copy.wait()


def load(value):
    return pl.pallas_call(
        load_kernel,
        out_shape=jax.ShapeDtypeStruct(value.shape, value.dtype),
        in_specs=[pl.BlockSpec(memory_space=pltpu.HBM)],
        out_specs=VMEM,
        scratch_shapes=[pltpu.SemaphoreType.DMA],
        compiler_params=params(16),
        cost_estimate=cost(0, 4 * value.size),
        name="load",
    )(value)


def per_device(
    teacher_hidden,
    teacher_gain,
    teacher_head,
    student_hidden,
    student_gain,
    student_head,
    cluster_weights,
    token_ids,
):
    branches = lax.axis_size("branch")
    size = lax.axis_size("tok")
    t = lax.axis_index("tok")
    rows, width = student_hidden.shape
    blocks = size // branches
    teacher_block, *sent = first_blocks(teacher_hidden, teacher_gain, student_hidden, student_gain, branches)

    loaded = load(student_head)
    own_partial, own_turned, inv_scale = own_dot(student_hidden, student_gain, loaded)
    turned, partials = [own_turned], [own_partial]
    for r in range(1, branches):
        mine = swap(sent[r - 1], "branch", r)
        other = swap(mine, "tok", 1)
        partial, fetched = other_dot(mine, other, loaded)
        turned.append(fetched)
        partials.append(swap(partial, "branch", r))

    got, keys = gather_blocks(teacher_block, size)
    teacher_stats, *exps = teacher_softmax(got, keys, teacher_head, blocks, branches)
    terms = [exps[0]] + [swap(exps[r], "branch", r) for r in range(1, branches)]

    weights = cluster_weights[:, 0].reshape(branches, rows)
    logits, stats = student_stats(partials, teacher_stats, weights, size)
    stats = lax.all_to_all(stats, ("branch", "tok"), 0, 0, tiled=True)
    logit_grads = make_grads(stats, logits, token_ids[None], terms, size)
    all_grads = [logit_grads] + [swap(logit_grads, "branch", r) for r in range(1, branches)]

    slice_width = width // size
    parts = []
    for r in range(branches):
        send = normed_grad_pieces(all_grads[r], loaded, blocks, 1)
        send = swap(send, "tok", 1)
        keep = normed_grad_pieces(all_grads[r], loaded, blocks, 0)
        folded = fold(keep, send, slice_width)
        parts.append([folded[0]] + [swap(folded[k], "tok", 2 * k) for k in range(1, blocks // 2)])
    def to_owner(value, r, kz):
        perm = []
        for bb in range(branches):
            for rest in range(blocks):
                perm.append((bb * size + (bb ^ kz) * blocks + rest, (bb ^ r) * size + bb * blocks + rest))
        return lax.ppermute(value, ("branch", "tok"), perm)

    early = join(parts[0], max(1, slice_width // rows))
    arrived = [early] + [to_owner(early, 0, kz) for kz in range(1, branches)]
    *late, rest = split(early, parts[1:], turned)
    for r in range(1, branches):
        arrived += [to_owner(late[r - 1], r, kz) for kz in range(branches)]
    rests = [rest] + [to_owner(rest, 0, kz) for kz in range(1, branches)]

    grad_head = head_grad(all_grads, turned, 0, [])
    grad_head = head_grad(all_grads, turned, 1, [grad_head])

    hidden_cols = lax.dynamic_slice_in_dim(student_hidden, t * slice_width, slice_width, 1)
    gain_cols = lax.dynamic_slice_in_dim(student_gain, t * slice_width, slice_width, 0)
    grad_hidden, grad_gain = finish(arrived, rests, inv_scale, hidden_cols, gain_cols[None], width)
    return (grad_head, grad_hidden, grad_gain[0])


def solution(mesh):
    in_specs = (
        P("branch", "tok", None),
        P("branch", None),
        P("branch", None, "tok"),
        P("branch", None),
        P(),
        P("branch", "tok"),
        P(None, "branch"),
        P("branch"),
    )
    out_specs = (P("branch", "tok"), P("branch", "tok"), P("tok"))
    return jax.shard_map(per_device, mesh=mesh, in_specs=in_specs, out_specs=out_specs, check_vma=False)
```

```python
import functools

import jax
import jax.numpy as jnp
from jax import lax
from jax.experimental import pallas as pl
from jax.experimental.pallas import tpu as pltpu
from jax.sharding import PartitionSpec as P


DEN = 64

eps = 1e-05
mix_label = 0.25
loss_scale = 64.0


def swap(value, axis, flip):
    size = lax.axis_size(axis)
    return lax.ppermute(value, axis, [(i, i ^ flip) for i in range(size)])


VMEM = pl.BlockSpec(memory_space=pltpu.VMEM)
MIB = 1 << 20


def params(mib):
    return pltpu.CompilerParams(vmem_limit_bytes=mib * MIB)


def cost(flops, nbytes, exps=0):
    return pl.CostEstimate(flops=flops, bytes_accessed=nbytes, transcendentals=exps)


def position():
    b, t = lax.axis_index("branch"), lax.axis_index("tok")
    blocks = lax.axis_size("tok") // lax.axis_size("branch")
    return b, t, lax.rem(t, blocks), lax.div(t, blocks) ^ b


def normalized(values, gain):
    values = values.astype(jnp.float32)
    scale = lax.rsqrt(jnp.mean(values * values, axis=-1, keepdims=True) + eps)
    return (values * scale * gain).astype(jnp.bfloat16), scale


def first_kernel(branches, *refs):
    teacher, teacher_gain, student, student_gain = refs[:4]
    block_ref, *sent = refs[4 : 4 + branches]
    th_ref, tg_ref, sh_ref, sg_ref, normed_ref, sems = refs[4 + branches :]
    b = lax.axis_index("branch")
    half, part = sent[0].shape
    rows = pl.ds(pl.multiple_of(lax.axis_index("tok") % 2 * half, half), half)
    copies = [
        pltpu.make_async_copy(source, target, sems.at[i])
        for i, (source, target) in enumerate(
            ((student.at[rows], sh_ref), (student_gain, sg_ref), (teacher, th_ref), (teacher_gain, tg_ref))
        )
    ]
    for copy in copies:
        copy.start()
    for copy in copies[:2]:
        copy.wait()
    normed_ref[...], unused = normalized(sh_ref[...], sg_ref[...])
    for r in range(1, branches):
        sent[r - 1][...] = normed_ref[:, pl.ds(pl.multiple_of((b ^ r) * part, part), part)]
    for copy in copies[2:]:
        copy.wait()
    block_ref[...], unused = normalized(th_ref[0], tg_ref[...])


def first_blocks(teacher_hidden, teacher_gain, student_hidden, student_gain, branches):
    rows, width = student_hidden.shape
    part = width // branches
    bf16, f32 = jnp.bfloat16, jnp.float32
    return pl.pallas_call(
        functools.partial(first_kernel, branches),
        out_shape=(
            jax.ShapeDtypeStruct(teacher_hidden.shape[1:], bf16),
            *[jax.ShapeDtypeStruct((rows // 2, part), bf16)] * (branches - 1),
        ),
        in_specs=[pl.BlockSpec(memory_space=pl.ANY)] * 4,
        out_specs=(VMEM,) * branches,
        scratch_shapes=[
            pltpu.VMEM(teacher_hidden.shape, bf16),
            pltpu.VMEM((1, width), f32),
            pltpu.VMEM((rows // 2, width), bf16),
            pltpu.VMEM((1, width), f32),
            pltpu.VMEM((rows // 2, width), bf16),
            pltpu.SemaphoreType.DMA((4,)),
        ],
        compiler_params=params(60),
        cost_estimate=cost(8 * rows * width, 4 * rows * width),
        name="first",
    )(teacher_hidden, teacher_gain, student_hidden, student_gain[None])


def gather_blocks(block, size):
    got = {0: block}
    for k in range(8, size, 8):
        got[k] = swap(block, "tok", k)
    for k in range(0, size, 8):
        got[k + 4] = swap(got[k], "tok", 4)
    got[6] = swap(block, "tok", 6)
    for k in range(0, size, 4):
        if k != 4:
            got[k + 2] = swap(got[k], "tok", 2)
    evens = sorted(got)
    half = len(evens) // 2
    arrays = [got[k] for k in evens]
    keys = [(k,) for k in evens]
    for group in (evens[:half], evens[half:]):
        arrays.append(swap(jnp.concatenate([got[k] for k in group], axis=0), "tok", 1))
        keys.append(tuple(k + 1 for k in group))
    return arrays, tuple(keys)


def own_dot_kernel(rows_ref, gain_ref, w_ref, out_ref, turned_ref, inv_ref, normed_ref):
    place = position()
    normed_ref[...], inv_ref[...] = normalized(rows_ref[...], gain_ref[...])
    part = turned_ref.shape[0]
    own = normed_ref[:, pl.ds(pl.multiple_of(place[0] * part, part), part)]
    turned_ref[...] = jnp.transpose(own)
    out_ref[...] = jnp.dot(own, w_ref[...], preferred_element_type=jnp.float32)


def own_dot(hidden, gain, head):
    rows, width = hidden.shape
    return pl.pallas_call(
        own_dot_kernel,
        out_shape=(
            jax.ShapeDtypeStruct((rows, head.shape[1]), jnp.float32),
            jax.ShapeDtypeStruct((head.shape[0], rows), jnp.bfloat16),
            jax.ShapeDtypeStruct((rows, 1), jnp.float32),
        ),
        in_specs=[VMEM] * 3,
        out_specs=(VMEM,) * 3,
        scratch_shapes=[pltpu.VMEM((rows, width), jnp.bfloat16)],
        compiler_params=params(16),
        cost_estimate=cost(2 * rows * head.size, 2 * head.size),
        name="owndot",
    )(hidden, gain[None], head)


def other_dot_kernel(mine_ref, other_ref, w_ref, out_ref, turned_ref, rows_ref):
    place = position()
    half = mine_ref.shape[0]
    core = place[1] % 2
    rows_ref[pl.ds(pl.multiple_of(core * half, half), half), :] = mine_ref[...]
    rows_ref[pl.ds(pl.multiple_of((1 - core) * half, half), half), :] = other_ref[...]
    out_ref[...] = jnp.dot(rows_ref[...], w_ref[...], preferred_element_type=jnp.float32)
    turned_ref[...] = jnp.transpose(rows_ref[...])


def other_dot(mine, other, head):
    rows = 2 * mine.shape[0]
    return pl.pallas_call(
        other_dot_kernel,
        out_shape=(
            jax.ShapeDtypeStruct((rows, head.shape[1]), jnp.float32),
            jax.ShapeDtypeStruct((mine.shape[1], rows), jnp.bfloat16),
        ),
        in_specs=[VMEM] * 3,
        out_specs=(VMEM, VMEM),
        scratch_shapes=[pltpu.VMEM((rows, mine.shape[1]), jnp.bfloat16)],
        compiler_params=params(16),
        cost_estimate=cost(2 * rows * head.size, 2 * head.size),
        name="otherdot",
    )(mine, other, head)


EXTRA = 8


def extra_rows(values, dtype):
    first = [value.astype(dtype).astype(jnp.float32) for value in values]
    rest = [value - lead for value, lead in zip(values, first)]
    empty = jnp.zeros((EXTRA - 2 * len(values), values[0].shape[1]), jnp.float32)
    return jnp.concatenate(first + rest + [empty], axis=0).astype(dtype)


def extra_values(rows, count):
    rows = rows.astype(jnp.float32)
    return [rows[i : i + 1] + rows[count + i : count + i + 1] for i in range(count)]


def tile_of(cols):
    return next((tile for tile in (256, 128) if cols % tile == 0), cols)


def column(row):
    count = row.shape[1]
    return jnp.transpose(jnp.broadcast_to(row, (128, count)))[:, :1]


def as_row(col):
    return jnp.transpose(jnp.broadcast_to(col, (col.shape[0], 128)))[:1]


def teacher_kernel(keys, half, *refs):
    place = position()
    blocks = refs[: len(keys)]
    w_ref, weight_ref, stat_ref, *exps = refs[len(keys) : -2]
    rows_ref, logits_ref = refs[-2:]
    mine = place[1] ^ (place[0] * half)
    for ref, owned in zip(blocks, keys):
        count = ref.shape[0] // len(owned)
        for j, k in enumerate(owned):
            start = pl.multiple_of((mine ^ k) * count, count)
            rows_ref[pl.ds(start, count), :] = ref[j * count : (j + 1) * count, :]

    cols = w_ref.shape[2]
    tile = tile_of(cols)
    if tile == cols:
        logits_ref[...] = jnp.dot(rows_ref[...], w_ref[0], preferred_element_type=jnp.float32)
    else:

        @pl.loop(0, cols // tile)
        def _(step):
            at = pl.ds(pl.multiple_of(step * tile, tile), tile)
            logits_ref[:, at] = jnp.dot(rows_ref[...], w_ref[0, :, at], preferred_element_type=jnp.float32)

    logits = logits_ref[...]
    top = jnp.max(logits, axis=1, keepdims=True)
    scaled = jnp.exp(logits - top)
    rows = exps[0].shape[0] - EXTRA
    for r, ref in enumerate(exps):
        ref[:rows] = scaled[r * rows : (r + 1) * rows].astype(ref.dtype)
        ref[rows:] = jnp.zeros((EXTRA, cols), ref.dtype)
        weight = weight_ref[pl.ds(place[0] ^ r, 1), :].astype(jnp.float32)
        ref[rows:, :rows] = extra_rows([weight], ref.dtype)
    stat_ref[0:1, :] = as_row(top)
    stat_ref[1:2, :] = as_row(jnp.sum(scaled, axis=1, keepdims=True))


def teacher_softmax(got, keys, head, weights, half):
    branches = weights.shape[0]
    width, cols = head.shape[1:]
    tokens = sum(part.shape[0] for part in got)
    return pl.pallas_call(
        functools.partial(teacher_kernel, keys, half),
        out_shape=(
            jax.ShapeDtypeStruct((2, tokens), jnp.float32),
            *[jax.ShapeDtypeStruct((tokens // branches + EXTRA, cols), jnp.bfloat16)] * branches,
        ),
        in_specs=[VMEM] * (len(got) + 2),
        out_specs=(VMEM,) * (1 + branches),
        scratch_shapes=[pltpu.VMEM((tokens, width), jnp.bfloat16), pltpu.VMEM((tokens, cols), jnp.float32)],
        compiler_params=params(28),
        cost_estimate=cost(2 * tokens * width * cols, 2 * width * cols, tokens * cols),
        name="teacher",
    )(*got, head, weights)


def stats_kernel(count, *refs):
    place = position()
    parts = refs[:count]
    teacher_ref, logits_ref, out_ref = refs[count:]
    logits = parts[0][...]
    for ref in parts[1:]:
        logits = logits + ref[...]
    logits_ref[...] = logits
    top = jnp.max(logits, axis=1, keepdims=True)
    total = jnp.sum(jnp.exp(logits - top), axis=1, keepdims=True)
    rows = logits.shape[0]
    size = out_ref.shape[0] // count
    student = jnp.concatenate([as_row(top), as_row(total)], axis=0)
    for r in range(count):
        there = place[0] ^ r
        block = jnp.concatenate([teacher_ref[:, r * rows : (r + 1) * rows], student], axis=0)
        out_ref[pl.ds(there * size, size)] = jnp.broadcast_to(block[None], (size, 4, rows))


def student_stats(parts, teacher_stats, size):
    rows, cols = parts[0].shape
    count = len(parts)
    return pl.pallas_call(
        functools.partial(stats_kernel, count),
        out_shape=(
            jax.ShapeDtypeStruct((rows, cols), jnp.float32),
            jax.ShapeDtypeStruct((count * size, 4, rows), jnp.float32),
        ),
        in_specs=[VMEM] * (count + 1),
        out_specs=(VMEM, VMEM),
        compiler_params=params(12),
        cost_estimate=cost(8 * rows * cols, 12 * rows * cols, rows * cols),
        name="stats",
    )(*parts, teacher_stats)


def grads_kernel(count, size, stats_ref, logits_ref, ids_ref, *refs):
    place = position()
    terms = refs[:count]
    grads_ref = refs[count]
    b, t = place[0], place[1]
    rows, cols = logits_ref.shape
    logits = logits_ref[...]
    shard = lax.broadcasted_iota(jnp.int32, (rows, cols), 1)
    targets = jnp.where(shard == column(ids_ref[...]) - t * cols, mix_label, 0.0)
    probs = None
    for r in range(count):
        start = (b ^ r) * size
        block = stats_ref[pl.ds(start, size)]
        here = stats_ref[start + t]
        peak = jnp.max(block[:, 0, :], axis=0, keepdims=True)
        total = jnp.sum(block[:, 1, :] * jnp.exp(block[:, 0, :] - peak), axis=0, keepdims=True)
        weight = extra_values(terms[r][rows:, :rows], 1)[0]
        scale = ((1.0 - mix_label) / DEN) * weight * jnp.exp(here[0:1] - peak) / total
        targets = targets + terms[r][:rows].astype(jnp.float32) * column(scale)
        if r == 0:
            peak = jnp.max(block[:, 2, :], axis=0, keepdims=True)
            total = jnp.sum(block[:, 3, :] * jnp.exp(block[:, 2, :] - peak), axis=0, keepdims=True)
            probs = jnp.exp(logits - column(peak)) / column(total)
    grads = (loss_scale * (probs - targets)).astype(grads_ref.dtype)
    grads_ref[:rows] = grads
    grads_ref[rows:] = jnp.zeros((EXTRA, cols), grads.dtype)
    dots = as_row(jnp.sum(grads.astype(jnp.float32) * logits, axis=1, keepdims=True))
    grads_ref[rows:, :rows] = extra_rows([dots], grads.dtype)


def make_grads(stats, logits, ids, terms, size):
    rows, cols = logits.shape
    count = len(terms)
    return pl.pallas_call(
        functools.partial(grads_kernel, count, size),
        out_shape=jax.ShapeDtypeStruct((rows + EXTRA, cols), jnp.bfloat16),
        in_specs=[VMEM] * (count + 3),
        out_specs=VMEM,
        compiler_params=params(12),
        cost_estimate=cost(16 * rows * cols, 10 * rows * cols, rows * cols),
        name="grads",
    )(stats, logits, ids, *terms)


def pieces_kernel(parity, width, grads_ref, w_ref, out_ref, turned_ref):
    place = position()
    rows = out_ref.shape[1]
    turned_ref[...] = jnp.transpose(grads_ref[:rows])
    count = (out_ref.shape[0] - EXTRA) // width
    for k in range(count):
        start = pl.multiple_of((place[2] ^ (2 * k + parity)) * width, width)
        acc = jnp.dot(w_ref[pl.ds(start, width)], turned_ref[...], preferred_element_type=jnp.float32)
        out_ref[k * width : (k + 1) * width] = acc.astype(out_ref.dtype)
    out_ref[count * width :] = grads_ref[rows:, :rows]


def normed_grad_pieces(grads, head, blocks, parity):
    rows, cols = grads.shape[0] - EXTRA, grads.shape[1]
    width = head.shape[0] // blocks
    return pl.pallas_call(
        functools.partial(pieces_kernel, parity, width),
        out_shape=jax.ShapeDtypeStruct((blocks // 2 * width + EXTRA, rows), jnp.bfloat16),
        in_specs=[VMEM] * 2,
        out_specs=VMEM,
        scratch_shapes=[pltpu.VMEM((cols, rows), jnp.bfloat16)],
        compiler_params=params(16),
        cost_estimate=cost(rows * head.size, head.size),
        name="pieces",
    )(grads, head)


def fold_kernel(mine_ref, got_ref, *out):
    f32 = jnp.float32
    width = out[0].shape[0] - EXTRA
    full = len(out) * width
    dots = extra_values(mine_ref[full:], 1)[0] + extra_values(got_ref[full:], 1)[0]
    for k, ref in enumerate(out):
        at = slice(k * width, (k + 1) * width)
        ref[:width] = (mine_ref[at].astype(f32) + got_ref[at].astype(f32)).astype(ref.dtype)
        ref[width:] = extra_rows([dots], ref.dtype)


def fold(mine, got, width):
    full, rows = mine.shape
    count = (full - EXTRA) // width
    return pl.pallas_call(
        fold_kernel,
        out_shape=(jax.ShapeDtypeStruct((width + EXTRA, rows), mine.dtype),) * count,
        in_specs=[VMEM, VMEM],
        out_specs=(VMEM,) * count,
        compiler_params=params(8),
        cost_estimate=cost(mine.size, 6 * mine.size),
        name="fold",
    )(mine, got)


def split_kernel(count, *refs):
    place = position()
    turned, out = refs[-2 * count : -count], refs[-count:]
    each = len(refs) // count - 2
    f32 = jnp.float32
    width, rows = out[0].shape[0] - EXTRA, out[0].shape[1]
    block = pl.multiple_of(place[2] * width, width)
    totals, dots, gain = [], [], 0.0
    for r in range(count):
        total = refs[r * each][...].astype(f32)
        for ref in refs[r * each + 1 : (r + 1) * each]:
            total = total + ref[...].astype(f32)
        dots.append(extra_values(total[width:], 1)[0])
        totals.append(total[:width])
        gain = gain + jnp.sum(totals[r] * turned[r][pl.ds(block, width)].astype(f32), axis=1, keepdims=True)
    gain = as_row(gain)
    lanes = min(width, rows)
    gains = [gain[:, i : i + lanes] for i in range(0, width, lanes)]
    if lanes < rows:
        gains = [jnp.concatenate([row, jnp.zeros((1, rows - lanes), f32)], axis=1) for row in gains]
    for r in range(count):
        total = totals[r].astype(out[0].dtype)
        extra = extra_rows([dots[r]] + gains, out[0].dtype)
        for kh in range(count):

            @pl.when((place[3] ^ kh) == r)
            def _():
                out[kh][:width] = total
                out[kh][width:] = extra


def split(parts, turned):
    count = len(parts)
    shape = parts[0][0].shape
    each = len(parts[0])
    return pl.pallas_call(
        functools.partial(split_kernel, count),
        out_shape=(jax.ShapeDtypeStruct(shape, parts[0][0].dtype),) * count,
        in_specs=[VMEM] * (count * (each + 1)),
        out_specs=(VMEM,) * count,
        compiler_params=params(8),
        cost_estimate=cost(8 * count * shape[0] * shape[1], 12 * count * shape[0] * shape[1]),
        name="split",
    )(*[part for some in parts for part in some], *turned)


def head_grad_kernel(count, half, tile, *refs):
    grads, turned = refs[:count], refs[count : 2 * count]
    out_ref, grads_ref, total_ref, sems = refs[-4:]
    rows = grads_ref.shape[0] // count
    for r in range(count):
        grads_ref[r * rows : (r + 1) * rows, :] = grads[r][:rows]
    copies = []
    for i in range(total_ref.shape[0] // tile):
        here = slice(i * tile, (i + 1) * tile)
        start = half * total_ref.shape[0] + i * tile
        lhs = jnp.concatenate([ref[start : start + tile] for ref in turned], axis=1)
        total_ref[here] = jnp.dot(lhs, grads_ref[...], preferred_element_type=jnp.float32)
        copy = pltpu.make_async_copy(total_ref.at[here], out_ref.at[pl.ds(start, tile)], sems.at[i])
        copy.start()
        copies.append(copy)
    for copy in copies:
        copy.wait()


def head_grad(grads, turned, half, done):
    count = len(grads)
    cols = grads[0].shape[1]
    part, rows = turned[0].shape
    tile = tile_of(part // 2)
    steps = part // tile // 2
    whole = pl.BlockSpec(memory_space=pl.ANY)
    return pl.pallas_call(
        functools.partial(head_grad_kernel, count, half, tile),
        out_shape=jax.ShapeDtypeStruct((part, cols), jnp.float32),
        in_specs=[VMEM] * (2 * count) + [whole] * len(done),
        out_specs=whole,
        scratch_shapes=[
            pltpu.VMEM((count * rows, cols), jnp.bfloat16),
            pltpu.VMEM((part // 2, cols), jnp.float32),
            pltpu.SemaphoreType.DMA((steps,)),
        ],
        input_output_aliases={2 * count: 0} if done else {},
        compiler_params=params(16),
        cost_estimate=cost(count * rows * part * cols, 2 * part * cols),
        name="headgrad",
    )(*grads, *turned, *done)


def last_kernel(count, width, inv_ref, hidden_ref, gain_ref, *refs):
    parts = refs[:count]
    out_ref, gain_out_ref = refs[count:]
    total = parts[0][...].astype(jnp.float32)
    for ref in parts[1:]:
        total = total + ref[...].astype(jnp.float32)
    piece, rows = total.shape[0] - EXTRA, total.shape[1]
    lanes = min(piece, rows)
    dots, *gains = extra_values(total[piece:], 1 + piece // lanes)
    gain_out_ref[...] = jnp.concatenate([row[:, :lanes] for row in gains], axis=1) / gain_ref[...]
    normed_grads = jnp.transpose(total[:piece])
    inv = inv_ref[...]
    scaled = hidden_ref[...].astype(jnp.float32) * inv
    out_ref[...] = inv * gain_ref[...] * normed_grads - scaled * (inv * column(dots) / width)


def finish(parts, inv, hidden, gain, width):
    piece, rows = parts[0].shape[0] - EXTRA, parts[0].shape[1]
    return pl.pallas_call(
        functools.partial(last_kernel, len(parts), width),
        out_shape=(
            jax.ShapeDtypeStruct((rows, piece), jnp.float32),
            jax.ShapeDtypeStruct((1, piece), jnp.float32),
        ),
        in_specs=[VMEM] * (3 + len(parts)),
        out_specs=(VMEM, VMEM),
        compiler_params=params(12),
        cost_estimate=cost(16 * rows * piece, 12 * rows * piece),
        name="last",
    )(inv, hidden, gain, *parts)


def load_kernel(from_ref, to_ref, sem):
    copy = pltpu.make_async_copy(from_ref, to_ref, sem)
    copy.start()
    copy.wait()


def load(value):
    return pl.pallas_call(
        load_kernel,
        out_shape=jax.ShapeDtypeStruct(value.shape, value.dtype),
        in_specs=[pl.BlockSpec(memory_space=pltpu.HBM)],
        out_specs=VMEM,
        scratch_shapes=[pltpu.SemaphoreType.DMA],
        compiler_params=params(16),
        cost_estimate=cost(0, 4 * value.size),
        name="load",
    )(value)


def per_device(
    teacher_hidden,
    teacher_gain,
    teacher_head,
    student_hidden,
    student_gain,
    student_head,
    cluster_weights,
    token_ids,
):
    branches = lax.axis_size("branch")
    size = lax.axis_size("tok")
    t = lax.axis_index("tok")
    rows, width = student_hidden.shape
    blocks = size // branches
    teacher_block, *sent = first_blocks(teacher_hidden, teacher_gain, student_hidden, student_gain, branches)

    loaded = load(student_head)
    own_partial, own_turned, inv_scale = own_dot(student_hidden, student_gain, loaded)
    turned, partials = [own_turned], [own_partial]
    for r in range(1, branches):
        mine = swap(sent[r - 1], "branch", r)
        other = swap(mine, "tok", 1)
        partial, fetched = other_dot(mine, other, loaded)
        turned.append(fetched)
        partials.append(swap(partial, "branch", r))

    got, keys = gather_blocks(teacher_block, size)
    weights = cluster_weights[:, 0].reshape(branches, rows)
    teacher_stats, *exps = teacher_softmax(got, keys, teacher_head, weights, blocks)
    terms = [exps[0]] + [swap(exps[r], "branch", r) for r in range(1, branches)]

    logits, stats = student_stats(partials, teacher_stats, size)
    stats = lax.all_to_all(stats, ("branch", "tok"), 0, 0, tiled=True)
    logit_grads = make_grads(stats, logits, token_ids[None], terms, size)
    all_grads = [logit_grads] + [swap(logit_grads, "branch", r) for r in range(1, branches)]

    slice_width = width // size
    parts = []
    for r in range(branches):
        send = normed_grad_pieces(all_grads[r], loaded, blocks, 1)
        send = swap(send, "tok", 1)
        keep = normed_grad_pieces(all_grads[r], loaded, blocks, 0)
        folded = fold(keep, send, slice_width)
        parts.append([folded[0]] + [swap(folded[k], "tok", 2 * k) for k in range(1, blocks // 2)])
    owned = split(parts, turned)
    arrived = []
    for kh in range(branches):
        perm = []
        for i in range(branches * size):
            bb, h, rest = i // size, (i % size) // blocks, i % blocks
            perm.append((i, (h ^ kh) * size + bb * blocks + rest))
        arrived.append(lax.ppermute(owned[kh], ("branch", "tok"), perm))

    grad_head = head_grad(all_grads, turned, 0, [])
    grad_head = head_grad(all_grads, turned, 1, [grad_head])

    hidden_cols = lax.dynamic_slice_in_dim(student_hidden, t * slice_width, slice_width, 1)
    gain_cols = lax.dynamic_slice_in_dim(student_gain, t * slice_width, slice_width, 0)
    grad_hidden, grad_gain = finish(arrived, inv_scale, hidden_cols, gain_cols[None], width)
    return (grad_head, grad_hidden, grad_gain[0])


def solution(mesh):
    in_specs = (
        P("branch", "tok", None),
        P("branch", None),
        P("branch", None, "tok"),
        P("branch", None),
        P(),
        P("branch", "tok"),
        P(None, "branch"),
        P("branch"),
    )
    out_specs = (P("branch", "tok"), P("branch", "tok"), P("tok"))
    return jax.shard_map(per_device, mesh=mesh, in_specs=in_specs, out_specs=out_specs, check_vma=False)
```

```python
import functools

import jax
import jax.numpy as jnp
from jax import lax
from jax.experimental import pallas as pl
from jax.experimental.pallas import tpu as pltpu
from jax.sharding import PartitionSpec as P


DEN = 64

eps = 1e-05
mix_label = 0.25
loss_scale = 64.0


def swap(value, axis, flip):
    size = lax.axis_size(axis)
    return lax.ppermute(value, axis, [(i, i ^ flip) for i in range(size)])


VMEM = pl.BlockSpec(memory_space=pltpu.VMEM)
MIB = 1 << 20


def params(mib):
    return pltpu.CompilerParams(vmem_limit_bytes=mib * MIB)


def cost(flops, nbytes, exps=0):
    return pl.CostEstimate(flops=flops, bytes_accessed=nbytes, transcendentals=exps)


def position():
    b, t = lax.axis_index("branch"), lax.axis_index("tok")
    blocks = lax.axis_size("tok") // lax.axis_size("branch")
    return b, t, lax.rem(t, blocks), lax.div(t, blocks) ^ b


def normalized(values, gain):
    values = values.astype(jnp.float32)
    scale = lax.rsqrt(jnp.mean(values * values, axis=-1, keepdims=True) + eps)
    return (values * scale * gain).astype(jnp.bfloat16), scale


def first_kernel(branches, *refs):
    teacher, teacher_gain, student, student_gain = refs[:4]
    block_ref, *sent = refs[4 : 4 + branches]
    th_ref, tg_ref, sh_ref, sg_ref, normed_ref, sems = refs[4 + branches :]
    b = lax.axis_index("branch")
    half, part = sent[0].shape
    rows = pl.ds(pl.multiple_of(lax.axis_index("tok") % 2 * half, half), half)
    copies = [
        pltpu.make_async_copy(source, target, sems.at[i])
        for i, (source, target) in enumerate(
            ((student.at[rows], sh_ref), (student_gain, sg_ref), (teacher, th_ref), (teacher_gain, tg_ref))
        )
    ]
    for copy in copies:
        copy.start()
    for copy in copies[:2]:
        copy.wait()
    normed_ref[...], unused = normalized(sh_ref[...], sg_ref[...])
    for r in range(1, branches):
        sent[r - 1][...] = normed_ref[:, pl.ds(pl.multiple_of((b ^ r) * part, part), part)]
    for copy in copies[2:]:
        copy.wait()
    block_ref[...], unused = normalized(th_ref[0], tg_ref[...])


def first_blocks(teacher_hidden, teacher_gain, student_hidden, student_gain, branches):
    rows, width = student_hidden.shape
    part = width // branches
    bf16, f32 = jnp.bfloat16, jnp.float32
    return pl.pallas_call(
        functools.partial(first_kernel, branches),
        out_shape=(
            jax.ShapeDtypeStruct(teacher_hidden.shape[1:], bf16),
            *[jax.ShapeDtypeStruct((rows // 2, part), bf16)] * (branches - 1),
        ),
        in_specs=[pl.BlockSpec(memory_space=pl.ANY)] * 4,
        out_specs=(VMEM,) * branches,
        scratch_shapes=[
            pltpu.VMEM(teacher_hidden.shape, bf16),
            pltpu.VMEM((1, width), f32),
            pltpu.VMEM((rows // 2, width), bf16),
            pltpu.VMEM((1, width), f32),
            pltpu.VMEM((rows // 2, width), bf16),
            pltpu.SemaphoreType.DMA((4,)),
        ],
        compiler_params=params(60),
        cost_estimate=cost(8 * rows * width, 4 * rows * width),
        name="first",
    )(teacher_hidden, teacher_gain, student_hidden, student_gain[None])


def gather_blocks(block, size):
    got = {0: block}
    for k in range(8, size, 8):
        got[k] = swap(block, "tok", k)
    for k in range(0, size, 8):
        got[k + 4] = swap(got[k], "tok", 4)
    got[6] = swap(block, "tok", 6)
    for k in range(0, size, 4):
        if k != 4:
            got[k + 2] = swap(got[k], "tok", 2)
    evens = sorted(got)
    half = len(evens) // 2
    arrays = [got[k] for k in evens]
    keys = [(k,) for k in evens]
    for group in (evens[:half], evens[half:]):
        arrays.append(swap(jnp.concatenate([got[k] for k in group], axis=0), "tok", 1))
        keys.append(tuple(k + 1 for k in group))
    return arrays, tuple(keys)


def own_dot_kernel(rows_ref, gain_ref, w_ref, out_ref, turned_ref, inv_ref, normed_ref):
    place = position()
    normed_ref[...], inv_ref[...] = normalized(rows_ref[...], gain_ref[...])
    part = turned_ref.shape[0]
    own = normed_ref[:, pl.ds(pl.multiple_of(place[0] * part, part), part)]
    turned_ref[...] = jnp.transpose(own)
    out_ref[...] = jnp.dot(own, w_ref[...], preferred_element_type=jnp.float32)


def own_dot(hidden, gain, head):
    rows, width = hidden.shape
    return pl.pallas_call(
        own_dot_kernel,
        out_shape=(
            jax.ShapeDtypeStruct((rows, head.shape[1]), jnp.float32),
            jax.ShapeDtypeStruct((head.shape[0], rows), jnp.bfloat16),
            jax.ShapeDtypeStruct((rows, 1), jnp.float32),
        ),
        in_specs=[VMEM] * 3,
        out_specs=(VMEM,) * 3,
        scratch_shapes=[pltpu.VMEM((rows, width), jnp.bfloat16)],
        compiler_params=params(16),
        cost_estimate=cost(2 * rows * head.size, 2 * head.size),
        name="owndot",
    )(hidden, gain[None], head)


def other_dot_kernel(mine_ref, other_ref, w_ref, out_ref, turned_ref, rows_ref):
    place = position()
    half = mine_ref.shape[0]
    core = place[1] % 2
    rows_ref[pl.ds(pl.multiple_of(core * half, half), half), :] = mine_ref[...]
    rows_ref[pl.ds(pl.multiple_of((1 - core) * half, half), half), :] = other_ref[...]
    out_ref[...] = jnp.dot(rows_ref[...], w_ref[...], preferred_element_type=jnp.float32)
    turned_ref[...] = jnp.transpose(rows_ref[...])


def other_dot(mine, other, head):
    rows = 2 * mine.shape[0]
    return pl.pallas_call(
        other_dot_kernel,
        out_shape=(
            jax.ShapeDtypeStruct((rows, head.shape[1]), jnp.float32),
            jax.ShapeDtypeStruct((mine.shape[1], rows), jnp.bfloat16),
        ),
        in_specs=[VMEM] * 3,
        out_specs=(VMEM, VMEM),
        scratch_shapes=[pltpu.VMEM((rows, mine.shape[1]), jnp.bfloat16)],
        compiler_params=params(16),
        cost_estimate=cost(2 * rows * head.size, 2 * head.size),
        name="otherdot",
    )(mine, other, head)


EXTRA = 8


def extra_rows(values, dtype):
    first = [value.astype(dtype).astype(jnp.float32) for value in values]
    rest = [value - lead for value, lead in zip(values, first)]
    empty = jnp.zeros((EXTRA - 2 * len(values), values[0].shape[1]), jnp.float32)
    return jnp.concatenate(first + rest + [empty], axis=0).astype(dtype)


def extra_values(rows, count):
    rows = rows.astype(jnp.float32)
    return [rows[i : i + 1] + rows[count + i : count + i + 1] for i in range(count)]


def tile_of(cols):
    return next((tile for tile in (256, 128) if cols % tile == 0), cols)


def column(row):
    count = row.shape[1]
    return jnp.transpose(jnp.broadcast_to(row, (128, count)))[:, :1]


def as_row(col):
    return jnp.transpose(jnp.broadcast_to(col, (col.shape[0], 128)))[:1]


def teacher_kernel(keys, half, *refs):
    place = position()
    blocks = refs[: len(keys)]
    w_ref, weight_ref, stat_ref, *exps = refs[len(keys) : -2]
    rows_ref, logits_ref = refs[-2:]
    mine = place[1] ^ (place[0] * half)
    for ref, owned in zip(blocks, keys):
        count = ref.shape[0] // len(owned)
        for j, k in enumerate(owned):
            start = pl.multiple_of((mine ^ k) * count, count)
            rows_ref[pl.ds(start, count), :] = ref[j * count : (j + 1) * count, :]

    cols = w_ref.shape[2]
    tile = tile_of(cols)
    if tile == cols:
        logits_ref[...] = jnp.dot(rows_ref[...], w_ref[0], preferred_element_type=jnp.float32)
    else:

        @pl.loop(0, cols // tile)
        def _(step):
            at = pl.ds(pl.multiple_of(step * tile, tile), tile)
            logits_ref[:, at] = jnp.dot(rows_ref[...], w_ref[0, :, at], preferred_element_type=jnp.float32)

    logits = logits_ref[...]
    top = jnp.max(logits, axis=1, keepdims=True)
    scaled = jnp.exp(logits - top)
    rows = exps[0].shape[0] - EXTRA
    for r, ref in enumerate(exps):
        ref[:rows] = scaled[r * rows : (r + 1) * rows].astype(ref.dtype)
        ref[rows:] = jnp.zeros((EXTRA, cols), ref.dtype)
        weight = weight_ref[pl.ds(place[0] ^ r, 1), :].astype(jnp.float32)
        ref[rows:, :rows] = extra_rows([weight], ref.dtype)
    stat_ref[0:1, :] = as_row(top)
    stat_ref[1:2, :] = as_row(jnp.sum(scaled, axis=1, keepdims=True))


def teacher_softmax(got, keys, head, weights, half):
    branches = weights.shape[0]
    width, cols = head.shape[1:]
    tokens = sum(part.shape[0] for part in got)
    return pl.pallas_call(
        functools.partial(teacher_kernel, keys, half),
        out_shape=(
            jax.ShapeDtypeStruct((2, tokens), jnp.float32),
            *[jax.ShapeDtypeStruct((tokens // branches + EXTRA, cols), jnp.bfloat16)] * branches,
        ),
        in_specs=[VMEM] * (len(got) + 2),
        out_specs=(VMEM,) * (1 + branches),
        scratch_shapes=[pltpu.VMEM((tokens, width), jnp.bfloat16), pltpu.VMEM((tokens, cols), jnp.float32)],
        compiler_params=params(28),
        cost_estimate=cost(2 * tokens * width * cols, 2 * width * cols, tokens * cols),
        name="teacher",
    )(*got, head, weights)


def stats_kernel(count, *refs):
    place = position()
    parts = refs[:count]
    teacher_ref, logits_ref, out_ref = refs[count:]
    logits = parts[0][...]
    for ref in parts[1:]:
        logits = logits + ref[...]
    logits_ref[...] = logits
    top = jnp.max(logits, axis=1, keepdims=True)
    total = jnp.sum(jnp.exp(logits - top), axis=1, keepdims=True)
    rows = logits.shape[0]
    size = out_ref.shape[0] // count
    student = jnp.concatenate([as_row(top), as_row(total)], axis=0)
    for r in range(count):
        there = place[0] ^ r
        block = jnp.concatenate([teacher_ref[:, r * rows : (r + 1) * rows], student], axis=0)
        out_ref[pl.ds(there * size, size)] = jnp.broadcast_to(block[None], (size, 4, rows))


def student_stats(parts, teacher_stats, size):
    rows, cols = parts[0].shape
    count = len(parts)
    return pl.pallas_call(
        functools.partial(stats_kernel, count),
        out_shape=(
            jax.ShapeDtypeStruct((rows, cols), jnp.float32),
            jax.ShapeDtypeStruct((count * size, 4, rows), jnp.float32),
        ),
        in_specs=[VMEM] * (count + 1),
        out_specs=(VMEM, VMEM),
        compiler_params=params(12),
        cost_estimate=cost(8 * rows * cols, 12 * rows * cols, rows * cols),
        name="stats",
    )(*parts, teacher_stats)


def grads_kernel(count, size, stats_ref, logits_ref, ids_ref, *refs):
    place = position()
    terms = refs[:count]
    grads_ref, dots_ref = refs[count:]
    b, t = place[0], place[1]
    rows, cols = logits_ref.shape
    logits = logits_ref[...]
    shard = lax.broadcasted_iota(jnp.int32, (rows, cols), 1)
    targets = jnp.where(shard == column(ids_ref[...]) - t * cols, mix_label, 0.0)
    probs = None
    for r in range(count):
        start = (b ^ r) * size
        block = stats_ref[pl.ds(start, size)]
        here = stats_ref[start + t]
        peak = jnp.max(block[:, 0, :], axis=0, keepdims=True)
        total = jnp.sum(block[:, 1, :] * jnp.exp(block[:, 0, :] - peak), axis=0, keepdims=True)
        weight = extra_values(terms[r][rows:, :rows], 1)[0]
        scale = ((1.0 - mix_label) / DEN) * weight * jnp.exp(here[0:1] - peak) / total
        targets = targets + terms[r][:rows].astype(jnp.float32) * column(scale)
        if r == 0:
            peak = jnp.max(block[:, 2, :], axis=0, keepdims=True)
            total = jnp.sum(block[:, 3, :] * jnp.exp(block[:, 2, :] - peak), axis=0, keepdims=True)
            probs = jnp.exp(logits - column(peak)) / column(total)
    grads = (loss_scale * (probs - targets)).astype(grads_ref.dtype)
    grads_ref[...] = grads
    dots = as_row(jnp.sum(grads.astype(jnp.float32) * logits, axis=1, keepdims=True))
    dots_ref[...] = extra_rows([dots], grads.dtype)


def make_grads(stats, logits, ids, terms, size):
    rows, cols = logits.shape
    count = len(terms)
    return pl.pallas_call(
        functools.partial(grads_kernel, count, size),
        out_shape=(jax.ShapeDtypeStruct((rows, cols), jnp.bfloat16), jax.ShapeDtypeStruct((EXTRA, rows), jnp.bfloat16)),
        in_specs=[VMEM] * (count + 3),
        out_specs=(VMEM, VMEM),
        compiler_params=params(12),
        cost_estimate=cost(16 * rows * cols, 10 * rows * cols, rows * cols),
        name="grads",
    )(stats, logits, ids, *terms)


def pieces_kernel(parity, width, grads_ref, dots_ref, w_ref, out_ref, turned_ref):
    place = position()
    turned_ref[...] = jnp.transpose(grads_ref[...])
    count = (out_ref.shape[0] - EXTRA) // width
    for k in range(count):
        start = pl.multiple_of((place[2] ^ (2 * k + parity)) * width, width)
        acc = jnp.dot(w_ref[pl.ds(start, width)], turned_ref[...], preferred_element_type=jnp.float32)
        out_ref[k * width : (k + 1) * width] = acc.astype(out_ref.dtype)
    out_ref[count * width :] = dots_ref[...]


def normed_grad_pieces(grads, dots, head, blocks, parity):
    rows, cols = grads.shape
    width = head.shape[0] // blocks
    return pl.pallas_call(
        functools.partial(pieces_kernel, parity, width),
        out_shape=jax.ShapeDtypeStruct((blocks // 2 * width + EXTRA, rows), jnp.bfloat16),
        in_specs=[VMEM] * 3,
        out_specs=VMEM,
        scratch_shapes=[pltpu.VMEM((cols, rows), jnp.bfloat16)],
        compiler_params=params(16),
        cost_estimate=cost(rows * head.size, head.size),
        name="pieces",
    )(grads, dots, head)


def fold_kernel(mine_ref, got_ref, *out):
    f32 = jnp.float32
    width = out[0].shape[0] - EXTRA
    full = len(out) * width
    dots = extra_values(mine_ref[full:], 1)[0] + extra_values(got_ref[full:], 1)[0]
    extra = extra_rows([dots], out[0].dtype)
    for k, ref in enumerate(out):
        at = slice(k * width, (k + 1) * width)
        ref[:width] = (mine_ref[at].astype(f32) + got_ref[at].astype(f32)).astype(ref.dtype)
        ref[width:] = extra


def fold(mine, got, width):
    full, rows = mine.shape
    count = (full - EXTRA) // width
    return pl.pallas_call(
        fold_kernel,
        out_shape=(jax.ShapeDtypeStruct((width + EXTRA, rows), mine.dtype),) * count,
        in_specs=[VMEM, VMEM],
        out_specs=(VMEM,) * count,
        compiler_params=params(8),
        cost_estimate=cost(mine.size, 6 * mine.size),
        name="fold",
    )(mine, got)


def split_kernel(count, *refs):
    place = position()
    turned, out = refs[-2 * count : -count], refs[-count:]
    each = len(refs) // count - 2
    f32 = jnp.float32
    width, rows = out[0].shape[0] - EXTRA, out[0].shape[1]
    block = pl.multiple_of(place[2] * width, width)
    totals, dots, gain = [], [], 0.0
    for r in range(count):
        total = refs[r * each][...].astype(f32)
        for ref in refs[r * each + 1 : (r + 1) * each]:
            total = total + ref[...].astype(f32)
        dots.append(extra_values(total[width:], 1)[0])
        totals.append(total[:width])
        gain = gain + jnp.sum(totals[r] * turned[r][pl.ds(block, width)].astype(f32), axis=1, keepdims=True)
    gain = as_row(gain)
    lanes = min(width, rows)
    gains = [gain[:, i : i + lanes] for i in range(0, width, lanes)]
    if lanes < rows:
        gains = [jnp.concatenate([row, jnp.zeros((1, rows - lanes), f32)], axis=1) for row in gains]
    for r in range(count):
        total = totals[r].astype(out[0].dtype)
        extra = extra_rows([dots[r]] + gains, out[0].dtype)
        for kh in range(count):

            @pl.when((place[3] ^ kh) == r)
            def _():
                out[kh][:width] = total
                out[kh][width:] = extra


def split(parts, turned):
    count = len(parts)
    shape = parts[0][0].shape
    each = len(parts[0])
    return pl.pallas_call(
        functools.partial(split_kernel, count),
        out_shape=(jax.ShapeDtypeStruct(shape, parts[0][0].dtype),) * count,
        in_specs=[VMEM] * (count * (each + 1)),
        out_specs=(VMEM,) * count,
        compiler_params=params(8),
        cost_estimate=cost(8 * count * shape[0] * shape[1], 12 * count * shape[0] * shape[1]),
        name="split",
    )(*[part for some in parts for part in some], *turned)


def head_grad_kernel(count, half, tile, *refs):
    grads, turned = refs[:count], refs[count : 2 * count]
    out_ref, grads_ref, total_ref, sems = refs[-4:]
    rows = grads_ref.shape[0] // count
    for r in range(count):
        grads_ref[r * rows : (r + 1) * rows, :] = grads[r][:rows]
    copies = []
    for i in range(total_ref.shape[0] // tile):
        here = slice(i * tile, (i + 1) * tile)
        start = half * total_ref.shape[0] + i * tile
        lhs = jnp.concatenate([ref[start : start + tile] for ref in turned], axis=1)
        total_ref[here] = jnp.dot(lhs, grads_ref[...], preferred_element_type=jnp.float32)
        copy = pltpu.make_async_copy(total_ref.at[here], out_ref.at[pl.ds(start, tile)], sems.at[i])
        copy.start()
        copies.append(copy)
    for copy in copies:
        copy.wait()


def head_grad(grads, turned, half, done):
    count = len(grads)
    cols = grads[0].shape[1]
    part, rows = turned[0].shape
    tile = tile_of(part // 2)
    steps = part // tile // 2
    whole = pl.BlockSpec(memory_space=pl.ANY)
    return pl.pallas_call(
        functools.partial(head_grad_kernel, count, half, tile),
        out_shape=jax.ShapeDtypeStruct((part, cols), jnp.float32),
        in_specs=[VMEM] * (2 * count) + [whole] * len(done),
        out_specs=whole,
        scratch_shapes=[
            pltpu.VMEM((count * rows, cols), jnp.bfloat16),
            pltpu.VMEM((part // 2, cols), jnp.float32),
            pltpu.SemaphoreType.DMA((steps,)),
        ],
        input_output_aliases={2 * count: 0} if done else {},
        compiler_params=params(16),
        cost_estimate=cost(count * rows * part * cols, 2 * part * cols),
        name="headgrad",
    )(*grads, *turned, *done)


def last_kernel(count, width, inv_ref, hidden_ref, gain_ref, *refs):
    parts = refs[:count]
    out_ref, gain_out_ref = refs[count:]
    total = parts[0][...].astype(jnp.float32)
    for ref in parts[1:]:
        total = total + ref[...].astype(jnp.float32)
    piece, rows = total.shape[0] - EXTRA, total.shape[1]
    lanes = min(piece, rows)
    dots, *gains = extra_values(total[piece:], 1 + piece // lanes)
    gain_out_ref[...] = jnp.concatenate([row[:, :lanes] for row in gains], axis=1) / gain_ref[...]
    normed_grads = jnp.transpose(total[:piece])
    inv = inv_ref[...]
    scaled = hidden_ref[...].astype(jnp.float32) * inv
    out_ref[...] = inv * gain_ref[...] * normed_grads - scaled * (inv * column(dots) / width)


def finish(parts, inv, hidden, gain, width):
    piece, rows = parts[0].shape[0] - EXTRA, parts[0].shape[1]
    return pl.pallas_call(
        functools.partial(last_kernel, len(parts), width),
        out_shape=(
            jax.ShapeDtypeStruct((rows, piece), jnp.float32),
            jax.ShapeDtypeStruct((1, piece), jnp.float32),
        ),
        in_specs=[VMEM] * (3 + len(parts)),
        out_specs=(VMEM, VMEM),
        compiler_params=params(12),
        cost_estimate=cost(16 * rows * piece, 12 * rows * piece),
        name="last",
    )(inv, hidden, gain, *parts)


def load_kernel(from_ref, to_ref, sem):
    copy = pltpu.make_async_copy(from_ref, to_ref, sem)
    copy.start()
    copy.wait()


def load(value):
    return pl.pallas_call(
        load_kernel,
        out_shape=jax.ShapeDtypeStruct(value.shape, value.dtype),
        in_specs=[pl.BlockSpec(memory_space=pltpu.HBM)],
        out_specs=VMEM,
        scratch_shapes=[pltpu.SemaphoreType.DMA],
        compiler_params=params(16),
        cost_estimate=cost(0, 4 * value.size),
        name="load",
    )(value)


def per_device(
    teacher_hidden,
    teacher_gain,
    teacher_head,
    student_hidden,
    student_gain,
    student_head,
    cluster_weights,
    token_ids,
):
    branches = lax.axis_size("branch")
    size = lax.axis_size("tok")
    t = lax.axis_index("tok")
    rows, width = student_hidden.shape
    blocks = size // branches
    teacher_block, *sent = first_blocks(teacher_hidden, teacher_gain, student_hidden, student_gain, branches)

    loaded = load(student_head)
    own_partial, own_turned, inv_scale = own_dot(student_hidden, student_gain, loaded)
    turned, partials = [own_turned], [own_partial]
    for r in range(1, branches):
        mine = swap(sent[r - 1], "branch", r)
        other = swap(mine, "tok", 1)
        partial, fetched = other_dot(mine, other, loaded)
        turned.append(fetched)
        partials.append(swap(partial, "branch", r))

    got, keys = gather_blocks(teacher_block, size)
    weights = cluster_weights[:, 0].reshape(branches, rows)
    teacher_stats, *exps = teacher_softmax(got, keys, teacher_head, weights, blocks)
    terms = [exps[0]] + [swap(exps[r], "branch", r) for r in range(1, branches)]

    logits, stats = student_stats(partials, teacher_stats, size)
    stats = lax.all_to_all(stats, ("branch", "tok"), 0, 0, tiled=True)
    logit_grads, dots = make_grads(stats, logits, token_ids[None], terms, size)
    all_grads = [logit_grads] + [swap(logit_grads, "branch", r) for r in range(1, branches)]
    all_dots = [dots] + [swap(dots, "branch", r) for r in range(1, branches)]

    slice_width = width // size
    parts = []
    for r in range(branches):
        send = normed_grad_pieces(all_grads[r], all_dots[r], loaded, blocks, 1)
        send = swap(send, "tok", 1)
        keep = normed_grad_pieces(all_grads[r], all_dots[r], loaded, blocks, 0)
        folded = fold(keep, send, slice_width)
        parts.append([folded[0]] + [swap(folded[k], "tok", 2 * k) for k in range(1, blocks // 2)])
    owned = split(parts, turned)
    arrived = []
    for kh in range(branches):
        perm = []
        for i in range(branches * size):
            bb, h, rest = i // size, (i % size) // blocks, i % blocks
            perm.append((i, (h ^ kh) * size + bb * blocks + rest))
        arrived.append(lax.ppermute(owned[kh], ("branch", "tok"), perm))

    grad_head = head_grad(all_grads, turned, 0, [])
    grad_head = head_grad(all_grads, turned, 1, [grad_head])

    hidden_cols = lax.dynamic_slice_in_dim(student_hidden, t * slice_width, slice_width, 1)
    gain_cols = lax.dynamic_slice_in_dim(student_gain, t * slice_width, slice_width, 0)
    grad_hidden, grad_gain = finish(arrived, inv_scale, hidden_cols, gain_cols[None], width)
    return (grad_head, grad_hidden, grad_gain[0])


def solution(mesh):
    in_specs = (
        P("branch", "tok", None),
        P("branch", None),
        P("branch", None, "tok"),
        P("branch", None),
        P(),
        P("branch", "tok"),
        P(None, "branch"),
        P("branch"),
    )
    out_specs = (P("branch", "tok"), P("branch", "tok"), P("tok"))
    return jax.shard_map(per_device, mesh=mesh, in_specs=in_specs, out_specs=out_specs, check_vma=False)
```
